768 devices in a mesh: gx: 48 (over x, z), gy: 16 (over y, core).
Axes of the slice: x: 4, y: 8, z: 12, core: 2. Of those that a mesh axis runs over, the one named last changes fastest.
Arguments:
- displacement: float32 [384, 64, 3, 128], P('gx', 'gy'), may hold values from -6 to 6
- volume: float32 [384, 64, 128], P('gx', 'gy'), may hold values from 0.5 to 2
- health: float32 [384, 64, 128], P('gx', 'gy'), may hold values from 0.2 to 1
- damage: int32 [384, 64, 128], P('gx', 'gy'), may hold values 0 or 1
- block_pairs: int32 [48, 16, 162, 4], P('gx', 'gy'), may hold values from -1 to 9, as said below
Outputs:
- deform_grad: float32 [384, 64, 9, 128], P('gx', 'gy')
- force_density: float32 [384, 64, 3, 128], P('gx', 'gy')
The draws below stay inside these ranges and needn't reach their ends.
Inputs may be any that keep to these rules, and one draw needn't show every extreme that they name: `block_pairs`: every row is (ax, ay, bx, by) with blocks in a device's frame: its own blocks at 1 to 8 and 1 to 4, the blocks beside them at 0 and 9, 0 and 5; (bx - ax, by - ay) is (1, 0), (0, 1), (1, 1) or (1, -1); both blocks lie inside the plate and at least one is the device's own. A pair of adjacent plate blocks is named at most once over all devices; pairs named nowhere are severed. Live rows come first, then rows of -1. In every draw some device names all 162 pairs that touch its blocks.
All inputs are finite; a program needn't handle non-finite values. No bound on the sum of `damage` on one device may be relied on, other than what follows from the above.
Results may differ from the reference program's by a relative error of at most 0.0003.
Values sent between devices are 32-bit elements; how exact they have to be, the bound alone decides.
A program may use at most 32 MiB of HBM per device.

```python
import math
import jax
import jax.numpy as jnp
import numpy as np
from jax import lax

PTS_BLK = 128
BX_DEV = 8
BY_DEV = 4
PLATE_X = 384
PLATE_Y = 64
PAIRS_MAX = 162
N_GX = 48
N_GY = 16


def pair_template():
    ext_x = BX_DEV + 2
    ext_y = BY_DEV + 2
    entries = []
    for first_x in range(ext_x):
        for first_y in range(ext_y):
            for kind_index, step_pair in enumerate(((1, 0), (0, 1), (1, 1), (1, -1))):
                second_x = first_x + step_pair[0]
                second_y = first_y + step_pair[1]
                inside_ext = 0 <= second_x < ext_x and 0 <= second_y < ext_y
                own_first = 1 <= first_x <= BX_DEV and 1 <= first_y <= BY_DEV
                own_second = 1 <= second_x <= BX_DEV and 1 <= second_y <= BY_DEV
                if inside_ext and (own_first or own_second):
                    entries.append((first_x, first_y, second_x, second_y, kind_index))
    return np.array(entries, dtype=np.int32)


def draw_block_pairs(key, part):
    template = jnp.asarray(pair_template())
    plate_x = BX_DEV * N_GX
    plate_y = BY_DEV * N_GY
    pick_side = jax.random.randint(jax.random.fold_in(key, 11), (plate_x, plate_y, 4), 0, 2)
    cut_flag = jax.random.randint(jax.random.fold_in(key, 12), (plate_x, plate_y, 4), 0, 8) == 0
    star_x = jax.random.randint(jax.random.fold_in(key, 13), (), 1, N_GX - 1)
    star_y = jax.random.randint(jax.random.fold_in(key, 14), (), 1, N_GY - 1)
    star_device = star_x * N_GY + star_y
    dev_x = jnp.arange(N_GX, dtype=jnp.int32)[:, None, None]
    dev_y = jnp.arange(N_GY, dtype=jnp.int32)[None, :, None]
    first_x = dev_x * BX_DEV + template[:, 0] - 1
    first_y = dev_y * BY_DEV + template[:, 1] - 1
    second_x = dev_x * BX_DEV + template[:, 2] - 1
    second_y = dev_y * BY_DEV + template[:, 3] - 1
    inside = (first_x >= 0) & (first_x < plate_x) & (first_y >= 0) & (first_y < plate_y)
    inside = inside & (second_x >= 0) & (second_x < plate_x) & (second_y >= 0) & (second_y < plate_y)
    owner_first = first_x // BX_DEV * N_GY + first_y // BY_DEV
    owner_second = second_x // BX_DEV * N_GY + second_y // BY_DEV
    anchor_x = jnp.clip(first_x, 0, plate_x - 1)
    anchor_y = jnp.clip(first_y, 0, plate_y - 1)
    kind_index = jnp.broadcast_to(template[:, 4], first_x.shape)
    chosen = pick_side[anchor_x, anchor_y, kind_index]
    severed = cut_flag[anchor_x, anchor_y, kind_index]
    touches = (owner_first == star_device) | (owner_second == star_device)
    runner = jnp.where(chosen == 0, owner_first, owner_second)
    runner = jnp.where(touches, star_device, runner)
    device = dev_x * N_GY + dev_y
    live_flag = inside & (runner == device) & (touches | jnp.logical_not(severed))
    order_noise = jax.random.randint(jax.random.fold_in(key, 15), first_x.shape, 0, PAIRS_MAX) * PAIRS_MAX + jnp.arange(PAIRS_MAX, dtype=jnp.int32)
    order_score = jnp.where(live_flag, 0, PAIRS_MAX * PAIRS_MAX) + order_noise
    slot_order = jnp.argsort(order_score, axis=-1, stable=True)
    rows_all = jnp.broadcast_to(template[:, 0:4], first_x.shape + (4,))
    picked = jnp.take_along_axis(rows_all, slot_order[..., None], axis=2)
    keep_flag = jnp.take_along_axis(live_flag, slot_order, axis=2)
    return jnp.where(keep_flag[..., None], picked, -1).astype(jnp.int32)


def touch_ends(values, key, smallest, top_value):
    extent = values.shape
    index_at = [jax.random.randint(jax.random.fold_in(key, axis), (), 0, extent[axis]) for axis in range(len(extent))]
    values = values.at[tuple(index_at)].set(smallest)
    longest = extent.index(max(extent))
    index_at[longest] = (index_at[longest] + 1) % extent[longest]
    return values.at[tuple(index_at)].set(top_value)


def block_scale(stream_key, dims, cuts, low, top_value):
    factor_of, own = 1.0, jax.random.fold_in(stream_key, 6)
    for axis_at, blocks in cuts:
        draws = jnp.exp(jax.random.uniform(jax.random.fold_in(own, axis_at), (blocks,), jnp.float32, low / len(cuts), top_value / len(cuts)))
        factor_of = factor_of * jnp.repeat(draws, dims[axis_at] // blocks).reshape([-1 if axis == axis_at else 1 for axis in range(len(dims))])
    return factor_of


def normal_values(rng, extent, width, reach, split=(), kind=jnp.bfloat16):
    values = jax.random.normal(rng, extent, jnp.float32) * width
    if len(split) > 0:
        values = block_scale(rng, extent, split, -0.22, 0.18) * values
    return jnp.clip(values, min=-reach, max=reach).astype(kind)


def setup_inputs(seed: int = 0) -> dict:
    arg_keys = jax.random.split(jax.random.key(seed), 6)
    displacement = normal_values(arg_keys[0], (PLATE_X, PLATE_Y, 3, PTS_BLK), 1.0, 6.0, ((0, 48), (1, 16)), jnp.float32)
    volume = jnp.clip(jnp.exp(math.log(2.0) - 1.3862944 * jax.random.uniform(arg_keys[1], (PLATE_X, PLATE_Y, PTS_BLK), jnp.float32) ** block_scale(arg_keys[1], (PLATE_X, PLATE_Y, PTS_BLK), ((0, 48), (1, 16)), -0.2, 0.2)), 0.5, 2.0)
    health = jnp.clip(0.2 + 0.8 * jax.random.uniform(arg_keys[2], (PLATE_X, PLATE_Y, PTS_BLK), jnp.float32) ** block_scale(arg_keys[2], (PLATE_X, PLATE_Y, PTS_BLK), ((0, 48), (1, 16)), -0.2, 0.2), 0.2, 1.0)
    damage = touch_ends((jax.random.randint(arg_keys[3], (PLATE_X, PLATE_Y, PTS_BLK), 0, 8) < 1).astype(jnp.int32), jax.random.fold_in(arg_keys[3], 1), 0, 1)
    block_pairs = draw_block_pairs(jax.random.fold_in(arg_keys[5], 71), 0)
    return dict(displacement=displacement, volume=volume, health=health, damage=damage, block_pairs=block_pairs)


highest = lax.Precision.HIGHEST
lame_first = 24.0
shear_modulus = 16.0
transpose_order = np.array([0, 3, 6, 1, 4, 7, 2, 5, 8])


def lattice(points):
    index = jnp.arange(points, dtype=jnp.int32)
    return jnp.stack([index % 4, (index // 4) % 4, index // 16])


def block_offset(step_x, step_y):
    return jnp.stack([4 * step_x, 4 * step_y, jnp.zeros_like(step_x)], axis=1)


def bond_weights(health_first, health_second, step_x, step_y):
    points = health_first.shape[-1]
    lattice_grid = lattice(points)
    shifted = lattice_grid[None] + block_offset(step_x, step_y)[:, :, None]
    distance = jnp.zeros((step_x.shape[0], points, points), jnp.int32)
    for comp_index in range(3):
        gap_comp = shifted[:, comp_index, None, :] - lattice_grid[None, comp_index, :, None]
        distance = distance + gap_comp * gap_comp
    linked = (distance <= 9) & (distance > 0)
    lower_health = jnp.minimum(health_first[:, :, None], health_second[:, None, :])
    return jnp.where(linked, lower_health, jnp.zeros_like(lower_health))


def positions(point_pack, step_x, step_y):
    reference_pos = (lattice(point_pack.shape[-1])[None] + block_offset(step_x, step_y)[:, :, None]).astype(jnp.float32)
    return reference_pos, reference_pos + point_pack[:, 0:3], point_pack[:, 3], point_pack[:, 4]


def shape_features(ref_pos, cur_pos, vol_pts):
    slot_count, points = ref_pos.shape[0], ref_pos.shape[-1]
    outer_rr = (ref_pos[:, :, None] * ref_pos[:, None]).reshape(slot_count, 9, points)
    outer_cr = (cur_pos[:, :, None] * ref_pos[:, None]).reshape(slot_count, 9, points)
    ones_row = jnp.ones((slot_count, 1, points), jnp.float32)
    return jnp.concatenate([outer_rr, outer_cr, ref_pos, cur_pos, ones_row], axis=1) * vol_pts[:, None]


def shape_terms(tile_sums, ref_pos, cur_pos):
    slot_count, points = ref_pos.shape[0], ref_pos.shape[-1]
    sum_rr = tile_sums[:, 0:9].reshape(slot_count, 3, 3, points)
    sum_cr = tile_sums[:, 9:18].reshape(slot_count, 3, 3, points)
    sum_r = tile_sums[:, 18:21]
    sum_c = tile_sums[:, 21:24]
    sum_one = tile_sums[:, 24][:, None, None]
    shape_k = sum_rr - ref_pos[:, :, None] * sum_r[:, None] - sum_r[:, :, None] * ref_pos[:, None] + sum_one * ref_pos[:, :, None] * ref_pos[:, None]
    shape_n = sum_cr - cur_pos[:, :, None] * sum_r[:, None] - sum_c[:, :, None] * ref_pos[:, None] + sum_one * cur_pos[:, :, None] * ref_pos[:, None]
    return jnp.concatenate([shape_k.reshape(slot_count, 9, points), shape_n.reshape(slot_count, 9, points)], axis=1)


def force_features(ref_pos, stress_map, vol_pts):
    slot_count, points = ref_pos.shape[0], ref_pos.shape[-1]
    mapped = jnp.sum(stress_map * ref_pos[:, None], axis=2)
    ones_row = jnp.ones((slot_count, 1, points), jnp.float32)
    return jnp.concatenate([mapped, stress_map.reshape(slot_count, 9, points), ref_pos, ones_row], axis=1) * vol_pts[:, None]


def force_terms(tile_sums, ref_pos, stress_map):
    slot_count, points = ref_pos.shape[0], ref_pos.shape[-1]
    sum_ar = tile_sums[:, 0:3]
    sum_a = tile_sums[:, 3:12].reshape(slot_count, 3, 3, points)
    spread = tile_sums[:, 12:15] - tile_sums[:, 15][:, None] * ref_pos
    return jnp.sum(stress_map * spread[:, None], axis=2) + sum_ar - jnp.sum(sum_a * ref_pos[:, None], axis=2)


def tile_terms(pack_first, pack_second, map_first, map_second, step_x, step_y, section):
    zero_step = jnp.zeros_like(step_x)
    ref_a, cur_a, vol_a, health_a = positions(pack_first, zero_step, zero_step)
    ref_b, cur_b, vol_b, health_b = positions(pack_second, step_x, step_y)
    weights = bond_weights(health_a, health_b, step_x, step_y)
    if section == "shape":
        feat_a = shape_features(ref_a, cur_a, vol_a)
        feat_b = shape_features(ref_b, cur_b, vol_b)
    else:
        feat_a = force_features(ref_a, map_first, vol_a)
        feat_b = force_features(ref_b, map_second, vol_b)
    sums_a = jnp.einsum("gcj,gij->gci", feat_b, weights, precision=highest)
    sums_b = jnp.einsum("gci,gij->gcj", feat_a, weights, precision=highest)
    if section == "shape":
        return shape_terms(sums_a, ref_a, cur_a), shape_terms(sums_b, ref_b, cur_b)
    return force_terms(sums_a, ref_a, map_first), force_terms(sums_b, ref_b, map_second)


def block_sums(row_pack, row_map, section):
    rows_count, points = row_pack.shape[0], row_pack.shape[-1]
    zero_step = jnp.zeros((rows_count,), jnp.int32)
    ref_pos, cur_pos, vol_pts, health_pts = positions(row_pack, zero_step, zero_step)
    weights = bond_weights(health_pts, health_pts, zero_step, zero_step)
    if section == "shape":
        feats = shape_features(ref_pos, cur_pos, vol_pts)
        return shape_terms(jnp.einsum("gcj,gij->gci", feats, weights, precision=highest), ref_pos, cur_pos)
    stress_map = row_map.reshape(rows_count, 3, 3, points)
    feats = force_features(ref_pos, stress_map, vol_pts)
    return force_terms(jnp.einsum("gcj,gij->gci", feats, weights, precision=highest), ref_pos, stress_map)


def pair_sums(ext_pack, ext_map, slot_list, section):
    ext_x, ext_y, fields, points = ext_pack.shape
    blocks = ext_x * ext_y
    flat_pack = ext_pack.reshape(blocks, fields, points)
    slot_count = slot_list.shape[0]
    turn_count = min(slot_count, 20)
    group_size = -(-slot_count // turn_count)
    filler = jnp.full((group_size * turn_count - slot_count, 4), -1, jnp.int32)
    padded_slots = jnp.concatenate([slot_list, filler], axis=0)
    comp_width = 18 if section == "shape" else 3
    block_ids = jnp.arange(blocks, dtype=jnp.int32)

    def one_group(running, group_slots):
        usable = group_slots[:, 0] >= 0
        first_block = jnp.where(usable, group_slots[:, 0] * ext_y + group_slots[:, 1], 0)
        second_block = jnp.where(usable, group_slots[:, 2] * ext_y + group_slots[:, 3], 0)
        step_x = jnp.where(usable, group_slots[:, 2] - group_slots[:, 0], 0)
        step_y = jnp.where(usable, group_slots[:, 3] - group_slots[:, 1], 0)
        if section == "shape":
            map_first, map_second = None, None
        else:
            flat_map = ext_map.reshape(blocks, 3, 3, points)
            map_first, map_second = flat_map[first_block], flat_map[second_block]
        to_first, to_second = tile_terms(flat_pack[first_block], flat_pack[second_block], map_first, map_second, step_x, step_y, section)
        hit_first = ((first_block[:, None] == block_ids[None]) & usable[:, None]).astype(jnp.float32)
        hit_second = ((second_block[:, None] == block_ids[None]) & usable[:, None]).astype(jnp.float32)
        running = running + jnp.dot(hit_first.T, to_first.reshape(group_size, comp_width * points), precision=highest, preferred_element_type=jnp.float32)
        running = running + jnp.dot(hit_second.T, to_second.reshape(group_size, comp_width * points), precision=highest, preferred_element_type=jnp.float32)
        return running, None

    running, _ = lax.scan(one_group, jnp.zeros((blocks, comp_width * points), jnp.float32), padded_slots.reshape(turn_count, group_size, 4))
    return running.reshape(ext_x, ext_y, comp_width, points)


def product_three(left_mat, right_mat):
    entry_list = []
    for row_index in range(3):
        for col_index in range(3):
            entry_list.append(left_mat[..., 3 * row_index, :] * right_mat[..., col_index, :] + left_mat[..., 3 * row_index + 1, :] * right_mat[..., 3 + col_index, :] + left_mat[..., 3 * row_index + 2, :] * right_mat[..., 6 + col_index, :])
    return jnp.stack(entry_list, axis=-2)


def invert_three(matrix):
    entry = [matrix[..., slot_index, :] for slot_index in range(9)]
    cof_00 = entry[4] * entry[8] - entry[5] * entry[7]
    cof_01 = entry[5] * entry[6] - entry[3] * entry[8]
    cof_02 = entry[3] * entry[7] - entry[4] * entry[6]
    cof_10 = entry[2] * entry[7] - entry[1] * entry[8]
    cof_11 = entry[0] * entry[8] - entry[2] * entry[6]
    cof_12 = entry[1] * entry[6] - entry[0] * entry[7]
    cof_20 = entry[1] * entry[5] - entry[2] * entry[4]
    cof_21 = entry[2] * entry[3] - entry[0] * entry[5]
    cof_22 = entry[0] * entry[4] - entry[1] * entry[3]
    determinant = entry[0] * cof_00 + entry[1] * cof_01 + entry[2] * cof_02
    adjugate = jnp.stack([cof_00, cof_10, cof_20, cof_01, cof_11, cof_21, cof_02, cof_12, cof_22], axis=-2)
    return adjugate / determinant[..., None, :]


def material(shape_sums, damage):
    identity = jnp.eye(3, dtype=jnp.float32).reshape(9)[:, None]
    inverse = invert_three(shape_sums[..., 0:9, :] + identity)
    deform_grad = product_three(shape_sums[..., 9:18, :], inverse)
    strain = 0.5 * (product_three(deform_grad[..., transpose_order, :], deform_grad) - identity)
    strain_trace = strain[..., 0, :] + strain[..., 4, :] + strain[..., 8, :]
    second_pk = lame_first * strain_trace[..., None, :] * identity + 2.0 * shear_modulus * strain
    first_pk = product_three(deform_grad, second_pk) * (1.0 - damage.astype(jnp.float32))[..., None, :]
    return deform_grad, product_three(first_pk, inverse)


def reference(displacement, volume, health, damage, block_pairs):
    point_pack = jnp.concatenate([displacement, volume[:, :, None], health[:, :, None]], axis=2)
    padded_pack = jnp.pad(point_pack, ((1, 1), (1, 1), (0, 0), (0, 0)))
    slot_lists = block_pairs.reshape(N_GX * N_GY, PAIRS_MAX, 4)
    device_ids = jnp.arange(N_GX * N_GY, dtype=jnp.int32)
    zero_index = jnp.zeros((), jnp.int32)

    def corner_of(device):
        return ((device // N_GY) * BX_DEV).astype(jnp.int32), ((device % N_GY) * BY_DEV).astype(jnp.int32)

    def window_of(array, device):
        corner_x, corner_y = corner_of(device)
        return lax.dynamic_slice(array, (corner_x, corner_y, zero_index, zero_index), (BX_DEV + 2, BY_DEV + 2) + array.shape[2:])

    def accumulate_pairs(section, padded_map, comp_width):
        def one_device(running, items):
            device, slot_list = items
            map_window = None if section == "shape" else window_of(padded_map, device)
            tile_total = pair_sums(window_of(padded_pack, device), map_window, slot_list, section)
            corner_x, corner_y = corner_of(device)
            start = (corner_x, corner_y, zero_index, zero_index)
            current = lax.dynamic_slice(running, start, tile_total.shape)
            return lax.dynamic_update_slice(running, current + tile_total, start), None

        running = jnp.zeros((PLATE_X + 2, PLATE_Y + 2, comp_width, PTS_BLK), jnp.float32)
        running, _ = lax.scan(one_device, running, (device_ids, slot_lists))
        return running[1:-1, 1:-1]

    own_shape = lax.map(lambda row_pack: block_sums(row_pack, None, "shape"), point_pack)
    shape_sums = accumulate_pairs("shape", None, 18) + own_shape
    deform_grad, stress_map = material(shape_sums, damage)
    padded_map = jnp.pad(stress_map, ((1, 1), (1, 1), (0, 0), (0, 0)))
    own_force = lax.map(lambda row_items: block_sums(row_items[0], row_items[1], "force"), (point_pack, stress_map))
    force_density = accumulate_pairs("force", padded_map, 3) + own_force
    return deform_grad, force_density
```

```python
import jax
import jax.numpy as jnp
from jax import lax
from jax.experimental import pallas as pl
from jax.experimental.pallas import tpu as pltpu
from jax.sharding import PartitionSpec as P

MESH = pl.DeviceIdType.MESH
LANES = 128
BXN, BYN = 8, 4
LAME, SHEAR = 24.0, 16.0
COLUMNS = {}
for _dy in range(-3, 4):
    for _dz in range(-3, 4):
        _rest = 9 - _dy * _dy - _dz * _dz
        if _rest >= 0:
            COLUMNS[(_dy, _dz)] = max(k for k in range(4) if k * k <= _rest)
W_AT, _n = {}, 0
for _key, _m in COLUMNS.items():
    W_AT[_key] = _n
    _n += 2 * _m + 1
W_COUNT = _n
X_SLOTS = ((-1, 0), (-1, 1), (-1, -1), (1, 0), (1, 1), (1, -1))


def direction(cx, cy):
    q = 3 * cx + cy
    return q - 1 if q > 0 else 3 - q


def iota(axis):
    return lax.broadcasted_iota(jnp.int32, (8, LANES), axis)


def take(tile, index):
    return jnp.take_along_axis(tile, index, axis=1, mode="promise_in_bounds")


def lane_roll(array, by):
    by = by % LANES
    return array if by == 0 else pltpu.roll(array, by, axis=array.ndim - 1)


def row_roll(tile, by):
    return pltpu.roll(tile, by % 8, axis=0)


def inverse_of(m):
    c00 = m[4] * m[8] - m[5] * m[7]
    c01 = m[5] * m[6] - m[3] * m[8]
    c02 = m[3] * m[7] - m[4] * m[6]
    c10 = m[2] * m[7] - m[1] * m[8]
    c11 = m[0] * m[8] - m[2] * m[6]
    c12 = m[1] * m[6] - m[0] * m[7]
    c20 = m[1] * m[5] - m[2] * m[4]
    c21 = m[2] * m[3] - m[0] * m[5]
    c22 = m[0] * m[4] - m[1] * m[3]
    scale = 1.0 / (m[0] * c00 + m[1] * c01 + m[2] * c02)
    return [c * scale for c in (c00, c10, c20, c01, c11, c21, c02, c12, c22)]


def product(a, b):
    return [
        a[3 * r] * b[c] + a[3 * r + 1] * b[3 + c] + a[3 * r + 2] * b[6 + c]
        for r in range(3)
        for c in range(3)
    ]


def times(k, value):
    return value if k == 1 else (-value if k == -1 else float(k) * value)


def add(total, value):
    return value if total is None else total + value


def extend(own, low_row, high_row, row, s):
    if s < 0:
        return jnp.where(row == 0, low_row(s + 4), row_roll(own[s + 4], 1))
    if s > 3:
        return jnp.where(row == 7, high_row(s - 4), row_roll(own[s - 4], -1))
    return own[s]


def kernel(
    disp, vol, hea, dam, pairs, dg_out, force_out,
    ysend, yrecv, xsend, xrecv, ysend2, yrecv2, xsend2, xrecv2,
    fields, own_u, health_m, weights, sums, ystress, xstress, force,
    ssem, rsem, ssem2, rsem2,
):
    n_gx, n_gy = lax.axis_size("gx"), lax.axis_size("gy")
    me_x, me_y = lax.axis_index("gx"), lax.axis_index("gy")

    def device(cx, cy):
        return (lax.rem(me_x + (cx + n_gx), n_gx), lax.rem(me_y + (cy + n_gy), n_gy))

    barrier = pltpu.get_barrier_semaphore()
    for cx in (-1, 0, 1):
        for cy in (-1, 0, 1):
            if cx or cy:
                pl.semaphore_signal(barrier, inc=1, device_id=device(cx, cy), device_id_type=MESH)

    row, lane = iota(0), iota(1)
    block_y, y_in, z_at = lane // 32, (lane // 8) % 4, lane % 8
    y_at = lane // 8

    ax, ay, bx, by = (pairs[i : i + 1, :] for i in range(4))
    q = 3 * (bx - ax) + (by - ay) - 1
    wide = lax.broadcasted_iota(jnp.int32, (LANES, 256), 0)
    tall = lax.broadcasted_iota(jnp.int32, (8, 256), 0)
    flags = None
    for at_x, at_y, way in ((ax, ay, q), (bx, by, q + 4)):
        in_row = jnp.where(tall == at_x - 1, 1.0, 0.0)
        in_lane = jnp.where(wide == 8 * at_y + way, 1.0, 0.0)
        flags = add(flags, lax.dot_general(
            in_row, in_lane, (((1,), (1,)), ((), ())), preferred_element_type=jnp.float32))

    to_x = [16 * z_at + 4 * y_in + t for t in range(4)]
    raw = []
    for b in range(BYN):
        v = vol[:, b, :]
        raw.append([hea[:, b, :], v] + [v * disp[:, b, c, :] for c in range(3)])
    u_raw = [[disp[:, b, c, :] for b in range(BYN)] for c in range(3)]

    def lattice_tile(of_block, t):
        got = take(of_block[0], to_x[t])
        for b in range(1, BYN):
            got = jnp.where(block_y == b, take(of_block[b], to_x[t]), got)
        return got

    own = []
    for f in range(5):
        ysend[0, f] = raw[0][f]
        ysend[1, f] = raw[3][f]
        own.append([lattice_tile([raw[b][f] for b in range(BYN)], t) for t in range(4)])
        for t in range(3):
            xsend[0, 3 * f + t : 3 * f + t + 1, :] = own[f][t][0:1]
            xsend[1, 3 * f + t : 3 * f + t + 1, :] = own[f][t + 1][7:8]
    ysend[0, 5] = flags
    ysend[1, 5] = flags
    xsend[0, 15:16, :] = flags[0:1]
    xsend[1, 15:16, :] = flags[7:8]
    pl.semaphore_wait(barrier, 8)

    def exchange(x_src, x_dst, y_src, y_dst, sends, recvs):
        copies = []
        for n, (cx, cy) in enumerate(X_SLOTS):
            copies.append(pltpu.make_async_remote_copy(
                src_ref=x_src.at[0 if cx == 1 else 1], dst_ref=x_dst.at[n],
                send_sem=sends.at[n], recv_sem=recvs.at[n],
                device_id=device(-cx, -cy), device_id_type=MESH))
        for n, cy in enumerate((1, -1)):
            copies.append(pltpu.make_async_remote_copy(
                src_ref=y_src.at[n], dst_ref=y_dst.at[n],
                send_sem=sends.at[6 + n], recv_sem=recvs.at[6 + n],
                device_id=device(0, -cy), device_id_type=MESH))
        for copy in copies:
            copy.start()
        return copies

    copies = exchange(xsend, xrecv, ysend, yrecv, ssem, rsem)

    for c in range(3):
        for t in range(4):
            own_u[c, t] = lattice_tile(u_raw[c], t)
    for copy in copies:
        copy.wait_recv()

    def flag_ext(tile, slots, cx):
        if cx == 0:
            return tile
        r = xrecv[slots[cx], 15:16, :]
        if cx < 0:
            return jnp.where(row == 0, r, row_roll(tile, 1))
        return jnp.where(row == 7, r, row_roll(tile, -1))

    seen = {}
    for cy, tile, slots in (
        (0, flags, {-1: 0, 1: 3}), (1, yrecv[0, 5], {-1: 1, 1: 4}), (-1, yrecv[1, 5], {-1: 2, 1: 5})
    ):
        for cx in (-1, 0, 1):
            seen[(cx, cy)] = flag_ext(tile, slots, cx)
    enabled = {}
    for cx in (-1, 0, 1):
        for cy in (-1, 0, 1):
            if cx == 0 and cy == 0:
                continue
            mine = take(flags, 8 * (block_y + 1) + direction(cx, cy))
            back = direction(-cx, -cy)
            theirs = take(seen[(cx, 0)], 8 * (block_y + cy + 1) + back)
            if cy == 1:
                theirs = jnp.where(block_y == 3, take(seen[(cx, 1)], 8 + back + 0 * lane), theirs)
            if cy == -1:
                theirs = jnp.where(block_y == 0, take(seen[(cx, -1)], 32 + back + 0 * lane), theirs)
            enabled[(cx, cy)] = jnp.minimum(jnp.maximum(mine, theirs), 1.0)

    for dy in range(-3, 4):
        deep = max(m for (a, _), m in COLUMNS.items() if a == dy)
        by_cx = {}
        for cx in (-1, 0, 1):
            near = enabled.get((cx, 0))
            if dy > 0:
                far = enabled[(cx, 1)]
                near = 1.0 if near is None else near
                by_cx[cx] = jnp.where(y_in + dy >= 4, far, near)
            elif dy < 0:
                far = enabled[(cx, -1)]
                near = 1.0 if near is None else near
                by_cx[cx] = jnp.where(y_in + dy < 0, far, near)
            else:
                by_cx[cx] = near
        for dx in range(-deep, deep + 1):
            for t in range(4):
                cx = (t + dx) // 4
                h = own[0][t]
                health_m[dy + 3, dx + 3, t] = h if by_cx[cx] is None else h * by_cx[cx]

    side_lane = lane < 64
    side = y_at < 8
    for f in range(5):
        beside = []
        for t in range(4):
            beside.append(jnp.where(side, take(yrecv[0, f], to_x[t]), take(yrecv[1, f], to_x[t])))

        def row_at(slot, t, f=f):
            return xrecv[slot, 3 * f + t : 3 * f + t + 1, :]

        def corner(low, high, t, f=f):
            return jnp.where(side_lane[0:1], row_at(low, t, f), row_at(high, t, f))

        for s in range(-3, 7):
            inner = extend(own[f], lambda t: row_at(0, t - 1), lambda t: row_at(3, t), row, s)
            fields[3, f, s + 3] = inner
            if s < -2 or s > 5:
                continue
            outer = extend(beside, lambda t: corner(1, 2, t - 1), lambda t: corner(4, 5, t), row, s)
            for k in (1, 2, 3):
                if k == 3 and not 0 <= s <= 3:
                    continue
                fields[3 + k, f, s + 3] = jnp.where(y_at < k, outer, inner)
                fields[3 - k, f, s + 3] = jnp.where(y_at >= 16 - k, outer, inner)

    z_ok = {dz: (z_at + dz >= 0) & (z_at + dz < 8) for dz in range(-3, 4)}

    def first_sums(half, carry):
        base = 2 * half
        total = {}
        for dy in range(-3, 4):
            part = {}
            for dz in range(-3, 4):
                if (dy, dz) not in COLUMNS:
                    continue
                deep = COLUMNS[(dy, dz)]
                turn = -(8 * dy + dz)
                src = [
                    lane_roll(fields[dy + 3, f, pl.ds(base + 3 - deep, 2 + 2 * deep)], turn)
                    for f in range(5)
                ]
                if dz != 0:
                    src[0] = jnp.where(z_ok[dz][None], src[0], 0.0)
                a0, a1, a2 = [None] * 4, [None] * 4, None
                for reach in range(deep + 1):
                    terms = []
                    for dx in (reach, -reach) if reach else (0,):
                        lo = deep + dx
                        w = jnp.minimum(
                            health_m[dy + 3, dx + 3, pl.ds(base, 2)], src[0][lo : lo + 2])
                        weights[W_AT[(dy, dz)] + lo, pl.ds(base, 2)] = w
                        if dy == 0 and dz == 0 and dx == 0:
                            continue
                        terms.append([w * src[k + 1][lo : lo + 2] for k in range(4)])
                    if not terms:
                        continue
                    for k in range(4):
                        both = terms[0][k] if reach == 0 else terms[0][k] + terms[1][k]
                        a0[k] = add(a0[k], both)
                        if reach:
                            a1[k] = add(a1[k], times(reach, terms[0][k] - terms[1][k]))
                            if k == 0:
                                a2 = add(a2, times(reach * reach, both))
                for k in range(4):
                    if dy != 0:
                        part["y", k] = add(part.get(("y", k)), a0[k])
                    if dz != 0:
                        part["z", k] = add(part.get(("z", k)), times(dz, a0[k]))
                    if a1[k] is not None:
                        part["x", k] = add(part.get(("x", k)), a1[k])
                if dz != 0:
                    part["zz"] = add(part.get("zz"), times(dz * dz, a0[0]))
                    if a1[0] is not None:
                        part["xz"] = add(part.get("xz"), times(dz, a1[0]))
                if a2 is not None:
                    part["xx"] = add(part.get("xx"), a2)
            for k in range(4):
                if dy != 0:
                    total["y", k] = add(total.get(("y", k)), times(dy, part["y", k]))
                for name in ("x", "z"):
                    if (name, k) in part:
                        total[name, k] = add(total.get((name, k)), part[name, k])
            if dy != 0:
                total["yy"] = add(total.get("yy"), times(dy * dy, part["y", 0]))
                for name, to in (("x", "xy"), ("z", "yz")):
                    if (name, 0) in part:
                        total[to] = add(total.get(to), times(dy, part[name, 0]))
            for name in ("xx", "zz", "xz"):
                if name in part:
                    total[name] = add(total.get(name), part[name])
        order = ["xx", "xy", "xz", "yy", "yz", "zz"] + [(a, k) for k in range(4) for a in "xyz"]
        for n, name in enumerate(order):
            sums[n, pl.ds(base, 2)] = total[name]
        return carry

    lax.fori_loop(0, 2, first_sums, 0)

    dam_raw = [dam[:, b, :].astype(jnp.float32) for b in range(BYN)]
    to_raw = [8 * (4 * b + (lane // 4) % 4) + lane // 16 for b in range(BYN)]
    x_in = lane % 4

    def block_tile(of_x, b):
        got = take(of_x[0], to_raw[b])
        for t in range(1, 4):
            got = jnp.where(x_in == t, take(of_x[t], to_raw[b]), got)
        return got

    deform, stress = [], []
    for t in range(4):
        kxx, kxy, kxz, kyy, kyz, kzz = (sums[n, t] for n in range(6))
        span = [sums[6 + n, t] for n in range(3)]
        sym = [kxx, kxy, kxz, kxy, kyy, kyz, kxz, kyz, kzz]
        moment = [
            sym[3 * c + d] + sums[9 + 3 * c + d, t] - own_u[c, t] * span[d]
            for c in range(3) for d in range(3)
        ]
        shape = [sym[n] + 1.0 if n % 4 == 0 else sym[n] for n in range(9)]
        inv = inverse_of(shape)
        grad = product(moment, inv)
        flip = [grad[3 * (n % 3) + n // 3] for n in range(9)]
        twice = product(flip, grad)
        strain = [0.5 * (twice[n] - 1.0) if n % 4 == 0 else 0.5 * twice[n] for n in range(9)]
        trace = LAME * (strain[0] + strain[4] + strain[8])
        second = [
            trace + 2.0 * SHEAR * strain[n] if n % 4 == 0 else 2.0 * SHEAR * strain[n]
            for n in range(9)
        ]
        intact = 1.0 - lattice_tile(dam_raw, t)
        first = [e * intact for e in product(grad, second)]
        mapped = product(first, inv)
        for c in range(3):
            force[c, t] = mapped[3 * c] * span[0] + mapped[3 * c + 1] * span[1] + mapped[3 * c + 2] * span[2]
        v = own[1][t]
        deform.append(grad)
        stress.append([v * e for e in mapped])

    for n in range(9):
        of_x = [stress[t][n] for t in range(4)]
        for t in range(3):
            xsend2[0, 3 * n + t : 3 * n + t + 1, :] = of_x[t][0:1]
            xsend2[1, 3 * n + t : 3 * n + t + 1, :] = of_x[t + 1][7:8]
        low = of_x[0]
        high = lane_roll(of_x[0], 32)
        for t in range(1, 4):
            low = jnp.where(block_y == t, lane_roll(of_x[t], 32 * t), low)
            high = jnp.where(block_y == t, lane_roll(of_x[t], 32 * (t - 3)), high)
        ysend2[0, n] = low
        ysend2[1, n] = high
        for t in range(4):
            xstress[n, t] = of_x[t]

    copies2 = exchange(xsend2, xrecv2, ysend2, yrecv2, ssem2, rsem2)

    for n in range(9):
        for b in range(BYN):
            dg_out[b, n] = block_tile([deform[t][n] for t in range(4)], b)
    for copy in copies2:
        copy.wait_recv()

    for n in range(9):
        mine = [xstress[n, t] for t in range(4)]
        beside = []
        for t in range(4):
            beside.append(jnp.where(
                side, lane_roll(yrecv2[0, n], -32 * t), lane_roll(yrecv2[1, n], 32 * (3 - t))))

        def row_at2(slot, t, n=n):
            return xrecv2[slot, 3 * n + t : 3 * n + t + 1, :]

        def corner2(low, high, t):
            return jnp.where(side_lane[0:1], row_at2(low, t), row_at2(high, t))

        for s in range(-3, 7):
            inner = extend(mine, lambda t: row_at2(0, t - 1), lambda t: row_at2(3, t), row, s)
            ystress[3, n, s + 3] = inner
            if s < -2 or s > 5:
                continue
            outer = extend(beside, lambda t: corner2(1, 2, t - 1), lambda t: corner2(4, 5, t), row, s)
            for k in (1, 2, 3):
                if k == 3 and not 0 <= s <= 3:
                    continue
                ystress[3 + k, n, s + 3] = jnp.where(y_at < k, outer, inner)
                ystress[3 - k, n, s + 3] = jnp.where(y_at >= 16 - k, outer, inner)

    def second_sums(c, carry):
        total = force[c]
        for dy in range(-3, 4):
            for dz in range(-3, 4):
                if (dy, dz) not in COLUMNS:
                    continue
                deep = COLUMNS[(dy, dz)]
                turn = -(8 * dy + dz)
                tiles = pl.ds(3 - deep, 4 + 2 * deep)
                fixed = None
                if dy != 0:
                    fixed = add(fixed, times(dy, ystress[dy + 3, 3 * c + 1, tiles]))
                if dz != 0:
                    fixed = add(fixed, times(dz, ystress[dy + 3, 3 * c + 2, tiles]))
                if fixed is not None:
                    fixed = lane_roll(fixed, turn)
                slope = lane_roll(ystress[dy + 3, 3 * c, tiles], turn) if deep else None
                for dx in range(-deep, deep + 1):
                    lo = deep + dx
                    value = None if fixed is None else fixed[lo : lo + 4]
                    if dx != 0:
                        value = add(value, times(dx, slope[lo : lo + 4]))
                    if value is not None:
                        total = total + weights[W_AT[(dy, dz)] + lo] * value
        force[c] = total
        return carry

    lax.fori_loop(0, 3, second_sums, 0)
    for c in range(3):
        for b in range(BYN):
            force_out[b, c] = block_tile([force[c, t] for t in range(4)], b)
    for copy in copies + copies2:
        copy.wait_send()


def local(displacement, volume, health, damage, block_pairs):
    pairs = jnp.pad(block_pairs[0, 0].T, ((0, 0), (0, 256 - block_pairs.shape[2])), constant_values=-1)
    f32 = jnp.float32
    vmem = pl.BlockSpec(memory_space=pltpu.VMEM)
    dg, force = pl.pallas_call(
        kernel,
        out_shape=(
            jax.ShapeDtypeStruct((BYN, 9, BXN, LANES), f32),
            jax.ShapeDtypeStruct((BYN, 3, BXN, LANES), f32),
        ),
        in_specs=[vmem] * 5,
        out_specs=(vmem, vmem),
        scratch_shapes=[
            pltpu.VMEM((2, 6, 8, LANES), f32),
            pltpu.VMEM((2, 6, 8, LANES), f32),
            pltpu.VMEM((2, 16, LANES), f32),
            pltpu.VMEM((6, 16, LANES), f32),
            pltpu.VMEM((2, 9, 8, LANES), f32),
            pltpu.VMEM((2, 9, 8, LANES), f32),
            pltpu.VMEM((2, 32, LANES), f32),
            pltpu.VMEM((6, 32, LANES), f32),
            pltpu.VMEM((7, 5, 10, 8, LANES), f32),
            pltpu.VMEM((3, 4, 8, LANES), f32),
            pltpu.VMEM((7, 7, 4, 8, LANES), f32),
            pltpu.VMEM((W_COUNT, 4, 8, LANES), f32),
            pltpu.VMEM((18, 4, 8, LANES), f32),
            pltpu.VMEM((7, 9, 10, 8, LANES), f32),
            pltpu.VMEM((9, 4, 8, LANES), f32),
            pltpu.VMEM((3, 4, 8, LANES), f32),
            pltpu.SemaphoreType.DMA((8,)),
            pltpu.SemaphoreType.DMA((8,)),
            pltpu.SemaphoreType.DMA((8,)),
            pltpu.SemaphoreType.DMA((8,)),
        ],
        compiler_params=pltpu.CompilerParams(collective_id=0, has_side_effects=True),
        name="peridynamics",
    )(displacement, volume, health, damage, pairs)
    return jnp.transpose(dg, (2, 0, 1, 3)), jnp.transpose(force, (2, 0, 1, 3))


def solution(mesh):
    in_specs = (
        P("gx", "gy", None, None),
        P("gx", "gy", None),
        P("gx", "gy", None),
        P("gx", "gy", None),
        P("gx", "gy", None, None),
    )
    out_specs = (P("gx", "gy", None, None), P("gx", "gy", None, None))
    return jax.shard_map(local, mesh=mesh, in_specs=in_specs, out_specs=out_specs, check_vma=False)
```

```python
import jax
import jax.numpy as jnp
from jax import lax
from jax.experimental import pallas as pl
from jax.experimental.pallas import tpu as pltpu
from jax.sharding import PartitionSpec as P

MESH = pl.DeviceIdType.MESH
LANES = 128
BXN, BYN = 8, 4
LAME, SHEAR = 24.0, 16.0
COLUMNS = {}
for _dy in range(-3, 4):
    for _dz in range(-3, 4):
        _rest = 9 - _dy * _dy - _dz * _dz
        if _rest >= 0:
            COLUMNS[(_dy, _dz)] = max(k for k in range(4) if k * k <= _rest)
W_AT, _n = {}, 0
for _key, _m in COLUMNS.items():
    W_AT[_key] = _n
    _n += 2 * _m + 1
W_COUNT = _n
CORNERS = ((-1, 1), (-1, -1), (1, 1), (1, -1))


def direction(cx, cy):
    q = 3 * cx + cy
    return q - 1 if q > 0 else 3 - q


def iota(axis):
    return lax.broadcasted_iota(jnp.int32, (8, LANES), axis)


def take(tile, index):
    return jnp.take_along_axis(tile, index, axis=1, mode="promise_in_bounds")


def lane_roll(array, by):
    by = by % LANES
    return array if by == 0 else pltpu.roll(array, by, axis=array.ndim - 1)


def row_roll(tile, by):
    return pltpu.roll(tile, by % 8, axis=0)


def inverse_of(m):
    c00 = m[4] * m[8] - m[5] * m[7]
    c01 = m[5] * m[6] - m[3] * m[8]
    c02 = m[3] * m[7] - m[4] * m[6]
    c10 = m[2] * m[7] - m[1] * m[8]
    c11 = m[0] * m[8] - m[2] * m[6]
    c12 = m[1] * m[6] - m[0] * m[7]
    c20 = m[1] * m[5] - m[2] * m[4]
    c21 = m[2] * m[3] - m[0] * m[5]
    c22 = m[0] * m[4] - m[1] * m[3]
    scale = 1.0 / (m[0] * c00 + m[1] * c01 + m[2] * c02)
    return [c * scale for c in (c00, c10, c20, c01, c11, c21, c02, c12, c22)]


def product(a, b):
    return [
        a[3 * r] * b[c] + a[3 * r + 1] * b[3 + c] + a[3 * r + 2] * b[6 + c]
        for r in range(3)
        for c in range(3)
    ]


def times(k, value):
    return value if k == 1 else (-value if k == -1 else float(k) * value)


def add(total, value):
    return value if total is None else total + value


def extend(own, low_row, high_row, row, s):
    if s < 0:
        return jnp.where(row == 0, low_row(s + 4), row_roll(own[s + 4], 1))
    if s > 3:
        return jnp.where(row == 7, high_row(s - 4), row_roll(own[s - 4], -1))
    return own[s]


def kernel(
    disp_in, vol_in, hea_in, dam_in, pairs_in, dg_out, force_out,
    disp, vol, hea, dam, pairs,
    ysend, yrecv, xsend, xrecv, csend, crecv,
    ysend2, yrecv2, xsend2, xrecv2, csend2, crecv2,
    fields, own_u, health_m, weights, sums, ystress, xstress, force,
    isem, ssem, rsem, ssem2, rsem2,
):
    loads = [
        pltpu.make_async_copy(src, dst, isem.at[n])
        for n, (src, dst) in enumerate((
            (pairs_in, pairs), (disp_in, disp), (vol_in, vol), (hea_in, hea), (dam_in, dam)))
    ]
    for load in loads:
        load.start()
    n_gx, n_gy = lax.axis_size("gx"), lax.axis_size("gy")
    me_x, me_y = lax.axis_index("gx"), lax.axis_index("gy")

    def device(cx, cy):
        return (lax.rem(me_x + (cx + n_gx), n_gx), lax.rem(me_y + (cy + n_gy), n_gy))

    barrier = pltpu.get_barrier_semaphore()
    for cx in (-1, 0, 1):
        for cy in (-1, 0, 1):
            if cx or cy:
                pl.semaphore_signal(barrier, inc=1, device_id=device(cx, cy), device_id_type=MESH)

    row, lane = iota(0), iota(1)
    block_y, y_in, z_at = lane // 32, (lane // 8) % 4, lane % 8
    y_at = lane // 8

    for load in loads:
        load.wait()
    slots = pairs.shape[1]
    ax, ay, bx, by = (pairs[i : i + 1, :] for i in range(4))
    q = 3 * (bx - ax) + (by - ay) - 1
    wide = lax.broadcasted_iota(jnp.int32, (LANES, slots), 0)
    tall = lax.broadcasted_iota(jnp.int32, (8, slots), 0)
    flags = None
    for at_x, at_y, way in ((ax, ay, q), (bx, by, q + 4)):
        in_row = jnp.where(tall == at_x - 1, 1.0, 0.0)
        in_lane = jnp.where(wide == 8 * at_y + way, 1.0, 0.0)
        flags = add(flags, lax.dot_general(
            in_row, in_lane, (((1,), (1,)), ((), ())), preferred_element_type=jnp.float32))

    def u_tile(c, b):
        return disp[pl.ds(4 * c + b, 8, stride=12), :]

    def row_tile(array, b):
        return array[pl.ds(b, 8, stride=4), :]

    raw = []
    for b in range(BYN):
        v = row_tile(vol, b)
        raw.append([row_tile(hea, b), v] + [v * u_tile(c, b) for c in range(3)])
    for n, b in enumerate((0, 3)):
        for f in range(5):
            ysend[n, f] = raw[b][f]
            for m, r in enumerate((0, 7)):
                csend[2 * m + n, f : f + 1, :] = raw[b][f][r : r + 1]
        ysend[n, 5] = flags
        for m, r in enumerate((0, 7)):
            csend[2 * m + n, 5:6, :] = flags[r : r + 1]
    for m, r in enumerate((0, 7)):
        xsend[m, 0:12, :] = disp[12 * r : 12 * r + 12, :]
        xsend[m, 12:16, :] = vol[4 * r : 4 * r + 4, :]
        xsend[m, 16:20, :] = hea[4 * r : 4 * r + 4, :]
        xsend[m, 20:21, :] = flags[r : r + 1]
    pl.semaphore_wait(barrier, 8)

    def exchange(x_pair, y_pair, c_pair, sends, recvs):
        moves = []
        for n, cx in enumerate((-1, 1)):
            moves.append((x_pair[0].at[1 - n], x_pair[1].at[n], -cx, 0))
        for n, cy in enumerate((1, -1)):
            moves.append((y_pair[0].at[n], y_pair[1].at[n], 0, -cy))
        for n, (cx, cy) in enumerate(CORNERS):
            at = 2 * (0 if cx == 1 else 1) + (0 if cy == 1 else 1)
            moves.append((c_pair[0].at[at], c_pair[1].at[n], -cx, -cy))
        copies = [
            pltpu.make_async_remote_copy(
                src_ref=src, dst_ref=dst, send_sem=sends.at[n], recv_sem=recvs.at[n],
                device_id=device(tx, ty), device_id_type=MESH)
            for n, (src, dst, tx, ty) in enumerate(moves)
        ]
        for copy in copies:
            copy.start()
        return copies

    copies = exchange((xsend, xrecv), (ysend, yrecv), (csend, crecv), ssem, rsem)

    to_x = [16 * z_at + 4 * y_in + t for t in range(4)]

    def lattice_tile(of_block, t):
        got = take(of_block[0], to_x[t])
        for b in range(1, BYN):
            got = jnp.where(block_y == b, take(of_block[b], to_x[t]), got)
        return got

    own = [[lattice_tile([raw[b][f] for b in range(BYN)], t) for t in range(4)] for f in range(5)]
    dam_raw = [row_tile(dam, b).astype(jnp.float32) for b in range(BYN)]
    for t in range(4):
        for c in range(3):
            own_u[c, t] = lattice_tile([u_tile(c, b) for b in range(BYN)], t)
        own_u[3, t] = 1.0 - lattice_tile(dam_raw, t)
    for copy in copies:
        copy.wait_recv()

    def flag_ext(tile, low, high, cx):
        if cx == 0:
            return tile
        if cx < 0:
            return jnp.where(row == 0, low, row_roll(tile, 1))
        return jnp.where(row == 7, high, row_roll(tile, -1))

    seen = {}
    for cy, tile, low, high in (
        (0, flags, xrecv[0, 20:21, :], xrecv[1, 20:21, :]),
        (1, yrecv[0, 5], crecv[0, 5:6, :], crecv[2, 5:6, :]),
        (-1, yrecv[1, 5], crecv[1, 5:6, :], crecv[3, 5:6, :]),
    ):
        for cx in (-1, 0, 1):
            seen[(cx, cy)] = flag_ext(tile, low, high, cx)
    enabled = {}
    for cx in (-1, 0, 1):
        for cy in (-1, 0, 1):
            if cx == 0 and cy == 0:
                continue
            mine = take(flags, 8 * (block_y + 1) + direction(cx, cy))
            back = direction(-cx, -cy)
            theirs = take(seen[(cx, 0)], 8 * (block_y + cy + 1) + back)
            if cy == 1:
                theirs = jnp.where(block_y == 3, take(seen[(cx, 1)], 8 + back + 0 * lane), theirs)
            if cy == -1:
                theirs = jnp.where(block_y == 0, take(seen[(cx, -1)], 32 + back + 0 * lane), theirs)
            enabled[(cx, cy)] = jnp.minimum(jnp.maximum(mine, theirs), 1.0)

    for dy in range(-3, 4):
        deep = max(m for (a, _), m in COLUMNS.items() if a == dy)
        by_cx = {}
        for cx in (-1, 0, 1):
            near = enabled.get((cx, 0))
            if dy > 0:
                far = enabled[(cx, 1)]
                near = 1.0 if near is None else near
                by_cx[cx] = jnp.where(y_in + dy >= 4, far, near)
            elif dy < 0:
                far = enabled[(cx, -1)]
                near = 1.0 if near is None else near
                by_cx[cx] = jnp.where(y_in + dy < 0, far, near)
            else:
                by_cx[cx] = near
        for dx in range(-deep, deep + 1):
            for t in range(4):
                cx = (t + dx) // 4
                h = own[0][t]
                health_m[dy + 3, dx + 3, t] = h if by_cx[cx] is None else h * by_cx[cx]

    side_lane = lane < 64
    edge = [
        jnp.concatenate([xrecv[0, 4 * k : 4 * k + 4, :], xrecv[1, 4 * k : 4 * k + 4, :]], axis=0)
        for k in (4, 3, 0, 1, 2)
    ]
    edge = edge[:2] + [edge[1] * e for e in edge[2:]]

    def edge_tile(f, t):
        got = jnp.where(row % 4 == block_y, take(edge[f], to_x[t]), 0.0)
        got = got + jnp.where(row % 2 == 0, row_roll(got, -1), row_roll(got, 1))
        return got + jnp.where(row % 4 < 2, row_roll(got, -2), row_roll(got, 2))

    corner_low = [
        jnp.where(side_lane, take(crecv[0], to_x[t]), take(crecv[1], to_x[t])) for t in range(4)]
    corner_high = [
        jnp.where(side_lane, take(crecv[2], to_x[t]), take(crecv[3], to_x[t])) for t in range(4)]
    for f in range(5):
        beside = []
        for t in range(4):
            beside.append(jnp.where(side_lane, take(yrecv[0, f], to_x[t]), take(yrecv[1, f], to_x[t])))
        rim = [edge_tile(f, t) for t in range(4)]

        for s in range(-3, 7):
            inner = extend(own[f], lambda t: rim[t], lambda t: rim[t], row, s)
            fields[3, f, s + 3] = inner
            if s < -2 or s > 5:
                continue
            outer = extend(
                beside, lambda t: corner_low[t][f : f + 1], lambda t: corner_high[t][f : f + 1], row, s)
            for k in (1, 2, 3):
                if k == 3 and not 0 <= s <= 3:
                    continue
                fields[3 + k, f, s + 3] = jnp.where(y_at < k, outer, inner)
                fields[3 - k, f, s + 3] = jnp.where(y_at >= 16 - k, outer, inner)

    z_ok = {dz: (z_at + dz >= 0) & (z_at + dz < 8) for dz in range(-3, 4)}

    def first_sums(half, carry):
        base = 2 * half
        total = {}
        for dy in range(-3, 4):
            part = {}
            for dz in range(-3, 4):
                if (dy, dz) not in COLUMNS:
                    continue
                deep = COLUMNS[(dy, dz)]
                turn = -(8 * dy + dz)
                src = [
                    lane_roll(fields[dy + 3, f, pl.ds(base + 3 - deep, 2 + 2 * deep)], turn)
                    for f in range(5)
                ]
                if dz != 0:
                    src[0] = jnp.where(z_ok[dz][None], src[0], 0.0)
                a0, a1, a2 = [None] * 4, [None] * 4, None
                for reach in range(deep + 1):
                    terms = []
                    for dx in (reach, -reach) if reach else (0,):
                        lo = deep + dx
                        w = jnp.minimum(
                            health_m[dy + 3, dx + 3, pl.ds(base, 2)], src[0][lo : lo + 2])
                        weights[W_AT[(dy, dz)] + lo, pl.ds(base, 2)] = w
                        if dy == 0 and dz == 0 and dx == 0:
                            continue
                        terms.append([w * src[k + 1][lo : lo + 2] for k in range(4)])
                    if not terms:
                        continue
                    for k in range(4):
                        both = terms[0][k] if reach == 0 else terms[0][k] + terms[1][k]
                        a0[k] = add(a0[k], both)
                        if reach:
                            a1[k] = add(a1[k], times(reach, terms[0][k] - terms[1][k]))
                            if k == 0:
                                a2 = add(a2, times(reach * reach, both))
                for k in range(4):
                    if dy != 0:
                        part["y", k] = add(part.get(("y", k)), a0[k])
                    if dz != 0:
                        part["z", k] = add(part.get(("z", k)), times(dz, a0[k]))
                    if a1[k] is not None:
                        part["x", k] = add(part.get(("x", k)), a1[k])
                if dz != 0:
                    part["zz"] = add(part.get("zz"), times(dz * dz, a0[0]))
                    if a1[0] is not None:
                        part["xz"] = add(part.get("xz"), times(dz, a1[0]))
                if a2 is not None:
                    part["xx"] = add(part.get("xx"), a2)
            for k in range(4):
                if dy != 0:
                    total["y", k] = add(total.get(("y", k)), times(dy, part["y", k]))
                for name in ("x", "z"):
                    if (name, k) in part:
                        total[name, k] = add(total.get((name, k)), part[name, k])
            if dy != 0:
                total["yy"] = add(total.get("yy"), times(dy * dy, part["y", 0]))
                for name, to in (("x", "xy"), ("z", "yz")):
                    if (name, 0) in part:
                        total[to] = add(total.get(to), times(dy, part[name, 0]))
            for name in ("xx", "zz", "xz"):
                if name in part:
                    total[name] = add(total.get(name), part[name])
        order = ["xx", "xy", "xz", "yy", "yz", "zz"] + [(a, k) for k in range(4) for a in "xyz"]
        for n, name in enumerate(order):
            sums[n, pl.ds(base, 2)] = total[name]
        return carry

    lax.fori_loop(0, 2, first_sums, 0)

    to_raw = [8 * (4 * b + (lane // 4) % 4) + lane // 16 for b in range(BYN)]
    x_in = lane % 4

    def block_tile(of_x, b):
        got = take(of_x[0], to_raw[b])
        for t in range(1, 4):
            got = jnp.where(x_in == t, take(of_x[t], to_raw[b]), got)
        return got

    deform, stress = [], []
    for t in range(4):
        kxx, kxy, kxz, kyy, kyz, kzz = (sums[n, t] for n in range(6))
        span = [sums[6 + n, t] for n in range(3)]
        sym = [kxx, kxy, kxz, kxy, kyy, kyz, kxz, kyz, kzz]
        moment = [
            sym[3 * c + d] + sums[9 + 3 * c + d, t] - own_u[c, t] * span[d]
            for c in range(3) for d in range(3)
        ]
        shape = [sym[n] + 1.0 if n % 4 == 0 else sym[n] for n in range(9)]
        inv = inverse_of(shape)
        grad = product(moment, inv)
        flip = [grad[3 * (n % 3) + n // 3] for n in range(9)]
        twice = product(flip, grad)
        strain = [0.5 * (twice[n] - 1.0) if n % 4 == 0 else 0.5 * twice[n] for n in range(9)]
        trace = LAME * (strain[0] + strain[4] + strain[8])
        second = [
            trace + 2.0 * SHEAR * strain[n] if n % 4 == 0 else 2.0 * SHEAR * strain[n]
            for n in range(9)
        ]
        first = [e * own_u[3, t] for e in product(grad, second)]
        mapped = product(first, inv)
        for c in range(3):
            force[c, t] = mapped[3 * c] * span[0] + mapped[3 * c + 1] * span[1] + mapped[3 * c + 2] * span[2]
        v = own[1][t]
        deform.append(grad)
        stress.append([v * e for e in mapped])

    for n in range(9):
        of_x = [stress[t][n] for t in range(4)]
        for t in range(3):
            xsend2[0, 3 * n + t : 3 * n + t + 1, :] = of_x[t][0:1]
            xsend2[1, 3 * n + t : 3 * n + t + 1, :] = of_x[t + 1][7:8]
        low = of_x[0]
        high = lane_roll(of_x[0], 32)
        for t in range(1, 4):
            low = jnp.where(block_y == t, lane_roll(of_x[t], 32 * t), low)
            high = jnp.where(block_y == t, lane_roll(of_x[t], 32 * (t - 3)), high)
        for k, tile in enumerate((low, high)):
            ysend2[k, n] = tile
            for m, r in enumerate((0, 7)):
                csend2[2 * m + k, n : n + 1, :] = tile[r : r + 1]
        for t in range(4):
            xstress[n, t] = of_x[t]

    copies2 = exchange((xsend2, xrecv2), (ysend2, yrecv2), (csend2, crecv2), ssem2, rsem2)

    for n in range(9):
        for b in range(BYN):
            dg_out[pl.ds(4 * n + b, 8, stride=36), :] = block_tile([deform[t][n] for t in range(4)], b)
    for copy in copies2:
        copy.wait_recv()

    def corner2(low, high):
        return [
            jnp.where(lane[0:1] < 64, lane_roll(crecv2[low], -32 * t), lane_roll(crecv2[high], 32 * (3 - t)))
            for t in range(4)
        ]

    corner_low2, corner_high2 = corner2(0, 1), corner2(2, 3)
    for n in range(9):
        mine = [xstress[n, t] for t in range(4)]
        beside = []
        for t in range(4):
            beside.append(jnp.where(
                side_lane, lane_roll(yrecv2[0, n], -32 * t), lane_roll(yrecv2[1, n], 32 * (3 - t))))

        def row_at2(slot, t, n=n):
            return xrecv2[slot, 3 * n + t : 3 * n + t + 1, :]

        for s in range(-3, 7):
            inner = extend(mine, lambda t: row_at2(0, t - 1), lambda t: row_at2(1, t), row, s)
            ystress[3, n, s + 3] = inner
            if s < -2 or s > 5:
                continue
            outer = extend(
                beside, lambda t: corner_low2[t][n : n + 1], lambda t: corner_high2[t][n : n + 1], row, s)
            for k in (1, 2, 3):
                if k == 3 and not 0 <= s <= 3:
                    continue
                ystress[3 + k, n, s + 3] = jnp.where(y_at < k, outer, inner)
                ystress[3 - k, n, s + 3] = jnp.where(y_at >= 16 - k, outer, inner)

    def second_sums(c, carry):
        total = force[c]
        for dy in range(-3, 4):
            for dz in range(-3, 4):
                if (dy, dz) not in COLUMNS:
                    continue
                deep = COLUMNS[(dy, dz)]
                turn = -(8 * dy + dz)
                tiles = pl.ds(3 - deep, 4 + 2 * deep)
                fixed = None
                if dy != 0:
                    fixed = add(fixed, times(dy, ystress[dy + 3, 3 * c + 1, tiles]))
                if dz != 0:
                    fixed = add(fixed, times(dz, ystress[dy + 3, 3 * c + 2, tiles]))
                if fixed is not None:
                    fixed = lane_roll(fixed, turn)
                slope = lane_roll(ystress[dy + 3, 3 * c, tiles], turn) if deep else None
                for dx in range(-deep, deep + 1):
                    lo = deep + dx
                    value = None if fixed is None else fixed[lo : lo + 4]
                    if dx != 0:
                        value = add(value, times(dx, slope[lo : lo + 4]))
                    if value is not None:
                        total = total + weights[W_AT[(dy, dz)] + lo] * value
        force[c] = total
        return carry

    lax.fori_loop(0, 3, second_sums, 0)
    for c in range(3):
        for b in range(BYN):
            force_out[pl.ds(4 * c + b, 8, stride=12), :] = block_tile([force[c, t] for t in range(4)], b)
    for copy in copies + copies2:
        copy.wait_send()


def store(dg, force, dg_out, force_out, sem):
    copies = [
        pltpu.make_async_copy(dg, dg_out, sem.at[0]),
        pltpu.make_async_copy(force, force_out, sem.at[1]),
    ]
    for copy in copies:
        copy.start()
    for copy in copies:
        copy.wait()


def local(displacement, volume, health, damage, block_pairs):
    pairs = block_pairs[0, 0].T
    disp = jnp.transpose(displacement, (0, 2, 1, 3)).reshape(-1, LANES)
    rows = [a.reshape(-1, LANES) for a in (volume, health, damage)]
    f32 = jnp.float32
    vmem = pl.BlockSpec(memory_space=pltpu.VMEM)
    dg, force = pl.pallas_call(
        kernel,
        out_shape=(
            pltpu.VMEM((BXN * 9 * BYN, LANES), f32),
            pltpu.VMEM((BXN * 3 * BYN, LANES), f32),
        ),
        in_specs=[pl.BlockSpec(memory_space=pl.ANY)] * 5,
        out_specs=(vmem, vmem),
        scratch_shapes=[
            pltpu.VMEM(disp.shape, f32),
            pltpu.VMEM(rows[0].shape, f32),
            pltpu.VMEM(rows[1].shape, f32),
            pltpu.VMEM(rows[2].shape, jnp.int32),
            pltpu.VMEM(pairs.shape, jnp.int32),
            pltpu.VMEM((2, 6, 8, LANES), f32),
            pltpu.VMEM((2, 6, 8, LANES), f32),
            pltpu.VMEM((2, 24, LANES), f32),
            pltpu.VMEM((2, 24, LANES), f32),
            pltpu.VMEM((4, 8, LANES), f32),
            pltpu.VMEM((4, 8, LANES), f32),
            pltpu.VMEM((2, 9, 8, LANES), f32),
            pltpu.VMEM((2, 9, 8, LANES), f32),
            pltpu.VMEM((2, 32, LANES), f32),
            pltpu.VMEM((2, 32, LANES), f32),
            pltpu.VMEM((4, 16, LANES), f32),
            pltpu.VMEM((4, 16, LANES), f32),
            pltpu.VMEM((7, 5, 10, 8, LANES), f32),
            pltpu.VMEM((4, 4, 8, LANES), f32),
            pltpu.VMEM((7, 7, 4, 8, LANES), f32),
            pltpu.VMEM((W_COUNT, 4, 8, LANES), f32),
            pltpu.VMEM((18, 4, 8, LANES), f32),
            pltpu.VMEM((7, 9, 10, 8, LANES), f32),
            pltpu.VMEM((9, 4, 8, LANES), f32),
            pltpu.VMEM((3, 4, 8, LANES), f32),
            pltpu.SemaphoreType.DMA((5,)),
            pltpu.SemaphoreType.DMA((8,)),
            pltpu.SemaphoreType.DMA((8,)),
            pltpu.SemaphoreType.DMA((8,)),
            pltpu.SemaphoreType.DMA((8,)),
        ],
        compiler_params=pltpu.CompilerParams(collective_id=0, has_side_effects=True),
        name="peridynamics",
    )(disp, *rows, pairs)
    dg, force = (pltpu.with_memory_space_constraint(a, pltpu.VMEM) for a in (dg, force))
    hbm = pl.BlockSpec(memory_space=pltpu.HBM)
    dg, force = pl.pallas_call(
        store,
        out_shape=(
            jax.ShapeDtypeStruct(dg.shape, f32),
            jax.ShapeDtypeStruct(force.shape, f32),
        ),
        in_specs=[vmem] * 2,
        out_specs=(hbm, hbm),
        scratch_shapes=[pltpu.SemaphoreType.DMA((2,))],
        name="store",
    )(dg, force)
    dg, force = (a.reshape(BXN, -1, BYN, LANES) for a in (dg, force))
    return jnp.transpose(dg, (0, 2, 1, 3)), jnp.transpose(force, (0, 2, 1, 3))


def solution(mesh):
    in_specs = (
        P("gx", "gy", None, None),
        P("gx", "gy", None),
        P("gx", "gy", None),
        P("gx", "gy", None),
        P("gx", "gy", None, None),
    )
    out_specs = (P("gx", "gy", None, None), P("gx", "gy", None, None))
    return jax.shard_map(local, mesh=mesh, in_specs=in_specs, out_specs=out_specs, check_vma=False)
```

```python
import jax
import jax.numpy as jnp
from jax import lax
from jax.experimental import pallas as pl
from jax.experimental.pallas import tpu as pltpu
from jax.sharding import PartitionSpec as P

MESH = pl.DeviceIdType.MESH
LANES = 128
BXN, BYN = 8, 4
LAME, SHEAR = 24.0, 16.0
COLUMNS = {}
for _dy in range(-3, 4):
    for _dz in range(-3, 4):
        _rest = 9 - _dy * _dy - _dz * _dz
        if _rest >= 0:
            COLUMNS[(_dy, _dz)] = max(k for k in range(4) if k * k <= _rest)
W_AT, _n = {}, 0
for _key, _m in COLUMNS.items():
    W_AT[_key] = _n
    _n += 2 * _m + 1
W_COUNT = _n
CORNERS = ((-1, 1), (-1, -1), (1, 1), (1, -1))


REACH_TWO = {0: (2, 0, -2), 1: (3, 1, -2), 2: (3, 0, -1), 4: (1, 3, 2), 5: (0, 2, 2), 6: (0, 3, 1)}
REACH_THREE = {0: (1, 0, -3), 1: (2, 1, -3), 2: (3, 2, -3), 4: (2, 3, 3), 5: (1, 2, 3), 6: (0, 1, 3)}
ORDER = ["xx", "xy", "xz", "yy", "yz", "zz"] + [(a, k) for k in range(4) for a in "xyz"]
ENDS = [key for key in COLUMNS if COLUMNS[key] >= 1]


def direction(cx, cy):
    q = 3 * cx + cy
    return q - 1 if q > 0 else 3 - q


def iota(axis):
    return lax.broadcasted_iota(jnp.int32, (8, LANES), axis)


def take(tile, index):
    return jnp.take_along_axis(tile, index, axis=1, mode="promise_in_bounds")


def lane_roll(array, by):
    by = by % LANES
    return array if by == 0 else pltpu.roll(array, by, axis=array.ndim - 1)


def row_roll(tile, by):
    return pltpu.roll(tile, by % 8, axis=0)


def inverse_of(m):
    c00 = m[4] * m[8] - m[5] * m[7]
    c01 = m[5] * m[6] - m[3] * m[8]
    c02 = m[3] * m[7] - m[4] * m[6]
    c10 = m[2] * m[7] - m[1] * m[8]
    c11 = m[0] * m[8] - m[2] * m[6]
    c12 = m[1] * m[6] - m[0] * m[7]
    c20 = m[1] * m[5] - m[2] * m[4]
    c21 = m[2] * m[3] - m[0] * m[5]
    c22 = m[0] * m[4] - m[1] * m[3]
    scale = 1.0 / (m[0] * c00 + m[1] * c01 + m[2] * c02)
    return [c * scale for c in (c00, c10, c20, c01, c11, c21, c02, c12, c22)]


def product(a, b):
    return [
        a[3 * r] * b[c] + a[3 * r + 1] * b[3 + c] + a[3 * r + 2] * b[6 + c]
        for r in range(3)
        for c in range(3)
    ]


def times(k, value):
    return value if k == 1 else (-value if k == -1 else float(k) * value)


def add(total, value):
    return value if total is None else total + value


def extend(own, row, s):
    if s < 0:
        return jnp.where(row == 0, 0.0, row_roll(own[s + 4], 1))
    if s > 3:
        return jnp.where(row == 7, 0.0, row_roll(own[s - 4], -1))
    return own[s]


def place(row, table, tile_of):
    got = jnp.zeros((8, LANES), jnp.float32)
    for r, (tile, _, _) in table.items():
        got = jnp.where(row == r, tile_of(r < 4, tile), got)
    return got


def ends_of(row, packed, three):
    gone = jnp.where(row % 4 == 2, 0.0, packed)
    return gone + jnp.where(row % 4 == 0, row_roll(packed, -2), 0.0) + three


def with_ends(tile, ends, row, t):
    if t <= 2:
        tile = tile + jnp.where(row == 0, ends[t : t + 1], 0.0)
    if t >= 1:
        tile = tile + jnp.where(row == 7, ends[7 - t : 8 - t], 0.0)
    return tile


def kernel(
    disp_in, vol_in, hea_in, dam_in, pairs_in, dg_out, force_out,
    disp, vol, hea, dam, pairs,
    ysend, yrecv, xsend, xrecv, csend, crecv,
    ysend2, yrecv2, xsend2, xrecv2, csend2, crecv2,
    fields, own_u, health_m, weights, sums, ystress, xstress, force, end_weights,
    isem, ssem, rsem, ssem2, rsem2,
):
    loads = [
        pltpu.make_async_copy(src, dst, isem.at[n])
        for n, (src, dst) in enumerate((
            (pairs_in, pairs), (disp_in, disp), (vol_in, vol), (hea_in, hea), (dam_in, dam)))
    ]
    for load in loads:
        load.start()
    n_gx, n_gy = lax.axis_size("gx"), lax.axis_size("gy")
    me_x, me_y = lax.axis_index("gx"), lax.axis_index("gy")

    def device(cx, cy):
        return (lax.rem(me_x + (cx + n_gx), n_gx), lax.rem(me_y + (cy + n_gy), n_gy))

    barrier = pltpu.get_barrier_semaphore()
    for cx in (-1, 0, 1):
        for cy in (-1, 0, 1):
            if cx or cy:
                pl.semaphore_signal(barrier, inc=1, device_id=device(cx, cy), device_id_type=MESH)

    row, lane = iota(0), iota(1)
    block_y, y_in, z_at = lane // 32, (lane // 8) % 4, lane % 8
    y_at = lane // 8

    for load in loads:
        load.wait()
    slots = pairs.shape[1]
    ax, ay, bx, by = (pairs[i : i + 1, :] for i in range(4))
    q = 3 * (bx - ax) + (by - ay) - 1
    wide = lax.broadcasted_iota(jnp.int32, (LANES, slots), 0)
    tall = lax.broadcasted_iota(jnp.int32, (8, slots), 0)
    flags = None
    for at_x, at_y, way in ((ax, ay, q), (bx, by, q + 4)):
        in_row = jnp.where(tall == at_x - 1, 1.0, 0.0)
        in_lane = jnp.where(wide == 8 * at_y + way, 1.0, 0.0)
        flags = add(flags, lax.dot_general(
            in_row, in_lane, (((1,), (1,)), ((), ())), preferred_element_type=jnp.float32))

    def u_tile(c, b):
        return disp[pl.ds(4 * c + b, 8, stride=12), :]

    def row_tile(array, b):
        return array[pl.ds(b, 8, stride=4), :]

    raw = []
    for b in range(BYN):
        v = row_tile(vol, b)
        raw.append([row_tile(hea, b), v] + [v * u_tile(c, b) for c in range(3)])
    for n, b in enumerate((0, 3)):
        for f in range(5):
            ysend[n, f] = raw[b][f]
            for m, r in enumerate((0, 7)):
                csend[2 * m + n, f : f + 1, :] = raw[b][f][r : r + 1]
        ysend[n, 5] = flags
        for m, r in enumerate((0, 7)):
            csend[2 * m + n, 5:6, :] = flags[r : r + 1]
    for m, r in enumerate((0, 7)):
        xsend[m, 0:12, :] = disp[12 * r : 12 * r + 12, :]
        xsend[m, 12:16, :] = vol[4 * r : 4 * r + 4, :]
        xsend[m, 16:20, :] = hea[4 * r : 4 * r + 4, :]
        xsend[m, 20:21, :] = flags[r : r + 1]
    pl.semaphore_wait(barrier, 8)

    def exchange(x_pair, y_pair, c_pair, sends, recvs):
        moves = []
        for n, cx in enumerate((-1, 1)):
            moves.append((x_pair[0].at[1 - n], x_pair[1].at[n], -cx, 0))
        for n, cy in enumerate((1, -1)):
            moves.append((y_pair[0].at[n], y_pair[1].at[n], 0, -cy))
        for n, (cx, cy) in enumerate(CORNERS):
            at = 2 * (0 if cx == 1 else 1) + (0 if cy == 1 else 1)
            moves.append((c_pair[0].at[at], c_pair[1].at[n], -cx, -cy))
        copies = [
            pltpu.make_async_remote_copy(
                src_ref=src, dst_ref=dst, send_sem=sends.at[n], recv_sem=recvs.at[n],
                device_id=device(tx, ty), device_id_type=MESH)
            for n, (src, dst, tx, ty) in enumerate(moves)
        ]
        for copy in copies:
            copy.start()
        return copies

    copies = exchange((xsend, xrecv), (ysend, yrecv), (csend, crecv), ssem, rsem)

    to_x = [16 * z_at + 4 * y_in + t for t in range(4)]

    def lattice_tile(of_block, t):
        got = take(of_block[0], to_x[t])
        for b in range(1, BYN):
            got = jnp.where(block_y == b, take(of_block[b], to_x[t]), got)
        return got

    own = [[lattice_tile([raw[b][f] for b in range(BYN)], t) for t in range(4)] for f in range(5)]
    dam_raw = [row_tile(dam, b).astype(jnp.float32) for b in range(BYN)]
    for t in range(4):
        for c in range(3):
            own_u[c, t] = lattice_tile([u_tile(c, b) for b in range(BYN)], t)
        own_u[3, t] = 1.0 - lattice_tile(dam_raw, t)
    for copy in copies[2:4]:
        copy.wait_recv()

    def flag_ext(tile, cx):
        if cx == 0:
            return tile
        return jnp.where(row == (0 if cx < 0 else 7), 0.0, row_roll(tile, -cx))

    seen = {}
    for cy, tile in ((0, flags), (1, yrecv[0, 5]), (-1, yrecv[1, 5])):
        for cx in (-1, 0, 1):
            seen[(cx, cy)] = flag_ext(tile, cx)
    enabled = {}
    for cx in (-1, 0, 1):
        for cy in (-1, 0, 1):
            if cx == 0 and cy == 0:
                continue
            mine = take(flags, 8 * (block_y + 1) + direction(cx, cy))
            back = direction(-cx, -cy)
            theirs = take(seen[(cx, 0)], 8 * (block_y + cy + 1) + back)
            if cy == 1:
                theirs = jnp.where(block_y == 3, take(seen[(cx, 1)], 8 + back + 0 * lane), theirs)
            if cy == -1:
                theirs = jnp.where(block_y == 0, take(seen[(cx, -1)], 32 + back + 0 * lane), theirs)
            enabled[(cx, cy)] = jnp.minimum(jnp.maximum(mine, theirs), 1.0)

    for dy in range(-3, 4):
        deep = max(m for (a, _), m in COLUMNS.items() if a == dy)
        by_cx = {}
        for cx in (-1, 0, 1):
            near = enabled.get((cx, 0))
            if dy > 0:
                far = enabled[(cx, 1)]
                near = 1.0 if near is None else near
                by_cx[cx] = jnp.where(y_in + dy >= 4, far, near)
            elif dy < 0:
                far = enabled[(cx, -1)]
                near = 1.0 if near is None else near
                by_cx[cx] = jnp.where(y_in + dy < 0, far, near)
            else:
                by_cx[cx] = near
        for dx in range(-deep, deep + 1):
            for t in range(4):
                cx = (t + dx) // 4
                h = own[0][t]
                health_m[dy + 3, dx + 3, t] = h if by_cx[cx] is None else h * by_cx[cx]

    side_lane = lane < 64
    for f in range(5):
        beside = []
        for t in range(4):
            beside.append(jnp.where(side_lane, take(yrecv[0, f], to_x[t]), take(yrecv[1, f], to_x[t])))
        for s in range(-3, 7):
            inner = extend(own[f], row, s)
            fields[3, f, s + 3] = inner
            if s < -2 or s > 5:
                continue
            outer = extend(beside, row, s)
            for k in (1, 2, 3):
                if k == 3 and not 0 <= s <= 3:
                    continue
                fields[3 + k, f, s + 3] = jnp.where(y_at < k, outer, inner)
                fields[3 - k, f, s + 3] = jnp.where(y_at >= 16 - k, outer, inner)

    z_ok = {dz: (z_at + dz >= 0) & (z_at + dz < 8) for dz in range(-3, 4)}

    def first_sums(half, carry):
        base = 2 * half
        total = {}
        for dy in range(-3, 4):
            part = {}
            for dz in range(-3, 4):
                if (dy, dz) not in COLUMNS:
                    continue
                deep = COLUMNS[(dy, dz)]
                turn = -(8 * dy + dz)
                src = [
                    lane_roll(fields[dy + 3, f, pl.ds(base + 3 - deep, 2 + 2 * deep)], turn)
                    for f in range(5)
                ]
                if dz != 0:
                    src[0] = jnp.where(z_ok[dz][None], src[0], 0.0)
                a0, a1, a2 = [None] * 4, [None] * 4, None
                for reach in range(deep + 1):
                    terms = []
                    for dx in (reach, -reach) if reach else (0,):
                        lo = deep + dx
                        w = jnp.minimum(
                            health_m[dy + 3, dx + 3, pl.ds(base, 2)], src[0][lo : lo + 2])
                        weights[W_AT[(dy, dz)] + lo, pl.ds(base, 2)] = w
                        if dy == 0 and dz == 0 and dx == 0:
                            continue
                        terms.append([w * src[k + 1][lo : lo + 2] for k in range(4)])
                    if not terms:
                        continue
                    for k in range(4):
                        both = terms[0][k] if reach == 0 else terms[0][k] + terms[1][k]
                        a0[k] = add(a0[k], both)
                        if reach:
                            a1[k] = add(a1[k], times(reach, terms[0][k] - terms[1][k]))
                            if k == 0:
                                a2 = add(a2, times(reach * reach, both))
                for k in range(4):
                    if dy != 0:
                        part["y", k] = add(part.get(("y", k)), a0[k])
                    if dz != 0:
                        part["z", k] = add(part.get(("z", k)), times(dz, a0[k]))
                    if a1[k] is not None:
                        part["x", k] = add(part.get(("x", k)), a1[k])
                if dz != 0:
                    part["zz"] = add(part.get("zz"), times(dz * dz, a0[0]))
                    if a1[0] is not None:
                        part["xz"] = add(part.get("xz"), times(dz, a1[0]))
                if a2 is not None:
                    part["xx"] = add(part.get("xx"), a2)
            for k in range(4):
                if dy != 0:
                    total["y", k] = add(total.get(("y", k)), times(dy, part["y", k]))
                for name in ("x", "z"):
                    if (name, k) in part:
                        total[name, k] = add(total.get((name, k)), part[name, k])
            if dy != 0:
                total["yy"] = add(total.get("yy"), times(dy * dy, part["y", 0]))
                for name, to in (("x", "xy"), ("z", "yz")):
                    if (name, 0) in part:
                        total[to] = add(total.get(to), times(dy, part[name, 0]))
            for name in ("xx", "zz", "xz"):
                if name in part:
                    total[name] = add(total.get(name), part[name])
        for n, name in enumerate(ORDER):
            sums[n, pl.ds(base, 2)] = total[name]
        return carry

    lax.fori_loop(0, 2, first_sums, 0)

    for copy in copies[:2] + copies[4:]:
        copy.wait_recv()
    edge = [
        jnp.concatenate([xrecv[0, 4 * k : 4 * k + 4, :], xrecv[1, 4 * k : 4 * k + 4, :]], axis=0)
        for k in (4, 3, 0, 1, 2)
    ]
    edge = edge[:2] + [edge[1] * e for e in edge[2:]]

    def edge_tile(f, t):
        got = jnp.where(row % 4 == block_y, take(edge[f], to_x[t]), 0.0)
        got = got + jnp.where(row % 2 == 0, row_roll(got, -1), row_roll(got, 1))
        return got + jnp.where(row % 4 < 2, row_roll(got, -2), row_roll(got, 2))

    corner_low = [
        jnp.where(side_lane, take(crecv[0], to_x[t]), take(crecv[1], to_x[t])) for t in range(4)]
    corner_high = [
        jnp.where(side_lane, take(crecv[2], to_x[t]), take(crecv[3], to_x[t])) for t in range(4)]

    low_end = row < 4

    def end_rows(low, high):
        return jnp.where(low_end, low, high)

    end_flags = end_rows(flags[0:1], flags[7:8])
    end_seen = {
        0: end_rows(xrecv[0, 20:21, :], xrecv[1, 20:21, :]),
        1: end_rows(crecv[0, 5:6, :], crecv[2, 5:6, :]),
        -1: end_rows(crecv[1, 5:6, :], crecv[3, 5:6, :]),
    }
    end_enabled = {}
    for cy in (-1, 0, 1):
        forth = jnp.where(low_end, direction(-1, cy), direction(1, cy))
        back = jnp.where(low_end, direction(1, -cy), direction(-1, -cy))
        theirs = take(end_seen[0], 8 * (block_y + cy + 1) + back)
        if cy == 1:
            theirs = jnp.where(block_y == 3, take(end_seen[1], 8 + back), theirs)
        if cy == -1:
            theirs = jnp.where(block_y == 0, take(end_seen[-1], 32 + back), theirs)
        mine = take(end_flags, 8 * (block_y + 1) + forth)
        end_enabled[cy] = jnp.minimum(jnp.maximum(mine, theirs), 1.0)

    def end_health(table):
        got = jnp.zeros((8, LANES), jnp.float32)
        for r, (_, t, _) in table.items():
            got = jnp.where(row == r, own[0][t][0:1] if r < 4 else own[0][t][7:8], got)
        return got

    def steps(table):
        got = jnp.zeros((8, LANES), jnp.float32)
        for r, (_, _, dx) in table.items():
            got = jnp.where(row == r, float(dx), got)
        return got

    step_two, step_three = steps(REACH_TWO), steps(REACH_THREE)
    health_two = end_health(REACH_TWO)
    end_fields = {0: [], 1: [], 3: []}
    for f in range(5):
        rim = [edge_tile(f, t) for t in range(4)]
        end_fields[0].append(place(row, REACH_TWO, lambda low, t: rim[t]))
        end_fields[1].append(place(
            row, REACH_TWO, lambda low, t: (corner_low if low else corner_high)[t][f : f + 1]))
        end_fields[3].append(place(row, REACH_THREE, lambda low, t: rim[t]))

    end_total = {}
    for dy in range(-2, 3):
        held = health_two
        if dy > 0:
            held = health_two * jnp.where(y_in + dy >= 4, end_enabled[1], end_enabled[0])
        elif dy < 0:
            held = health_two * jnp.where(y_in + dy < 0, end_enabled[-1], end_enabled[0])
        else:
            held = health_two * end_enabled[0]
        src_y = []
        for f in range(5):
            inner, outer = end_fields[0][f], end_fields[1][f]
            if dy > 0:
                inner = jnp.where(y_at < dy, outer, inner)
            elif dy < 0:
                inner = jnp.where(y_at >= 16 + dy, outer, inner)
            src_y.append(inner)
        part = {}
        for dz in range(-3, 4):
            if COLUMNS.get((dy, dz), 0) < 1:
                continue
            src = [lane_roll(e, -(8 * dy + dz)) for e in src_y]
            h = src[0]
            if dz != 0:
                h = jnp.where(z_ok[dz], h, 0.0)
            if COLUMNS[(dy, dz)] == 1:
                h = jnp.where(row % 4 == 2, h, 0.0)
            w = jnp.minimum(held, h)
            end_weights[ENDS.index((dy, dz))] = w
            for k in range(4):
                value = w * src[k + 1]
                part["s", k] = add(part.get(("s", k)), value)
                if dz != 0:
                    part["z", k] = add(part.get(("z", k)), times(dz, value))
                    if k == 0:
                        part["zz"] = add(part.get("zz"), times(dz * dz, value))
        for name in part:
            end_total[name] = add(end_total.get(name), part[name])
        if dy != 0:
            for k in range(4):
                end_total["y", k] = add(end_total.get(("y", k)), times(dy, part["s", k]))
            end_total["yy"] = add(end_total.get("yy"), times(dy * dy, part["s", 0]))
            end_total["yz"] = add(end_total.get("yz"), times(dy, part["z", 0]))
    for k in range(4):
        end_total["x", k] = step_two * end_total["s", k]
    end_total["xx"] = step_two * end_total["x", 0]
    end_total["xy"] = step_two * end_total["y", 0]
    end_total["xz"] = step_two * end_total["z", 0]
    w = jnp.minimum(end_health(REACH_THREE) * end_enabled[0], end_fields[3][0])
    end_weights[len(ENDS)] = w
    three = {("x", k): step_three * (w * end_fields[3][k + 1]) for k in range(4)}
    three["xx"] = step_three * three["x", 0]
    end_sums = [ends_of(row, end_total[name], three.get(name, 0.0)) for name in ORDER]

    to_raw = [8 * (4 * b + (lane // 4) % 4) + lane // 16 for b in range(BYN)]
    x_in = lane % 4

    def block_tile(of_x, b):
        got = take(of_x[0], to_raw[b])
        for t in range(1, 4):
            got = jnp.where(x_in == t, take(of_x[t], to_raw[b]), got)
        return got

    deform, stress = [], []
    for t in range(4):
        full = [with_ends(sums[n, t], end_sums[n], row, t) for n in range(18)]
        kxx, kxy, kxz, kyy, kyz, kzz = full[:6]
        span = full[6:9]
        sym = [kxx, kxy, kxz, kxy, kyy, kyz, kxz, kyz, kzz]
        moment = [
            sym[3 * c + d] + full[9 + 3 * c + d] - own_u[c, t] * span[d]
            for c in range(3) for d in range(3)
        ]
        shape = [sym[n] + 1.0 if n % 4 == 0 else sym[n] for n in range(9)]
        inv = inverse_of(shape)
        grad = product(moment, inv)
        flip = [grad[3 * (n % 3) + n // 3] for n in range(9)]
        twice = product(flip, grad)
        strain = [0.5 * (twice[n] - 1.0) if n % 4 == 0 else 0.5 * twice[n] for n in range(9)]
        trace = LAME * (strain[0] + strain[4] + strain[8])
        second = [
            trace + 2.0 * SHEAR * strain[n] if n % 4 == 0 else 2.0 * SHEAR * strain[n]
            for n in range(9)
        ]
        first = [e * own_u[3, t] for e in product(grad, second)]
        mapped = product(first, inv)
        for c in range(3):
            force[c, t] = mapped[3 * c] * span[0] + mapped[3 * c + 1] * span[1] + mapped[3 * c + 2] * span[2]
        v = own[1][t]
        deform.append(grad)
        stress.append([v * e for e in mapped])

    for n in range(9):
        of_x = [stress[t][n] for t in range(4)]
        for t in range(3):
            xsend2[0, 3 * n + t : 3 * n + t + 1, :] = of_x[t][0:1]
            xsend2[1, 3 * n + t : 3 * n + t + 1, :] = of_x[t + 1][7:8]
        low = of_x[0]
        high = lane_roll(of_x[0], 32)
        for t in range(1, 4):
            low = jnp.where(block_y == t, lane_roll(of_x[t], 32 * t), low)
            high = jnp.where(block_y == t, lane_roll(of_x[t], 32 * (t - 3)), high)
        for k, tile in enumerate((low, high)):
            ysend2[k, n] = tile
            for m, r in enumerate((0, 7)):
                csend2[2 * m + k, n : n + 1, :] = tile[r : r + 1]
        for t in range(4):
            xstress[n, t] = of_x[t]

    copies2 = exchange((xsend2, xrecv2), (ysend2, yrecv2), (csend2, crecv2), ssem2, rsem2)

    for n in range(9):
        for b in range(BYN):
            dg_out[pl.ds(4 * n + b, 8, stride=36), :] = block_tile([deform[t][n] for t in range(4)], b)
    for copy in copies2[2:4]:
        copy.wait_recv()

    for n in range(9):
        mine = [xstress[n, t] for t in range(4)]
        beside = []
        for t in range(4):
            beside.append(jnp.where(
                side_lane, lane_roll(yrecv2[0, n], -32 * t), lane_roll(yrecv2[1, n], 32 * (3 - t))))

        for s in range(-3, 7):
            inner = extend(mine, row, s)
            ystress[3, n, s + 3] = inner
            if s < -2 or s > 5:
                continue
            outer = extend(beside, row, s)
            for k in (1, 2, 3):
                if k == 3 and not 0 <= s <= 3:
                    continue
                ystress[3 + k, n, s + 3] = jnp.where(y_at < k, outer, inner)
                ystress[3 - k, n, s + 3] = jnp.where(y_at >= 16 - k, outer, inner)

    def second_sums(c, carry):
        total = force[c]
        for dy in range(-3, 4):
            for dz in range(-3, 4):
                if (dy, dz) not in COLUMNS:
                    continue
                deep = COLUMNS[(dy, dz)]
                turn = -(8 * dy + dz)
                tiles = pl.ds(3 - deep, 4 + 2 * deep)
                fixed = None
                if dy != 0:
                    fixed = add(fixed, times(dy, ystress[dy + 3, 3 * c + 1, tiles]))
                if dz != 0:
                    fixed = add(fixed, times(dz, ystress[dy + 3, 3 * c + 2, tiles]))
                if fixed is not None:
                    fixed = lane_roll(fixed, turn)
                slope = lane_roll(ystress[dy + 3, 3 * c, tiles], turn) if deep else None
                for dx in range(-deep, deep + 1):
                    lo = deep + dx
                    value = None if fixed is None else fixed[lo : lo + 4]
                    if dx != 0:
                        value = add(value, times(dx, slope[lo : lo + 4]))
                    if value is not None:
                        total = total + weights[W_AT[(dy, dz)] + lo] * value
        force[c] = total
        return carry

    lax.fori_loop(0, 3, second_sums, 0)

    for copy in copies2[:2] + copies2[4:]:
        copy.wait_recv()

    def corner2(low, high):
        return [
            jnp.where(lane[0:1] < 64, lane_roll(crecv2[low], -32 * t), lane_roll(crecv2[high], 32 * (3 - t)))
            for t in range(4)
        ]

    corner_low2, corner_high2 = corner2(0, 1), corner2(2, 3)

    def halo_row(n, low, t):
        return xrecv2[0, 3 * n + t - 1 : 3 * n + t, :] if low else xrecv2[1, 3 * n + t : 3 * n + t + 1, :]

    end_inner, end_outer, end_force = [], [], []
    for n in range(9):
        scale = step_two if n % 3 == 0 else 1.0
        end_inner.append(scale * place(row, REACH_TWO, lambda low, t: halo_row(n, low, t)))
        end_outer.append(scale * place(
            row, REACH_TWO, lambda low, t: (corner_low2 if low else corner_high2)[t][n : n + 1]))
    for c in range(3):
        total = None
        for dy in range(-2, 3):
            src_y = []
            for d in range(3):
                inner, outer = end_inner[3 * c + d], end_outer[3 * c + d]
                if dy > 0:
                    inner = jnp.where(y_at < dy, outer, inner)
                elif dy < 0:
                    inner = jnp.where(y_at >= 16 + dy, outer, inner)
                src_y.append(inner)
            fixed = src_y[0] if dy == 0 else src_y[0] + times(dy, src_y[1])
            for dz in range(-3, 4):
                if COLUMNS.get((dy, dz), 0) < 1:
                    continue
                value = fixed if dz == 0 else fixed + times(dz, src_y[2])
                value = lane_roll(value, -(8 * dy + dz))
                total = add(total, end_weights[ENDS.index((dy, dz))] * value)
        three = step_three * place(row, REACH_THREE, lambda low, t: halo_row(3 * c, low, t))
        end_force.append(ends_of(row, total, end_weights[len(ENDS)] * three))
    for c in range(3):
        full_force = [with_ends(force[c, t], end_force[c], row, t) for t in range(4)]
        for b in range(BYN):
            force_out[pl.ds(4 * c + b, 8, stride=12), :] = block_tile(full_force, b)
    for copy in copies + copies2:
        copy.wait_send()


def store(dg, force, dg_out, force_out, sem):
    copies = [
        pltpu.make_async_copy(dg, dg_out, sem.at[0]),
        pltpu.make_async_copy(force, force_out, sem.at[1]),
    ]
    for copy in copies:
        copy.start()
    for copy in copies:
        copy.wait()


def local(displacement, volume, health, damage, block_pairs):
    pairs = block_pairs[0, 0].T
    disp = jnp.transpose(displacement, (0, 2, 1, 3)).reshape(-1, LANES)
    rows = [a.reshape(-1, LANES) for a in (volume, health, damage)]
    f32 = jnp.float32
    vmem = pl.BlockSpec(memory_space=pltpu.VMEM)
    dg, force = pl.pallas_call(
        kernel,
        out_shape=(
            pltpu.VMEM((BXN * 9 * BYN, LANES), f32),
            pltpu.VMEM((BXN * 3 * BYN, LANES), f32),
        ),
        in_specs=[pl.BlockSpec(memory_space=pl.ANY)] * 5,
        out_specs=(vmem, vmem),
        scratch_shapes=[
            pltpu.VMEM(disp.shape, f32),
            pltpu.VMEM(rows[0].shape, f32),
            pltpu.VMEM(rows[1].shape, f32),
            pltpu.VMEM(rows[2].shape, jnp.int32),
            pltpu.VMEM(pairs.shape, jnp.int32),
            pltpu.VMEM((2, 6, 8, LANES), f32),
            pltpu.VMEM((2, 6, 8, LANES), f32),
            pltpu.VMEM((2, 24, LANES), f32),
            pltpu.VMEM((2, 24, LANES), f32),
            pltpu.VMEM((4, 8, LANES), f32),
            pltpu.VMEM((4, 8, LANES), f32),
            pltpu.VMEM((2, 9, 8, LANES), f32),
            pltpu.VMEM((2, 9, 8, LANES), f32),
            pltpu.VMEM((2, 32, LANES), f32),
            pltpu.VMEM((2, 32, LANES), f32),
            pltpu.VMEM((4, 16, LANES), f32),
            pltpu.VMEM((4, 16, LANES), f32),
            pltpu.VMEM((7, 5, 10, 8, LANES), f32),
            pltpu.VMEM((4, 4, 8, LANES), f32),
            pltpu.VMEM((7, 7, 4, 8, LANES), f32),
            pltpu.VMEM((W_COUNT, 4, 8, LANES), f32),
            pltpu.VMEM((18, 4, 8, LANES), f32),
            pltpu.VMEM((7, 9, 10, 8, LANES), f32),
            pltpu.VMEM((9, 4, 8, LANES), f32),
            pltpu.VMEM((3, 4, 8, LANES), f32),
            pltpu.VMEM((len(ENDS) + 1, 8, LANES), f32),
            pltpu.SemaphoreType.DMA((5,)),
            pltpu.SemaphoreType.DMA((8,)),
            pltpu.SemaphoreType.DMA((8,)),
            pltpu.SemaphoreType.DMA((8,)),
            pltpu.SemaphoreType.DMA((8,)),
        ],
        compiler_params=pltpu.CompilerParams(collective_id=0, has_side_effects=True),
        name="peridynamics",
    )(disp, *rows, pairs)
    dg, force = (pltpu.with_memory_space_constraint(a, pltpu.VMEM) for a in (dg, force))
    hbm = pl.BlockSpec(memory_space=pltpu.HBM)
    dg, force = pl.pallas_call(
        store,
        out_shape=(
            jax.ShapeDtypeStruct(dg.shape, f32),
            jax.ShapeDtypeStruct(force.shape, f32),
        ),
        in_specs=[vmem] * 2,
        out_specs=(hbm, hbm),
        scratch_shapes=[pltpu.SemaphoreType.DMA((2,))],
        name="store",
    )(dg, force)
    dg, force = (a.reshape(BXN, -1, BYN, LANES) for a in (dg, force))
    return jnp.transpose(dg, (0, 2, 1, 3)), jnp.transpose(force, (0, 2, 1, 3))


def solution(mesh):
    in_specs = (
        P("gx", "gy", None, None),
        P("gx", "gy", None),
        P("gx", "gy", None),
        P("gx", "gy", None),
        P("gx", "gy", None, None),
    )
    out_specs = (P("gx", "gy", None, None), P("gx", "gy", None, None))
    return jax.shard_map(local, mesh=mesh, in_specs=in_specs, out_specs=out_specs, check_vma=False)
```

```python
import jax
import jax.numpy as jnp
from jax import lax
from jax.experimental import pallas as pl
from jax.experimental.pallas import tpu as pltpu
from jax.sharding import PartitionSpec as P

MESH = pl.DeviceIdType.MESH
LANES = 128
BXN, BYN = 8, 4
LAME, SHEAR = 24.0, 16.0
COLUMNS = {}
for _dy in range(-3, 4):
    for _dz in range(-3, 4):
        _rest = 9 - _dy * _dy - _dz * _dz
        if _rest >= 0:
            COLUMNS[(_dy, _dz)] = max(k for k in range(4) if k * k <= _rest)
W_AT, _n = {}, 0
for _key, _m in COLUMNS.items():
    W_AT[_key] = _n
    _n += 2 * _m + 1
W_COUNT = _n
CORNERS = ((-1, 1), (-1, -1), (1, 1), (1, -1))


REACH_TWO = {0: (2, 0, -2), 1: (3, 1, -2), 2: (3, 0, -1), 4: (1, 3, 2), 5: (0, 2, 2), 6: (0, 3, 1)}
REACH_THREE = {0: (1, 0, -3), 1: (2, 1, -3), 2: (3, 2, -3), 4: (2, 3, 3), 5: (1, 2, 3), 6: (0, 1, 3)}
ORDER = ["xx", "xy", "xz", "yy", "yz", "zz"] + [(a, k) for k in range(4) for a in "xyz"]
OTHERS = (-3, -2, -1, 1, 2, 3)
FIRST = 0
ENDS = [key for key in COLUMNS if COLUMNS[key] >= 1]


def direction(cx, cy):
    q = 3 * cx + cy
    return q - 1 if q > 0 else 3 - q


def iota(axis):
    return lax.broadcasted_iota(jnp.int32, (8, LANES), axis)


def take(tile, index):
    return jnp.take_along_axis(tile, index, axis=1, mode="promise_in_bounds")


def lane_roll(array, by):
    by = by % LANES
    return array if by == 0 else pltpu.roll(array, by, axis=array.ndim - 1)


def row_roll(tile, by):
    return pltpu.roll(tile, by % 8, axis=0)


def inverse_of(m):
    c00 = m[4] * m[8] - m[5] * m[7]
    c01 = m[5] * m[6] - m[3] * m[8]
    c02 = m[3] * m[7] - m[4] * m[6]
    c10 = m[2] * m[7] - m[1] * m[8]
    c11 = m[0] * m[8] - m[2] * m[6]
    c12 = m[1] * m[6] - m[0] * m[7]
    c20 = m[1] * m[5] - m[2] * m[4]
    c21 = m[2] * m[3] - m[0] * m[5]
    c22 = m[0] * m[4] - m[1] * m[3]
    scale = 1.0 / (m[0] * c00 + m[1] * c01 + m[2] * c02)
    return [c * scale for c in (c00, c10, c20, c01, c11, c21, c02, c12, c22)]


def product(a, b):
    return [
        a[3 * r] * b[c] + a[3 * r + 1] * b[3 + c] + a[3 * r + 2] * b[6 + c]
        for r in range(3)
        for c in range(3)
    ]


def times(k, value):
    return value if k == 1 else (-value if k == -1 else float(k) * value)


def add(total, value):
    return value if total is None else total + value


def spread(own, deep, clear=None):
    if deep == 0:
        return own
    low = pltpu.roll(own[4 - deep :], 1, axis=1)
    high = pltpu.roll(own[:deep], 7, axis=1)
    if clear is not None:
        low = jnp.where(clear == 0, 0.0, low)
        high = jnp.where(clear == 7, 0.0, high)
    return jnp.concatenate([low, own, high], axis=0)


def place(row, table, tile_of):
    got = jnp.zeros((8, LANES), jnp.float32)
    for r, (tile, _, _) in table.items():
        got = jnp.where(row == r, tile_of(r < 4, tile), got)
    return got


def ends_of(row, packed, three):
    gone = jnp.where(row % 4 == 2, 0.0, packed)
    return gone + jnp.where(row % 4 == 0, row_roll(packed, -2), 0.0) + three


def with_ends(tile, ends, row, t):
    if t <= 2:
        tile = tile + jnp.where(row == 0, ends[t : t + 1], 0.0)
    if t >= 1:
        tile = tile + jnp.where(row == 7, ends[7 - t : 8 - t], 0.0)
    return tile


def kernel(
    disp_in, vol_in, hea_in, dam_in, pairs_in, dg_out, force_out,
    disp, vol, hea, dam, pairs,
    ysend, yrecv, xsend, xrecv, csend, crecv,
    ysend2, yrecv2, xsend2, xrecv2, csend2, crecv2,
    fields, own_u, health_m, weights, sums, ystress, force, end_weights,
    isem, ssem, rsem, ssem2, rsem2,
):
    loads = [
        pltpu.make_async_copy(src, dst, isem.at[n])
        for n, (src, dst) in enumerate((
            (pairs_in, pairs), (disp_in, disp), (vol_in, vol), (hea_in, hea), (dam_in, dam)))
    ]
    for load in loads:
        load.start()
    n_gx, n_gy = lax.axis_size("gx"), lax.axis_size("gy")
    me_x, me_y = lax.axis_index("gx"), lax.axis_index("gy")

    def device(cx, cy):
        return (me_x + cx, me_y + cy)

    inside = {-1: (me_x > 0, me_y > 0), 1: (me_x < n_gx - 1, me_y < n_gy - 1)}

    def present(cx, cy):
        if cx and cy:
            return jnp.logical_and(inside[cx][0], inside[cy][1])
        return inside[cx][0] if cx else inside[cy][1]

    barrier = pltpu.get_barrier_semaphore()
    for cx in (-1, 0, 1):
        for cy in (-1, 0, 1):
            if cx or cy:

                @pl.when(present(cx, cy))
                def _():
                    pl.semaphore_signal(
                        barrier, inc=1, device_id=device(cx, cy), device_id_type=MESH)

    spans = [
        1 + inside[-1][axis].astype(jnp.int32) + inside[1][axis].astype(jnp.int32) for axis in (0, 1)]
    for n, cx in enumerate((-1, 1)):

        @pl.when(jnp.logical_not(present(cx, 0)))
        def _():
            xrecv[n] = jnp.zeros(xrecv.shape[1:], jnp.float32)
            xrecv2[n] = jnp.zeros(xrecv2.shape[1:], jnp.float32)

    for n, cy in enumerate((1, -1)):

        @pl.when(jnp.logical_not(present(0, cy)))
        def _():
            yrecv[n] = jnp.zeros(yrecv.shape[1:], jnp.float32)
            yrecv2[n] = jnp.zeros(yrecv2.shape[1:], jnp.float32)

    for n, (cx, cy) in enumerate(CORNERS):

        @pl.when(jnp.logical_not(present(cx, cy)))
        def _():
            crecv[n] = jnp.zeros(crecv.shape[1:], jnp.float32)
            crecv2[n] = jnp.zeros(crecv2.shape[1:], jnp.float32)

    row, lane = iota(0), iota(1)
    block_y, y_in, z_at = lane // 32, (lane // 8) % 4, lane % 8
    y_at = lane // 8

    for load in loads:
        load.wait()
    slots = pairs.shape[1]
    ax, ay, bx, by = (pairs[i : i + 1, :] for i in range(4))
    q = 3 * (bx - ax) + (by - ay) - 1
    wide = lax.broadcasted_iota(jnp.int32, (LANES, slots), 0)
    tall = lax.broadcasted_iota(jnp.int32, (8, slots), 0)
    flags = None
    for at_x, at_y, way in ((ax, ay, q), (bx, by, q + 4)):
        in_row = jnp.where(tall == at_x - 1, 1.0, 0.0)
        in_lane = jnp.where(wide == 8 * at_y + way, 1.0, 0.0)
        flags = add(flags, lax.dot_general(
            in_row, in_lane, (((1,), (1,)), ((), ())), preferred_element_type=jnp.float32))

    def u_tile(c, b):
        return disp[pl.ds(4 * c + b, 8, stride=12), :]

    def row_tile(array, b):
        return array[pl.ds(b, 8, stride=4), :]

    raw = []
    for b in range(BYN):
        v = row_tile(vol, b)
        raw.append([row_tile(hea, b), v] + [v * u_tile(c, b) for c in range(3)])
    for n, b in enumerate((0, 3)):
        for f in range(5):
            ysend[n, f] = raw[b][f]
            for m, r in enumerate((0, 7)):
                csend[2 * m + n, f : f + 1, :] = raw[b][f][r : r + 1]
        ysend[n, 5] = flags
        for m, r in enumerate((0, 7)):
            csend[2 * m + n, 5:6, :] = flags[r : r + 1]
    for m, r in enumerate((0, 7)):
        xsend[m, 0:12, :] = disp[12 * r : 12 * r + 12, :]
        xsend[m, 12:16, :] = vol[4 * r : 4 * r + 4, :]
        xsend[m, 16:20, :] = hea[4 * r : 4 * r + 4, :]
        xsend[m, 20:21, :] = flags[r : r + 1]
    pl.semaphore_wait(barrier, spans[0] * spans[1] - 1)

    def exchange(x_pair, y_pair, c_pair, sends, recvs):
        moves = []
        for n, cx in enumerate((-1, 1)):
            moves.append((x_pair[0].at[1 - n], x_pair[1].at[n], -cx, 0))
        for n, cy in enumerate((1, -1)):
            moves.append((y_pair[0].at[n], y_pair[1].at[n], 0, -cy))
        for n, (cx, cy) in enumerate(CORNERS):
            at = 2 * (0 if cx == 1 else 1) + (0 if cy == 1 else 1)
            moves.append((c_pair[0].at[at], c_pair[1].at[n], -cx, -cy))
        copies = [
            (pltpu.make_async_remote_copy(
                src_ref=src, dst_ref=dst, send_sem=sends.at[n], recv_sem=recvs.at[n],
                device_id=device(tx, ty), device_id_type=MESH), tx, ty)
            for n, (src, dst, tx, ty) in enumerate(moves)
        ]
        for copy, tx, ty in copies:

            @pl.when(present(tx, ty))
            def _():
                copy.start()

        return copies

    def arrive(copies):
        for copy, tx, ty in copies:

            @pl.when(present(-tx, -ty))
            def _():
                copy.wait_recv()

    copies = exchange((xsend, xrecv), (ysend, yrecv), (csend, crecv), ssem, rsem)

    to_x = [16 * z_at + 4 * y_in + t for t in range(4)]

    def lattice_tile(of_block, t):
        got = take(of_block[0], to_x[t])
        for b in range(1, BYN):
            got = jnp.where(block_y == b, take(of_block[b], to_x[t]), got)
        return got

    own = [[lattice_tile([raw[b][f] for b in range(BYN)], t) for t in range(4)] for f in range(5)]
    dam_raw = [row_tile(dam, b).astype(jnp.float32) for b in range(BYN)]
    for t in range(4):
        for c in range(3):
            own_u[c, t] = lattice_tile([u_tile(c, b) for b in range(BYN)], t)
        own_u[3, t] = 1.0 - lattice_tile(dam_raw, t)
    def flag_ext(tile, cx):
        if cx == 0:
            return tile
        return jnp.where(row == (0 if cx < 0 else 7), 0.0, row_roll(tile, -cx))

    seen, enabled = {}, {}

    def see(cy, tile):
        for cx in (-1, 0, 1):
            seen[(cx, cy)] = flag_ext(tile, cx)
        for cx in (-1, 0, 1):
            if cx == 0 and cy == 0:
                continue
            mine = take(flags, 8 * (block_y + 1) + direction(cx, cy))
            back = direction(-cx, -cy)
            theirs = take(seen[(cx, 0)], 8 * (block_y + cy + 1) + back)
            if cy == 1:
                theirs = jnp.where(block_y == 3, take(seen[(cx, 1)], 8 + back + 0 * lane), theirs)
            if cy == -1:
                theirs = jnp.where(block_y == 0, take(seen[(cx, -1)], 32 + back + 0 * lane), theirs)
            enabled[(cx, cy)] = jnp.minimum(jnp.maximum(mine, theirs), 1.0)

    def hold_health(dys):
        for dy in dys:
            deep = max(m for (a, _), m in COLUMNS.items() if a == dy)
            by_cx = {}
            for cx in (-1, 0, 1):
                near = enabled.get((cx, 0))
                if dy == 0:
                    by_cx[cx] = near
                    continue
                near = 1.0 if near is None else near
                if dy > 0:
                    by_cx[cx] = jnp.where(y_in + dy >= 4, enabled[(cx, 1)], near)
                else:
                    by_cx[cx] = jnp.where(y_in + dy < 0, enabled[(cx, -1)], near)
            for dx in range(-deep, deep + 1):
                for t in range(4):
                    flag = by_cx[(t + dx) // 4]
                    h = own[0][t]
                    health_m[dy + 3, dx + 3, t] = h if flag is None else h * flag

    z_ok = {dz: (z_at + dz >= 0) & (z_at + dz < 8) for dz in range(-3, 4)}

    def dz_of(dy):
        return [dz for dz in range(-3, 4) if (dy, dz) in COLUMNS]

    def gather_sums(k, dys, fresh):
        total = {}
        for dy in dys:
            part = {}
            for dz in dz_of(dy):
                deep = COLUMNS[(dy, dz)]
                turn = -(8 * dy + dz)
                value = spread(lane_roll(fields[dy + 3, k + 1], turn), deep)
                if k is FIRST:
                    h = lane_roll(fields[dy + 3, 0], turn)
                    if dz != 0:
                        h = jnp.where(z_ok[dz][None], h, 0.0)
                    h = spread(h, deep, row[None])
                a0, a1, a2 = None, None, None
                for reach in range(deep + 1):
                    terms = []
                    for dx in (reach, -reach) if reach else (0,):
                        lo = deep + dx
                        at = W_AT[(dy, dz)] + lo
                        if dy == 0 and dz == 0 and dx == 0:
                            continue
                        if k is FIRST:
                            w = jnp.minimum(health_m[dy + 3, dx + 3], h[lo : lo + 4])
                            weights[at] = w
                        else:
                            w = weights[at]
                        terms.append(w * value[lo : lo + 4])
                    if not terms:
                        continue
                    both = terms[0] if reach == 0 else terms[0] + terms[1]
                    a0 = add(a0, both)
                    if reach:
                        a1 = add(a1, times(reach, terms[0] - terms[1]))
                        if k is FIRST:
                            a2 = add(a2, times(reach * reach, both))
                if dy != 0:
                    part["y"] = add(part.get("y"), a0)
                if dz != 0:
                    part["z"] = add(part.get("z"), times(dz, a0))
                    if k is FIRST:
                        part["zz"] = add(part.get("zz"), times(dz * dz, a0))
                        if a1 is not None:
                            part["xz"] = add(part.get("xz"), times(dz, a1))
                if a1 is not None:
                    part["x"] = add(part.get("x"), a1)
                if a2 is not None:
                    part["xx"] = add(part.get("xx"), a2)
            for name in ("x", "z", "xx", "zz", "xz"):
                if name in part:
                    total[name] = add(total.get(name), part[name])
            if dy != 0:
                total["y"] = add(total.get("y"), times(dy, part["y"]))
                if k is FIRST:
                    total["yy"] = add(total.get("yy"), times(dy * dy, part["y"]))
                    for name, to in (("x", "xy"), ("z", "yz")):
                        if name in part:
                            total[to] = add(total.get(to), times(dy, part[name]))
        for n, name in enumerate(("x", "y", "z")):
            if name in total:
                at = 6 + 3 * k + n
                sums[at] = total[name] if fresh or name == "y" else sums[at] + total[name]
        for n, name in enumerate(ORDER[:6]):
            if name in total:
                sums[n] = total[name] if fresh or "y" in name else sums[n] + total[name]

    def first_sums(dys, fresh):
        gather_sums(FIRST, dys, fresh)

        def feature(k, carry):
            gather_sums(k, dys, fresh)
            return carry

        lax.fori_loop(1, 4, feature, 0)

    see(0, flags)
    hold_health((0,))
    for f in range(5):
        for t in range(4):
            fields[3, f, t] = own[f][t]
    first_sums((0,), True)

    arrive(copies[2:4])
    see(1, yrecv[0, 5])
    see(-1, yrecv[1, 5])
    hold_health(OTHERS)

    side_lane = lane < 64
    for f in range(5):
        for t in range(4):
            outer = jnp.where(side_lane, take(yrecv[0, f], to_x[t]), take(yrecv[1, f], to_x[t]))
            for k in (1, 2, 3):
                fields[3 + k, f, t] = jnp.where(y_at < k, outer, own[f][t])
                fields[3 - k, f, t] = jnp.where(y_at >= 16 - k, outer, own[f][t])
    first_sums(OTHERS, False)

    arrive(copies[:2] + copies[4:])
    edge = [
        jnp.concatenate([xrecv[0, 4 * k : 4 * k + 4, :], xrecv[1, 4 * k : 4 * k + 4, :]], axis=0)
        for k in (4, 3, 0, 1, 2)
    ]
    edge = edge[:2] + [edge[1] * e for e in edge[2:]]

    def edge_tile(f, t):
        got = jnp.where(row % 4 == block_y, take(edge[f], to_x[t]), 0.0)
        got = got + jnp.where(row % 2 == 0, row_roll(got, -1), row_roll(got, 1))
        return got + jnp.where(row % 4 < 2, row_roll(got, -2), row_roll(got, 2))

    corner_low = [
        jnp.where(side_lane, take(crecv[0], to_x[t]), take(crecv[1], to_x[t])) for t in range(4)]
    corner_high = [
        jnp.where(side_lane, take(crecv[2], to_x[t]), take(crecv[3], to_x[t])) for t in range(4)]

    low_end = row < 4

    def end_rows(low, high):
        return jnp.where(low_end, low, high)

    end_flags = end_rows(flags[0:1], flags[7:8])
    end_seen = {
        0: end_rows(xrecv[0, 20:21, :], xrecv[1, 20:21, :]),
        1: end_rows(crecv[0, 5:6, :], crecv[2, 5:6, :]),
        -1: end_rows(crecv[1, 5:6, :], crecv[3, 5:6, :]),
    }
    end_enabled = {}
    for cy in (-1, 0, 1):
        forth = jnp.where(low_end, direction(-1, cy), direction(1, cy))
        back = jnp.where(low_end, direction(1, -cy), direction(-1, -cy))
        theirs = take(end_seen[0], 8 * (block_y + cy + 1) + back)
        if cy == 1:
            theirs = jnp.where(block_y == 3, take(end_seen[1], 8 + back), theirs)
        if cy == -1:
            theirs = jnp.where(block_y == 0, take(end_seen[-1], 32 + back), theirs)
        mine = take(end_flags, 8 * (block_y + 1) + forth)
        end_enabled[cy] = jnp.minimum(jnp.maximum(mine, theirs), 1.0)

    def end_health(table):
        got = jnp.zeros((8, LANES), jnp.float32)
        for r, (_, t, _) in table.items():
            got = jnp.where(row == r, own[0][t][0:1] if r < 4 else own[0][t][7:8], got)
        return got

    def steps(table):
        got = jnp.zeros((8, LANES), jnp.float32)
        for r, (_, _, dx) in table.items():
            got = jnp.where(row == r, float(dx), got)
        return got

    step_two, step_three = steps(REACH_TWO), steps(REACH_THREE)
    health_two = end_health(REACH_TWO)
    end_fields = {0: [], 1: [], 3: []}
    for f in range(5):
        rim = [edge_tile(f, t) for t in range(4)]
        end_fields[0].append(place(row, REACH_TWO, lambda low, t: rim[t]))
        end_fields[1].append(place(
            row, REACH_TWO, lambda low, t: (corner_low if low else corner_high)[t][f : f + 1]))
        end_fields[3].append(place(row, REACH_THREE, lambda low, t: rim[t]))

    end_total = {}
    for dy in range(-2, 3):
        held = health_two
        if dy > 0:
            held = health_two * jnp.where(y_in + dy >= 4, end_enabled[1], end_enabled[0])
        elif dy < 0:
            held = health_two * jnp.where(y_in + dy < 0, end_enabled[-1], end_enabled[0])
        else:
            held = health_two * end_enabled[0]
        src_y = []
        for f in range(5):
            inner, outer = end_fields[0][f], end_fields[1][f]
            if dy > 0:
                inner = jnp.where(y_at < dy, outer, inner)
            elif dy < 0:
                inner = jnp.where(y_at >= 16 + dy, outer, inner)
            src_y.append(inner)
        part = {}
        for dz in range(-3, 4):
            if COLUMNS.get((dy, dz), 0) < 1:
                continue
            src = [lane_roll(e, -(8 * dy + dz)) for e in src_y]
            h = src[0]
            if dz != 0:
                h = jnp.where(z_ok[dz], h, 0.0)
            if COLUMNS[(dy, dz)] == 1:
                h = jnp.where(row % 4 == 2, h, 0.0)
            w = jnp.minimum(held, h)
            end_weights[ENDS.index((dy, dz))] = w
            for k in range(4):
                value = w * src[k + 1]
                part["s", k] = add(part.get(("s", k)), value)
                if dz != 0:
                    part["z", k] = add(part.get(("z", k)), times(dz, value))
                    if k == 0:
                        part["zz"] = add(part.get("zz"), times(dz * dz, value))
        for name in part:
            end_total[name] = add(end_total.get(name), part[name])
        if dy != 0:
            for k in range(4):
                end_total["y", k] = add(end_total.get(("y", k)), times(dy, part["s", k]))
            end_total["yy"] = add(end_total.get("yy"), times(dy * dy, part["s", 0]))
            end_total["yz"] = add(end_total.get("yz"), times(dy, part["z", 0]))
    for k in range(4):
        end_total["x", k] = step_two * end_total["s", k]
    end_total["xx"] = step_two * end_total["x", 0]
    end_total["xy"] = step_two * end_total["y", 0]
    end_total["xz"] = step_two * end_total["z", 0]
    w = jnp.minimum(end_health(REACH_THREE) * end_enabled[0], end_fields[3][0])
    end_weights[len(ENDS)] = w
    three = {("x", k): step_three * (w * end_fields[3][k + 1]) for k in range(4)}
    three["xx"] = step_three * three["x", 0]
    end_sums = [ends_of(row, end_total[name], three.get(name, 0.0)) for name in ORDER]

    to_raw = [8 * (4 * b + (lane // 4) % 4) + lane // 16 for b in range(BYN)]
    x_in = lane % 4

    def block_tile(of_x, b):
        got = take(of_x[0], to_raw[b])
        for t in range(1, 4):
            got = jnp.where(x_in == t, take(of_x[t], to_raw[b]), got)
        return got

    deform, stress = [], []
    for t in range(4):
        full = [with_ends(sums[n, t], end_sums[n], row, t) for n in range(18)]
        kxx, kxy, kxz, kyy, kyz, kzz = full[:6]
        span = full[6:9]
        sym = [kxx, kxy, kxz, kxy, kyy, kyz, kxz, kyz, kzz]
        moment = [
            sym[3 * c + d] + full[9 + 3 * c + d] - own_u[c, t] * span[d]
            for c in range(3) for d in range(3)
        ]
        shape = [sym[n] + 1.0 if n % 4 == 0 else sym[n] for n in range(9)]
        inv = inverse_of(shape)
        grad = product(moment, inv)
        flip = [grad[3 * (n % 3) + n // 3] for n in range(9)]
        twice = product(flip, grad)
        strain = [0.5 * (twice[n] - 1.0) if n % 4 == 0 else 0.5 * twice[n] for n in range(9)]
        trace = LAME * (strain[0] + strain[4] + strain[8])
        second = [
            trace + 2.0 * SHEAR * strain[n] if n % 4 == 0 else 2.0 * SHEAR * strain[n]
            for n in range(9)
        ]
        first = [e * own_u[3, t] for e in product(grad, second)]
        mapped = product(first, inv)
        for c in range(3):
            force[c, t] = mapped[3 * c] * span[0] + mapped[3 * c + 1] * span[1] + mapped[3 * c + 2] * span[2]
        v = own[1][t]
        deform.append(grad)
        stress.append([v * e for e in mapped])

    for n in range(9):
        of_x = [stress[t][n] for t in range(4)]
        for t in range(3):
            xsend2[0, 3 * n + t : 3 * n + t + 1, :] = of_x[t][0:1]
            xsend2[1, 3 * n + t : 3 * n + t + 1, :] = of_x[t + 1][7:8]
        low = of_x[0]
        high = lane_roll(of_x[0], 32)
        for t in range(1, 4):
            low = jnp.where(block_y == t, lane_roll(of_x[t], 32 * t), low)
            high = jnp.where(block_y == t, lane_roll(of_x[t], 32 * (t - 3)), high)
        for k, tile in enumerate((low, high)):
            ysend2[k, n] = tile
            for m, r in enumerate((0, 7)):
                csend2[2 * m + k, n : n + 1, :] = tile[r : r + 1]
        for t in range(4):
            ystress[3, n, t] = of_x[t]

    copies2 = exchange((xsend2, xrecv2), (ysend2, yrecv2), (csend2, crecv2), ssem2, rsem2)

    for n in range(9):
        for b in range(BYN):
            dg_out[pl.ds(4 * n + b, 8, stride=36), :] = block_tile([deform[t][n] for t in range(4)], b)
    def second_sums(dys):
        def component(c, carry):
            total = force[c]
            for dy in dys:
                for dz in dz_of(dy):
                    deep = COLUMNS[(dy, dz)]
                    turn = -(8 * dy + dz)
                    fixed = None
                    if dy != 0:
                        fixed = add(fixed, times(dy, ystress[dy + 3, 3 * c + 1]))
                    if dz != 0:
                        fixed = add(fixed, times(dz, ystress[dy + 3, 3 * c + 2]))
                    if fixed is not None:
                        fixed = spread(lane_roll(fixed, turn), deep)
                    slope = spread(lane_roll(ystress[dy + 3, 3 * c], turn), deep) if deep else None
                    for dx in range(-deep, deep + 1):
                        lo = deep + dx
                        value = None if fixed is None else fixed[lo : lo + 4]
                        if dx != 0:
                            value = add(value, times(dx, slope[lo : lo + 4]))
                        if value is not None:
                            total = total + weights[W_AT[(dy, dz)] + lo] * value
            force[c] = total
            return carry

        lax.fori_loop(0, 3, component, 0)

    second_sums((0,))
    arrive(copies2[2:4])
    for n in range(9):
        for t in range(4):
            inner = ystress[3, n, t]
            outer = jnp.where(
                side_lane, lane_roll(yrecv2[0, n], -32 * t), lane_roll(yrecv2[1, n], 32 * (3 - t)))
            for k in (1, 2, 3):
                ystress[3 + k, n, t] = jnp.where(y_at < k, outer, inner)
                ystress[3 - k, n, t] = jnp.where(y_at >= 16 - k, outer, inner)
    second_sums(OTHERS)

    arrive(copies2[:2] + copies2[4:])

    def corner2(low, high):
        return [
            jnp.where(lane[0:1] < 64, lane_roll(crecv2[low], -32 * t), lane_roll(crecv2[high], 32 * (3 - t)))
            for t in range(4)
        ]

    corner_low2, corner_high2 = corner2(0, 1), corner2(2, 3)

    def halo_row(n, low, t):
        return xrecv2[0, 3 * n + t - 1 : 3 * n + t, :] if low else xrecv2[1, 3 * n + t : 3 * n + t + 1, :]

    end_inner, end_outer, end_force = [], [], []
    for n in range(9):
        scale = step_two if n % 3 == 0 else 1.0
        end_inner.append(scale * place(row, REACH_TWO, lambda low, t: halo_row(n, low, t)))
        end_outer.append(scale * place(
            row, REACH_TWO, lambda low, t: (corner_low2 if low else corner_high2)[t][n : n + 1]))
    for c in range(3):
        total = None
        for dy in range(-2, 3):
            src_y = []
            for d in range(3):
                inner, outer = end_inner[3 * c + d], end_outer[3 * c + d]
                if dy > 0:
                    inner = jnp.where(y_at < dy, outer, inner)
                elif dy < 0:
                    inner = jnp.where(y_at >= 16 + dy, outer, inner)
                src_y.append(inner)
            fixed = src_y[0] if dy == 0 else src_y[0] + times(dy, src_y[1])
            for dz in range(-3, 4):
                if COLUMNS.get((dy, dz), 0) < 1:
                    continue
                value = fixed if dz == 0 else fixed + times(dz, src_y[2])
                value = lane_roll(value, -(8 * dy + dz))
                total = add(total, end_weights[ENDS.index((dy, dz))] * value)
        three = step_three * place(row, REACH_THREE, lambda low, t: halo_row(3 * c, low, t))
        end_force.append(ends_of(row, total, end_weights[len(ENDS)] * three))
    for c in range(3):
        full_force = [with_ends(force[c, t], end_force[c], row, t) for t in range(4)]
        for b in range(BYN):
            force_out[pl.ds(4 * c + b, 8, stride=12), :] = block_tile(full_force, b)
    for copy, tx, ty in copies + copies2:

        @pl.when(present(tx, ty))
        def _():
            copy.wait_send()


def store(dg, force, dg_out, force_out, sem):
    copies = [
        pltpu.make_async_copy(dg, dg_out, sem.at[0]),
        pltpu.make_async_copy(force, force_out, sem.at[1]),
    ]
    for copy in copies:
        copy.start()
    for copy in copies:
        copy.wait()


def local(displacement, volume, health, damage, block_pairs):
    pairs = block_pairs[0, 0].T
    disp = jnp.transpose(displacement, (0, 2, 1, 3)).reshape(-1, LANES)
    rows = [a.reshape(-1, LANES) for a in (volume, health, damage)]
    f32 = jnp.float32
    vmem = pl.BlockSpec(memory_space=pltpu.VMEM)
    dg, force = pl.pallas_call(
        kernel,
        out_shape=(
            pltpu.VMEM((BXN * 9 * BYN, LANES), f32),
            pltpu.VMEM((BXN * 3 * BYN, LANES), f32),
        ),
        in_specs=[pl.BlockSpec(memory_space=pl.ANY)] * 5,
        out_specs=(vmem, vmem),
        scratch_shapes=[
            pltpu.VMEM(disp.shape, f32),
            pltpu.VMEM(rows[0].shape, f32),
            pltpu.VMEM(rows[1].shape, f32),
            pltpu.VMEM(rows[2].shape, jnp.int32),
            pltpu.VMEM(pairs.shape, jnp.int32),
            pltpu.VMEM((2, 6, 8, LANES), f32),
            pltpu.VMEM((2, 6, 8, LANES), f32),
            pltpu.VMEM((2, 24, LANES), f32),
            pltpu.VMEM((2, 24, LANES), f32),
            pltpu.VMEM((4, 8, LANES), f32),
            pltpu.VMEM((4, 8, LANES), f32),
            pltpu.VMEM((2, 9, 8, LANES), f32),
            pltpu.VMEM((2, 9, 8, LANES), f32),
            pltpu.VMEM((2, 27, LANES), f32),
            pltpu.VMEM((2, 27, LANES), f32),
            pltpu.VMEM((4, 9, LANES), f32),
            pltpu.VMEM((4, 9, LANES), f32),
            pltpu.VMEM((7, 5, 4, 8, LANES), f32),
            pltpu.VMEM((4, 4, 8, LANES), f32),
            pltpu.VMEM((7, 7, 4, 8, LANES), f32),
            pltpu.VMEM((W_COUNT, 4, 8, LANES), f32),
            pltpu.VMEM((18, 4, 8, LANES), f32),
            pltpu.VMEM((7, 9, 4, 8, LANES), f32),
            pltpu.VMEM((3, 4, 8, LANES), f32),
            pltpu.VMEM((len(ENDS) + 1, 8, LANES), f32),
            pltpu.SemaphoreType.DMA((5,)),
            pltpu.SemaphoreType.DMA((8,)),
            pltpu.SemaphoreType.DMA((8,)),
            pltpu.SemaphoreType.DMA((8,)),
            pltpu.SemaphoreType.DMA((8,)),
        ],
        compiler_params=pltpu.CompilerParams(collective_id=0, has_side_effects=True),
        name="peridynamics",
    )(disp, *rows, pairs)
    dg, force = (pltpu.with_memory_space_constraint(a, pltpu.VMEM) for a in (dg, force))
    hbm = pl.BlockSpec(memory_space=pltpu.HBM)
    dg, force = pl.pallas_call(
        store,
        out_shape=(
            jax.ShapeDtypeStruct(dg.shape, f32),
            jax.ShapeDtypeStruct(force.shape, f32),
        ),
        in_specs=[vmem] * 2,
        out_specs=(hbm, hbm),
        scratch_shapes=[pltpu.SemaphoreType.DMA((2,))],
        name="store",
    )(dg, force)
    dg, force = (a.reshape(BXN, -1, BYN, LANES) for a in (dg, force))
    return jnp.transpose(dg, (0, 2, 1, 3)), jnp.transpose(force, (0, 2, 1, 3))


def solution(mesh):
    in_specs = (
        P("gx", "gy", None, None),
        P("gx", "gy", None),
        P("gx", "gy", None),
        P("gx", "gy", None),
        P("gx", "gy", None, None),
    )
    out_specs = (P("gx", "gy", None, None), P("gx", "gy", None, None))
    return jax.shard_map(local, mesh=mesh, in_specs=in_specs, out_specs=out_specs, check_vma=False)
```

```python
import jax
import jax.numpy as jnp
from jax import lax
from jax.experimental import pallas as pl
from jax.experimental.pallas import tpu as pltpu
from jax.sharding import PartitionSpec as P

MESH = pl.DeviceIdType.MESH
LANES = 128
BXN, BYN = 8, 4
LAME, SHEAR = 24.0, 16.0
COLUMNS = {}
for _dy in range(-3, 4):
    for _dz in range(-3, 4):
        _rest = 9 - _dy * _dy - _dz * _dz
        if _rest >= 0:
            COLUMNS[(_dy, _dz)] = max(k for k in range(4) if k * k <= _rest)
W_AT, _n = {}, 0
for _key, _m in COLUMNS.items():
    W_AT[_key] = _n
    _n += 2 * _m + 1
W_COUNT = _n
PLANE = 12
CORNERS = ((-1, 1), (-1, -1), (1, 1), (1, -1))


REACH_TWO = {0: (2, 0, -2), 1: (3, 1, -2), 2: (3, 0, -1), 4: (1, 3, 2), 5: (0, 2, 2), 6: (0, 3, 1)}
REACH_THREE = {0: (1, 0, -3), 1: (2, 1, -3), 2: (3, 2, -3), 4: (2, 3, 3), 5: (1, 2, 3), 6: (0, 1, 3)}
ORDER = ["xx", "xy", "xz", "yy", "yz", "zz"] + [(a, k) for k in range(4) for a in "xyz"]
OTHERS = (-3, -2, -1, 1, 2, 3)
FIRST = 0
ENDS = [key for key in COLUMNS if COLUMNS[key] >= 1]


def direction(cx, cy):
    q = 3 * cx + cy
    return q - 1 if q > 0 else 3 - q


def iota(axis):
    return lax.broadcasted_iota(jnp.int32, (8, LANES), axis)


def take(tile, index):
    return jnp.take_along_axis(tile, index, axis=1, mode="promise_in_bounds")


def lane_roll(array, by):
    by = by % LANES
    return array if by == 0 else pltpu.roll(array, by, axis=array.ndim - 1)


def row_roll(tile, by):
    return pltpu.roll(tile, by % 8, axis=0)


def inverse_of(m):
    c00 = m[4] * m[8] - m[5] * m[7]
    c01 = m[5] * m[6] - m[3] * m[8]
    c02 = m[3] * m[7] - m[4] * m[6]
    c10 = m[2] * m[7] - m[1] * m[8]
    c11 = m[0] * m[8] - m[2] * m[6]
    c12 = m[1] * m[6] - m[0] * m[7]
    c20 = m[1] * m[5] - m[2] * m[4]
    c21 = m[2] * m[3] - m[0] * m[5]
    c22 = m[0] * m[4] - m[1] * m[3]
    scale = 1.0 / (m[0] * c00 + m[1] * c01 + m[2] * c02)
    return [c * scale for c in (c00, c10, c20, c01, c11, c21, c02, c12, c22)]


def product(a, b):
    return [
        a[3 * r] * b[c] + a[3 * r + 1] * b[3 + c] + a[3 * r + 2] * b[6 + c]
        for r in range(3)
        for c in range(3)
    ]


def times(k, value):
    return value if k == 1 else (-value if k == -1 else float(k) * value)


def add(total, value):
    return value if total is None else total + value


def spread(own, deep, clear=None):
    if deep == 0:
        return own
    low = pltpu.roll(own[4 - deep :], 1, axis=1)
    high = pltpu.roll(own[:deep], 7, axis=1)
    if clear is not None:
        low = jnp.where(clear == 0, 0.0, low)
        high = jnp.where(clear == 7, 0.0, high)
    return jnp.concatenate([low, own, high], axis=0)


def place(row, table, tile_of):
    got = jnp.zeros((8, LANES), jnp.float32)
    for r, (tile, _, _) in table.items():
        got = jnp.where(row == r, tile_of(r < 4, tile), got)
    return got


def ends_of(row, packed, three):
    gone = jnp.where(row % 4 == 2, 0.0, packed)
    return gone + jnp.where(row % 4 == 0, row_roll(packed, -2), 0.0) + three


def with_ends(tile, ends, row, t):
    if t <= 2:
        tile = tile + jnp.where(row == 0, ends[t : t + 1], 0.0)
    if t >= 1:
        tile = tile + jnp.where(row == 7, ends[7 - t : 8 - t], 0.0)
    return tile


def kernel(
    disp_in, vol_in, hea_in, dam_in, pairs_in, dg_out, force_out,
    disp, vol, hea, dam, pairs,
    ysend, yrecv, xsend, xrecv, csend, crecv, cpass,
    ysend2, yrecv2, xsend2, xrecv2, csend2, crecv2,
    fields, own_u, health_m, weights, sums, ystress, force, deform, end_weights,
    isem, ssem, rsem, ssem2, rsem2,
):
    loads = [
        pltpu.make_async_copy(src, dst, isem.at[n])
        for n, (src, dst) in enumerate((
            (pairs_in, pairs), (disp_in, disp), (vol_in, vol), (hea_in, hea), (dam_in, dam)))
    ]
    for load in loads:
        load.start()
    n_gx, n_gy = lax.axis_size("gx"), lax.axis_size("gy")
    me_x, me_y = lax.axis_index("gx"), lax.axis_index("gy")

    def device(cx, cy):
        return (me_x + cx, me_y + cy)

    inside = {-1: (me_x > 0, me_y > 0), 1: (me_x < n_gx - 1, me_y < n_gy - 1)}

    def present(cx, cy):
        if cx and cy:
            return jnp.logical_and(inside[cx][0], inside[cy][1])
        return inside[cx][0] if cx else inside[cy][1]

    early = jnp.logical_and(lax.rem(me_x, PLANE) == 0, inside[-1][0])
    late = jnp.logical_and(lax.rem(me_x, PLANE) == PLANE - 1, inside[1][0])

    def direct_to(cx, cy):
        here = present(cx, cy)
        return jnp.logical_and(here, jnp.logical_not(early)) if cx == -1 and cy else here

    def direct_from(cx, cy):
        here = present(cx, cy)
        return jnp.logical_and(here, jnp.logical_not(late)) if cx == 1 and cy else here

    barrier = pltpu.get_barrier_semaphore()
    waits = 0
    for cx in (-1, 0, 1):
        for cy in (-1, 0, 1):
            if cx or cy:

                @pl.when(direct_from(cx, cy))
                def _():
                    pl.semaphore_signal(
                        barrier, inc=1, device_id=device(cx, cy), device_id_type=MESH)

                waits = waits + direct_to(cx, cy).astype(jnp.int32)

    for n, cx in enumerate((-1, 1)):

        @pl.when(jnp.logical_not(present(cx, 0)))
        def _():
            xrecv[n] = jnp.zeros(xrecv.shape[1:], jnp.float32)
            xrecv2[n] = jnp.zeros(xrecv2.shape[1:], jnp.float32)

    for n, cy in enumerate((1, -1)):

        @pl.when(jnp.logical_not(present(0, cy)))
        def _():
            yrecv[n] = jnp.zeros(yrecv.shape[1:], jnp.float32)
            yrecv2[n] = jnp.zeros(yrecv2.shape[1:], jnp.float32)

    for n, (cx, cy) in enumerate(CORNERS):

        @pl.when(jnp.logical_not(present(cx, cy)))
        def _():
            crecv2[n] = jnp.zeros(crecv2.shape[1:], jnp.float32)

    row, lane = iota(0), iota(1)
    block_y, y_in, z_at = lane // 32, (lane // 8) % 4, lane % 8
    y_at = lane // 8

    for n, (cx, cy) in enumerate(CORNERS):
        empty = jnp.logical_not(present(cx, cy))
        if cx == 1:
            empty = jnp.logical_and(empty, jnp.logical_not(late))

        @pl.when(empty)
        def _():
            crecv[n] = jnp.zeros(crecv.shape[1:], jnp.float32)

    for load in loads:
        load.wait()
    slots = pairs.shape[1]
    ax, ay, bx, by = (pairs[i : i + 1, :] for i in range(4))
    q = 3 * (bx - ax) + (by - ay) - 1
    wide = lax.broadcasted_iota(jnp.int32, (LANES, slots), 0)
    tall = lax.broadcasted_iota(jnp.int32, (8, slots), 0)
    flags = None
    for at_x, at_y, way in ((ax, ay, q), (bx, by, q + 4)):
        in_row = jnp.where(tall == at_x - 1, 1.0, 0.0)
        in_lane = jnp.where(wide == 8 * at_y + way, 1.0, 0.0)
        flags = add(flags, lax.dot_general(
            in_row, in_lane, (((1,), (1,)), ((), ())), preferred_element_type=jnp.float32))

    def u_tile(c, b):
        return disp[pl.ds(4 * c + b, 8, stride=12), :]

    def row_tile(array, b):
        return array[pl.ds(b, 8, stride=4), :]

    raw = []
    for b in range(BYN):
        v = row_tile(vol, b)
        raw.append([row_tile(hea, b), v] + [v * u_tile(c, b) for c in range(3)])
    for n, b in enumerate((0, 3)):
        for f in range(5):
            ysend[n, f] = raw[b][f]
            for m, r in enumerate((0, 7)):
                csend[2 * m + n, f : f + 1, :] = raw[b][f][r : r + 1]
        ysend[n, 5] = flags
        for m, r in enumerate((0, 7)):
            csend[2 * m + n, 5:6, :] = flags[r : r + 1]
    for m, r in enumerate((0, 7)):
        xsend[m, 0:12, :] = disp[12 * r : 12 * r + 12, :]
        xsend[m, 12:16, :] = vol[4 * r : 4 * r + 4, :]
        xsend[m, 16:20, :] = hea[4 * r : 4 * r + 4, :]
        xsend[m, 20:21, :] = flags[r : r + 1]
    pl.semaphore_wait(barrier, waits)

    def y_moves(src, dst):
        return [(src.at[n], dst.at[n], 0, -cy) for n, cy in enumerate((1, -1))]

    def x_moves(src, dst):
        return [(src.at[1 - n], dst.at[n], -cx, 0) for n, cx in enumerate((-1, 1))]

    def corner_moves(src, dst):
        return [
            (src.at[2 * (0 if cx == 1 else 1) + (0 if cy == 1 else 1)], dst.at[n], -cx, -cy)
            for n, (cx, cy) in enumerate(CORNERS)
        ]

    def exchange(moves, sends, recvs, first=0, to=present):
        copies = [
            (pltpu.make_async_remote_copy(
                src_ref=src, dst_ref=dst, send_sem=sends.at[first + n], recv_sem=recvs.at[first + n],
                device_id=device(tx, ty), device_id_type=MESH), tx, ty)
            for n, (src, dst, tx, ty) in enumerate(moves)
        ]
        for copy, tx, ty in copies:

            @pl.when(to(tx, ty))
            def _():
                copy.start()

        return copies

    def arrive(copies, come=present):
        for copy, tx, ty in copies:

            @pl.when(come(-tx, -ty))
            def _():
                copy.wait_recv()

    copies = exchange(
        corner_moves(csend, crecv) + x_moves(xsend, xrecv) + y_moves(ysend, yrecv),
        ssem, rsem, to=direct_to)

    around = pltpu.make_async_remote_copy(
        src_ref=cpass, dst_ref=crecv.at[2:4], send_sem=ssem.at[8], recv_sem=rsem.at[8],
        device_id=device(-1, 0), device_id_type=MESH)

    @pl.when(early)
    def _():
        arrive(copies[6:])
        for n in range(2):
            for f in range(6):
                cpass[n, f : f + 1, :] = yrecv[n, f, 0:1, :]
        around.start()

    to_x = [16 * z_at + 4 * y_in + t for t in range(4)]

    def lattice_tile(of_block, t):
        got = take(of_block[0], to_x[t])
        for b in range(1, BYN):
            got = jnp.where(block_y == b, take(of_block[b], to_x[t]), got)
        return got

    own = [[lattice_tile([raw[b][f] for b in range(BYN)], t) for t in range(4)] for f in range(5)]
    dam_raw = [row_tile(dam, b).astype(jnp.float32) for b in range(BYN)]
    for t in range(4):
        for c in range(3):
            own_u[c, t] = lattice_tile([u_tile(c, b) for b in range(BYN)], t)
        own_u[3, t] = 1.0 - lattice_tile(dam_raw, t)
    def flag_ext(tile, cx):
        if cx == 0:
            return tile
        return jnp.where(row == (0 if cx < 0 else 7), 0.0, row_roll(tile, -cx))

    seen, enabled = {}, {}

    def see(cy, tile):
        for cx in (-1, 0, 1):
            seen[(cx, cy)] = flag_ext(tile, cx)
        for cx in (-1, 0, 1):
            if cx == 0 and cy == 0:
                continue
            mine = take(flags, 8 * (block_y + 1) + direction(cx, cy))
            back = direction(-cx, -cy)
            theirs = take(seen[(cx, 0)], 8 * (block_y + cy + 1) + back)
            if cy == 1:
                theirs = jnp.where(block_y == 3, take(seen[(cx, 1)], 8 + back + 0 * lane), theirs)
            if cy == -1:
                theirs = jnp.where(block_y == 0, take(seen[(cx, -1)], 32 + back + 0 * lane), theirs)
            enabled[(cx, cy)] = jnp.minimum(jnp.maximum(mine, theirs), 1.0)

    def hold_health(dys):
        for dy in dys:
            deep = max(m for (a, _), m in COLUMNS.items() if a == dy)
            by_cx = {}
            for cx in (-1, 0, 1):
                near = enabled.get((cx, 0))
                if dy == 0:
                    by_cx[cx] = near
                    continue
                near = 1.0 if near is None else near
                if dy > 0:
                    by_cx[cx] = jnp.where(y_in + dy >= 4, enabled[(cx, 1)], near)
                else:
                    by_cx[cx] = jnp.where(y_in + dy < 0, enabled[(cx, -1)], near)
            for dx in range(-deep, deep + 1):
                for t in range(4):
                    flag = by_cx[(t + dx) // 4]
                    h = own[0][t]
                    health_m[dy + 3, dx + 3, t] = h if flag is None else h * flag

    z_ok = {dz: (z_at + dz >= 0) & (z_at + dz < 8) for dz in range(-3, 4)}

    def dz_of(dy):
        return [dz for dz in range(-3, 4) if (dy, dz) in COLUMNS]

    def gather_sums(k, dys, fresh):
        total = {}
        for dy in dys:
            part = {}
            for dz in dz_of(dy):
                deep = COLUMNS[(dy, dz)]
                turn = -(8 * dy + dz)
                value = spread(lane_roll(fields[dy + 3, k + 1], turn), deep)
                if k is FIRST:
                    h = lane_roll(fields[dy + 3, 0], turn)
                    if dz != 0:
                        h = jnp.where(z_ok[dz][None], h, 0.0)
                    h = spread(h, deep, row[None])
                a0, a1, a2 = None, None, None
                for reach in range(deep + 1):
                    terms = []
                    for dx in (reach, -reach) if reach else (0,):
                        lo = deep + dx
                        at = W_AT[(dy, dz)] + lo
                        if dy == 0 and dz == 0 and dx == 0:
                            continue
                        if k is FIRST:
                            w = jnp.minimum(health_m[dy + 3, dx + 3], h[lo : lo + 4])
                            weights[at] = w
                        else:
                            w = weights[at]
                        terms.append(w * value[lo : lo + 4])
                    if not terms:
                        continue
                    both = terms[0] if reach == 0 else terms[0] + terms[1]
                    a0 = add(a0, both)
                    if reach:
                        a1 = add(a1, times(reach, terms[0] - terms[1]))
                        if k is FIRST:
                            a2 = add(a2, times(reach * reach, both))
                if dy != 0:
                    part["y"] = add(part.get("y"), a0)
                if dz != 0:
                    part["z"] = add(part.get("z"), times(dz, a0))
                    if k is FIRST:
                        part["zz"] = add(part.get("zz"), times(dz * dz, a0))
                        if a1 is not None:
                            part["xz"] = add(part.get("xz"), times(dz, a1))
                if a1 is not None:
                    part["x"] = add(part.get("x"), a1)
                if a2 is not None:
                    part["xx"] = add(part.get("xx"), a2)
            for name in ("x", "z", "xx", "zz", "xz"):
                if name in part:
                    total[name] = add(total.get(name), part[name])
            if dy != 0:
                total["y"] = add(total.get("y"), times(dy, part["y"]))
                if k is FIRST:
                    total["yy"] = add(total.get("yy"), times(dy * dy, part["y"]))
                    for name, to in (("x", "xy"), ("z", "yz")):
                        if name in part:
                            total[to] = add(total.get(to), times(dy, part[name]))
        for n, name in enumerate(("x", "y", "z")):
            if name in total:
                at = 6 + 3 * k + n
                sums[at] = total[name] if fresh or name == "y" else sums[at] + total[name]
        for n, name in enumerate(ORDER[:6]):
            if name in total:
                sums[n] = total[name] if fresh or "y" in name else sums[n] + total[name]

    def first_sums(dys, fresh):
        gather_sums(FIRST, dys, fresh)

        def feature(k, carry):
            gather_sums(k, dys, fresh)
            return carry

        lax.fori_loop(1, 4, feature, 0)

    see(0, flags)
    hold_health((0,))
    for f in range(5):
        for t in range(4):
            fields[3, f, t] = own[f][t]
    first_sums((0,), True)

    arrive(copies[6:], lambda cx, cy: jnp.logical_and(present(cx, cy), jnp.logical_not(early)))
    see(1, yrecv[0, 5])
    see(-1, yrecv[1, 5])
    hold_health(OTHERS)

    side_lane = lane < 64
    for f in range(5):
        for t in range(4):
            outer = jnp.where(side_lane, take(yrecv[0, f], to_x[t]), take(yrecv[1, f], to_x[t]))
            for k in (1, 2, 3):
                fields[3 + k, f, t] = jnp.where(y_at < k, outer, own[f][t])
                fields[3 - k, f, t] = jnp.where(y_at >= 16 - k, outer, own[f][t])
    first_sums(OTHERS, False)

    def end_pack(tile_of):
        got = jnp.zeros((8, LANES), jnp.float32)
        for t in range(3):
            got = jnp.where(row == t, tile_of(t)[0:1], got)
            got = jnp.where(row == 6 - t, tile_of(t + 1)[7:8], got)
        return got

    end_sums = [end_pack(lambda t: sums[n, t]) for n in range(18)]
    end_u = [end_pack(lambda t: own_u[c, t]) for c in range(4)]
    end_volume = end_pack(lambda t: own[1][t])

    def row_sum(tile):
        tile = tile + jnp.where(row % 2 == 0, row_roll(tile, -1), row_roll(tile, 1))
        return tile + jnp.where(row % 4 < 2, row_roll(tile, -2), row_roll(tile, 2))

    arrive(copies[:6], direct_from)

    @pl.when(late)
    def _():
        around.wait_recv()

    edge = [
        jnp.concatenate([xrecv[0, 4 * k : 4 * k + 4, :], xrecv[1, 4 * k : 4 * k + 4, :]], axis=0)
        for k in (4, 3, 0, 1, 2)
    ]
    edge = edge[:2] + [edge[1] * e for e in edge[2:]]

    def edge_tile(f, t):
        return row_sum(jnp.where(row % 4 == block_y, take(edge[f], to_x[t]), 0.0))

    corner_low = [
        jnp.where(side_lane, take(crecv[0], to_x[t]), take(crecv[1], to_x[t])) for t in range(4)]
    corner_high = [
        jnp.where(side_lane, take(crecv[2], to_x[t]), take(crecv[3], to_x[t])) for t in range(4)]

    low_end = row < 4

    def end_rows(low, high):
        return jnp.where(low_end, low, high)

    end_flags = end_rows(flags[0:1], flags[7:8])
    end_seen = {
        0: end_rows(xrecv[0, 20:21, :], xrecv[1, 20:21, :]),
        1: end_rows(crecv[0, 5:6, :], crecv[2, 5:6, :]),
        -1: end_rows(crecv[1, 5:6, :], crecv[3, 5:6, :]),
    }
    end_enabled = {}
    for cy in (-1, 0, 1):
        forth = jnp.where(low_end, direction(-1, cy), direction(1, cy))
        back = jnp.where(low_end, direction(1, -cy), direction(-1, -cy))
        theirs = take(end_seen[0], 8 * (block_y + cy + 1) + back)
        if cy == 1:
            theirs = jnp.where(block_y == 3, take(end_seen[1], 8 + back), theirs)
        if cy == -1:
            theirs = jnp.where(block_y == 0, take(end_seen[-1], 32 + back), theirs)
        mine = take(end_flags, 8 * (block_y + 1) + forth)
        end_enabled[cy] = jnp.minimum(jnp.maximum(mine, theirs), 1.0)

    def end_health(table):
        got = jnp.zeros((8, LANES), jnp.float32)
        for r, (_, t, _) in table.items():
            got = jnp.where(row == r, own[0][t][0:1] if r < 4 else own[0][t][7:8], got)
        return got

    def steps(table):
        got = jnp.zeros((8, LANES), jnp.float32)
        for r, (_, _, dx) in table.items():
            got = jnp.where(row == r, float(dx), got)
        return got

    step_two, step_three = steps(REACH_TWO), steps(REACH_THREE)
    health_two = end_health(REACH_TWO)
    end_fields = {0: [], 1: [], 3: []}
    for f in range(5):
        rim = [edge_tile(f, t) for t in range(4)]
        end_fields[0].append(place(row, REACH_TWO, lambda low, t: rim[t]))
        end_fields[1].append(place(
            row, REACH_TWO, lambda low, t: (corner_low if low else corner_high)[t][f : f + 1]))
        end_fields[3].append(place(row, REACH_THREE, lambda low, t: rim[t]))

    end_total = {}
    for dy in range(-2, 3):
        held = health_two
        if dy > 0:
            held = health_two * jnp.where(y_in + dy >= 4, end_enabled[1], end_enabled[0])
        elif dy < 0:
            held = health_two * jnp.where(y_in + dy < 0, end_enabled[-1], end_enabled[0])
        else:
            held = health_two * end_enabled[0]
        src_y = []
        for f in range(5):
            inner, outer = end_fields[0][f], end_fields[1][f]
            if dy > 0:
                inner = jnp.where(y_at < dy, outer, inner)
            elif dy < 0:
                inner = jnp.where(y_at >= 16 + dy, outer, inner)
            src_y.append(inner)
        part = {}
        for dz in range(-3, 4):
            if COLUMNS.get((dy, dz), 0) < 1:
                continue
            src = [lane_roll(e, -(8 * dy + dz)) for e in src_y]
            h = src[0]
            if dz != 0:
                h = jnp.where(z_ok[dz], h, 0.0)
            if COLUMNS[(dy, dz)] == 1:
                h = jnp.where(row % 4 == 2, h, 0.0)
            w = jnp.minimum(held, h)
            end_weights[ENDS.index((dy, dz))] = w
            for k in range(4):
                value = w * src[k + 1]
                part["s", k] = add(part.get(("s", k)), value)
                if dz != 0:
                    part["z", k] = add(part.get(("z", k)), times(dz, value))
                    if k == 0:
                        part["zz"] = add(part.get("zz"), times(dz * dz, value))
        for name in part:
            end_total[name] = add(end_total.get(name), part[name])
        if dy != 0:
            for k in range(4):
                end_total["y", k] = add(end_total.get(("y", k)), times(dy, part["s", k]))
            end_total["yy"] = add(end_total.get("yy"), times(dy * dy, part["s", 0]))
            end_total["yz"] = add(end_total.get("yz"), times(dy, part["z", 0]))
    for k in range(4):
        end_total["x", k] = step_two * end_total["s", k]
    end_total["xx"] = step_two * end_total["x", 0]
    end_total["xy"] = step_two * end_total["y", 0]
    end_total["xz"] = step_two * end_total["z", 0]
    w = jnp.minimum(end_health(REACH_THREE) * end_enabled[0], end_fields[3][0])
    end_weights[len(ENDS)] = w
    three = {("x", k): step_three * (w * end_fields[3][k + 1]) for k in range(4)}
    three["xx"] = step_three * three["x", 0]
    end_more = [ends_of(row, end_total[name], three.get(name, 0.0)) for name in ORDER]

    def material(full, u):
        kxx, kxy, kxz, kyy, kyz, kzz = full[:6]
        span = full[6:9]
        sym = [kxx, kxy, kxz, kxy, kyy, kyz, kxz, kyz, kzz]
        moment = [
            sym[3 * c + d] + full[9 + 3 * c + d] - u[c] * span[d]
            for c in range(3) for d in range(3)
        ]
        shape = [sym[n] + 1.0 if n % 4 == 0 else sym[n] for n in range(9)]
        inv = inverse_of(shape)
        grad = product(moment, inv)
        flip = [grad[3 * (n % 3) + n // 3] for n in range(9)]
        twice = product(flip, grad)
        strain = [0.5 * (twice[n] - 1.0) if n % 4 == 0 else 0.5 * twice[n] for n in range(9)]
        trace = LAME * (strain[0] + strain[4] + strain[8])
        second = [
            trace + 2.0 * SHEAR * strain[n] if n % 4 == 0 else 2.0 * SHEAR * strain[n]
            for n in range(9)
        ]
        first = [e * u[3] for e in product(grad, second)]
        return grad, product(first, inv)

    _, end_mapped = material([a + b for a, b in zip(end_sums, end_more)], end_u)
    for n in range(9):
        tile = end_volume * end_mapped[n]
        xsend2[0, 3 * n : 3 * n + 3, :] = tile[0:3]
        xsend2[1, 3 * n : 3 * n + 3, :] = tile[4:7]
        for k, slot in enumerate((0, 3)):
            wide_tile = take(tile, 32 * slot + lane % 32)
            wide_tile = jnp.where(block_y == row % 4, wide_tile, 0.0)
            wide_tile = wide_tile + (row_roll(wide_tile, -1) + row_roll(wide_tile, -2))
            for m in range(2):
                csend2[2 * m + k, n : n + 1, :] = wide_tile[4 * m : 4 * m + 1]
    copies2 = exchange(corner_moves(csend2, crecv2) + x_moves(xsend2, xrecv2), ssem2, rsem2)

    to_raw = [8 * (4 * b + (lane // 4) % 4) + lane // 16 for b in range(BYN)]
    x_in = lane % 4

    def block_tile(of_x, b):
        got = take(of_x[0], to_raw[b])
        for t in range(1, 4):
            got = jnp.where(x_in == t, take(of_x[t], to_raw[b]), got)
        return got

    stress = []
    for t in range(4):
        full = [with_ends(sums[n, t], end_more[n], row, t) for n in range(18)]
        grad, mapped = material(full, [own_u[c, t] for c in range(4)])
        span = full[6:9]
        for c in range(3):
            force[c, t] = mapped[3 * c] * span[0] + mapped[3 * c + 1] * span[1] + mapped[3 * c + 2] * span[2]
        v = own[1][t]
        for n in range(9):
            deform[n, t] = grad[n]
        stress.append([v * e for e in mapped])

    for n in range(9):
        of_x = [stress[t][n] for t in range(4)]
        low = of_x[0]
        high = lane_roll(of_x[0], 32)
        for t in range(1, 4):
            low = jnp.where(block_y == t, lane_roll(of_x[t], 32 * t), low)
            high = jnp.where(block_y == t, lane_roll(of_x[t], 32 * (t - 3)), high)
        for k, tile in enumerate((low, high)):
            ysend2[k, n] = tile
        for t in range(4):
            ystress[3, n, t] = of_x[t]

    copies2 += exchange(y_moves(ysend2, yrecv2), ssem2, rsem2, 6)

    def second_sums(dys):
        def component(c, carry):
            total = force[c]
            for dy in dys:
                for dz in dz_of(dy):
                    deep = COLUMNS[(dy, dz)]
                    turn = -(8 * dy + dz)
                    fixed = None
                    if dy != 0:
                        fixed = add(fixed, times(dy, ystress[dy + 3, 3 * c + 1]))
                    if dz != 0:
                        fixed = add(fixed, times(dz, ystress[dy + 3, 3 * c + 2]))
                    if fixed is not None:
                        fixed = spread(lane_roll(fixed, turn), deep)
                    slope = spread(lane_roll(ystress[dy + 3, 3 * c], turn), deep) if deep else None
                    for dx in range(-deep, deep + 1):
                        lo = deep + dx
                        value = None if fixed is None else fixed[lo : lo + 4]
                        if dx != 0:
                            value = add(value, times(dx, slope[lo : lo + 4]))
                        if value is not None:
                            total = total + weights[W_AT[(dy, dz)] + lo] * value
            force[c] = total
            return carry

        lax.fori_loop(0, 3, component, 0)

    second_sums((0,))
    for n in range(9):
        for b in range(BYN):
            dg_out[pl.ds(4 * n + b, 8, stride=36), :] = block_tile([deform[n, t] for t in range(4)], b)

    arrive(copies2[6:])
    for n in range(9):
        for t in range(4):
            inner = ystress[3, n, t]
            outer = jnp.where(
                side_lane, lane_roll(yrecv2[0, n], -32 * t), lane_roll(yrecv2[1, n], 32 * (3 - t)))
            for k in (1, 2, 3):
                ystress[3 + k, n, t] = jnp.where(y_at < k, outer, inner)
                ystress[3 - k, n, t] = jnp.where(y_at >= 16 - k, outer, inner)
    second_sums(OTHERS)

    for c in range(3):
        for b in range(BYN):
            force_out[pl.ds(4 * c + b, 8, stride=12), :] = block_tile([force[c, t] for t in range(4)], b)

    arrive(copies2[:6])

    def corner2(low, high, slots):
        return [
            jnp.where(lane[0:1] < 64, lane_roll(crecv2[low], -32 * k), lane_roll(crecv2[high], 32 * (3 - k)))
            for k in slots
        ]

    corner_low2, corner_high2 = corner2(0, 1, (3, 2, 1, 0)), corner2(2, 3, (0, 1, 2, 3))

    def halo_row(n, low, t):
        at = 3 * n + (3 - t if low else t)
        return xrecv2[0 if low else 1, at : at + 1, :]

    end_inner, end_outer, end_force = [], [], []
    for n in range(9):
        scale = step_two if n % 3 == 0 else 1.0
        end_inner.append(scale * place(row, REACH_TWO, lambda low, t: halo_row(n, low, t)))
        end_outer.append(scale * place(
            row, REACH_TWO, lambda low, t: (corner_low2 if low else corner_high2)[t][n : n + 1]))
    for c in range(3):
        total = None
        for dy in range(-2, 3):
            src_y = []
            for d in range(3):
                inner, outer = end_inner[3 * c + d], end_outer[3 * c + d]
                if dy > 0:
                    inner = jnp.where(y_at < dy, outer, inner)
                elif dy < 0:
                    inner = jnp.where(y_at >= 16 + dy, outer, inner)
                src_y.append(inner)
            fixed = src_y[0] if dy == 0 else src_y[0] + times(dy, src_y[1])
            for dz in range(-3, 4):
                if COLUMNS.get((dy, dz), 0) < 1:
                    continue
                value = fixed if dz == 0 else fixed + times(dz, src_y[2])
                value = lane_roll(value, -(8 * dy + dz))
                total = add(total, end_weights[ENDS.index((dy, dz))] * value)
        three = step_three * place(row, REACH_THREE, lambda low, t: halo_row(3 * c, low, t))
        end_force.append(ends_of(row, total, end_weights[len(ENDS)] * three))
    own_x = jnp.where(low_end, row, 7 - row)
    for c in range(3):
        for b in range(BYN):
            at = pl.ds(4 * c + b, 8, stride=12)
            more = row_sum(jnp.where(x_in == own_x, take(end_force[c], to_raw[b]), 0.0))
            force_out[at, :] = force_out[at, :] + jnp.where(row % 7 == 0, more, 0.0)
    for group, to in ((copies, direct_to), (copies2, present)):
        for copy, tx, ty in group:

            @pl.when(to(tx, ty))
            def _():
                copy.wait_send()

    @pl.when(early)
    def _():
        around.wait_send()


def store(dg, force, dg_out, force_out, sem):
    copies = [
        pltpu.make_async_copy(dg, dg_out, sem.at[0]),
        pltpu.make_async_copy(force, force_out, sem.at[1]),
    ]
    for copy in copies:
        copy.start()
    for copy in copies:
        copy.wait()


def local(displacement, volume, health, damage, block_pairs):
    pairs = block_pairs[0, 0].T
    disp = jnp.transpose(displacement, (0, 2, 1, 3)).reshape(-1, LANES)
    rows = [a.reshape(-1, LANES) for a in (volume, health, damage)]
    f32 = jnp.float32
    vmem = pl.BlockSpec(memory_space=pltpu.VMEM)
    dg, force = pl.pallas_call(
        kernel,
        out_shape=(
            pltpu.VMEM((BXN * 9 * BYN, LANES), f32),
            pltpu.VMEM((BXN * 3 * BYN, LANES), f32),
        ),
        in_specs=[pl.BlockSpec(memory_space=pl.ANY)] * 5,
        out_specs=(vmem, vmem),
        scratch_shapes=[
            pltpu.VMEM(disp.shape, f32),
            pltpu.VMEM(rows[0].shape, f32),
            pltpu.VMEM(rows[1].shape, f32),
            pltpu.VMEM(rows[2].shape, jnp.int32),
            pltpu.VMEM(pairs.shape, jnp.int32),
            pltpu.VMEM((2, 6, 8, LANES), f32),
            pltpu.VMEM((2, 6, 8, LANES), f32),
            pltpu.VMEM((2, 24, LANES), f32),
            pltpu.VMEM((2, 24, LANES), f32),
            pltpu.VMEM((4, 8, LANES), f32),
            pltpu.VMEM((4, 8, LANES), f32),
            pltpu.VMEM((2, 8, LANES), f32),
            pltpu.VMEM((2, 9, 8, LANES), f32),
            pltpu.VMEM((2, 9, 8, LANES), f32),
            pltpu.VMEM((2, 27, LANES), f32),
            pltpu.VMEM((2, 27, LANES), f32),
            pltpu.VMEM((4, 9, LANES), f32),
            pltpu.VMEM((4, 9, LANES), f32),
            pltpu.VMEM((7, 5, 4, 8, LANES), f32),
            pltpu.VMEM((4, 4, 8, LANES), f32),
            pltpu.VMEM((7, 7, 4, 8, LANES), f32),
            pltpu.VMEM((W_COUNT, 4, 8, LANES), f32),
            pltpu.VMEM((18, 4, 8, LANES), f32),
            pltpu.VMEM((7, 9, 4, 8, LANES), f32),
            pltpu.VMEM((3, 4, 8, LANES), f32),
            pltpu.VMEM((9, 4, 8, LANES), f32),
            pltpu.VMEM((len(ENDS) + 1, 8, LANES), f32),
            pltpu.SemaphoreType.DMA((5,)),
            pltpu.SemaphoreType.DMA((9,)),
            pltpu.SemaphoreType.DMA((9,)),
            pltpu.SemaphoreType.DMA((8,)),
            pltpu.SemaphoreType.DMA((8,)),
        ],
        compiler_params=pltpu.CompilerParams(collective_id=0, has_side_effects=True),
        name="peridynamics",
    )(disp, *rows, pairs)
    dg, force = (pltpu.with_memory_space_constraint(a, pltpu.VMEM) for a in (dg, force))
    hbm = pl.BlockSpec(memory_space=pltpu.HBM)
    dg, force = pl.pallas_call(
        store,
        out_shape=(
            jax.ShapeDtypeStruct(dg.shape, f32),
            jax.ShapeDtypeStruct(force.shape, f32),
        ),
        in_specs=[vmem] * 2,
        out_specs=(hbm, hbm),
        scratch_shapes=[pltpu.SemaphoreType.DMA((2,))],
        name="store",
    )(dg, force)
    dg, force = (a.reshape(BXN, -1, BYN, LANES) for a in (dg, force))
    return jnp.transpose(dg, (0, 2, 1, 3)), jnp.transpose(force, (0, 2, 1, 3))


def solution(mesh):
    in_specs = (
        P("gx", "gy", None, None),
        P("gx", "gy", None),
        P("gx", "gy", None),
        P("gx", "gy", None),
        P("gx", "gy", None, None),
    )
    out_specs = (P("gx", "gy", None, None), P("gx", "gy", None, None))
    return jax.shard_map(local, mesh=mesh, in_specs=in_specs, out_specs=out_specs, check_vma=False)
```

```python
import jax
import jax.numpy as jnp
from jax import lax
from jax.experimental import pallas as pl
from jax.experimental.pallas import tpu as pltpu
from jax.sharding import PartitionSpec as P

MESH = pl.DeviceIdType.MESH
LANES = 128
BXN, BYN = 8, 4
LAME, SHEAR = 24.0, 16.0
COLUMNS = {}
for _dy in range(-3, 4):
    for _dz in range(-3, 4):
        _rest = 9 - _dy * _dy - _dz * _dz
        if _rest >= 0:
            COLUMNS[(_dy, _dz)] = max(k for k in range(4) if k * k <= _rest)
W_AT, _n = {}, 0
for _key, _m in COLUMNS.items():
    W_AT[_key] = _n
    _n += 2 * _m + 1
W_COUNT = _n
PLANE = 12
CORNERS = ((-1, 1), (-1, -1), (1, 1), (1, -1))


REACH_TWO = {0: (2, 0, -2), 1: (3, 1, -2), 2: (3, 0, -1), 4: (1, 3, 2), 5: (0, 2, 2), 6: (0, 3, 1)}
REACH_THREE = {0: (1, 0, -3), 1: (2, 1, -3), 2: (3, 2, -3), 4: (2, 3, 3), 5: (1, 2, 3), 6: (0, 1, 3)}
ORDER = ["xx", "xy", "xz", "yy", "yz", "zz"] + [(a, k) for k in range(4) for a in "xyz"]
OTHERS = (-3, -2, -1, 1, 2, 3)
FIRST = 0
ENDS = [key for key in COLUMNS if COLUMNS[key] >= 1]


def direction(cx, cy):
    q = 3 * cx + cy
    return q - 1 if q > 0 else 3 - q


def iota(axis):
    return lax.broadcasted_iota(jnp.int32, (8, LANES), axis)


def take(tile, index):
    return jnp.take_along_axis(tile, index, axis=1, mode="promise_in_bounds")


def lane_roll(array, by):
    by = by % LANES
    return array if by == 0 else pltpu.roll(array, by, axis=array.ndim - 1)


def row_roll(tile, by):
    return pltpu.roll(tile, by % 8, axis=0)


def inverse_of(m):
    c00 = m[4] * m[8] - m[5] * m[7]
    c01 = m[5] * m[6] - m[3] * m[8]
    c02 = m[3] * m[7] - m[4] * m[6]
    c10 = m[2] * m[7] - m[1] * m[8]
    c11 = m[0] * m[8] - m[2] * m[6]
    c12 = m[1] * m[6] - m[0] * m[7]
    c20 = m[1] * m[5] - m[2] * m[4]
    c21 = m[2] * m[3] - m[0] * m[5]
    c22 = m[0] * m[4] - m[1] * m[3]
    scale = 1.0 / (m[0] * c00 + m[1] * c01 + m[2] * c02)
    return [c * scale for c in (c00, c10, c20, c01, c11, c21, c02, c12, c22)]


def product(a, b):
    return [
        a[3 * r] * b[c] + a[3 * r + 1] * b[3 + c] + a[3 * r + 2] * b[6 + c]
        for r in range(3)
        for c in range(3)
    ]


def times(k, value):
    return value if k == 1 else (-value if k == -1 else float(k) * value)


def add(total, value):
    return value if total is None else total + value


def spread(own, deep, clear=None):
    if deep == 0:
        return own
    low = pltpu.roll(own[4 - deep :], 1, axis=1)
    high = pltpu.roll(own[:deep], 7, axis=1)
    if clear is not None:
        low = jnp.where(clear == 0, 0.0, low)
        high = jnp.where(clear == 7, 0.0, high)
    return jnp.concatenate([low, own, high], axis=0)


def place(row, table, tile_of):
    got = jnp.zeros((8, LANES), jnp.float32)
    for r, (tile, _, _) in table.items():
        got = jnp.where(row == r, tile_of(r < 4, tile), got)
    return got


def ends_of(row, packed, three):
    gone = jnp.where(row % 4 == 2, 0.0, packed)
    return gone + jnp.where(row % 4 == 0, row_roll(packed, -2), 0.0) + three


def with_ends(tile, ends, row, t):
    if t <= 2:
        tile = tile + jnp.where(row == 0, ends[t : t + 1], 0.0)
    if t >= 1:
        tile = tile + jnp.where(row == 7, ends[7 - t : 8 - t], 0.0)
    return tile


def kernel(
    disp_in, vol_in, hea_in, dam_in, pairs_in, dg_out, force_out,
    disp, vol, hea, dam, pairs,
    ysend, yrecv, xsend, xrecv, csend, crecv, cpass,
    ysend2, yrecv2, xsend2, xrecv2, csend2, crecv2,
    fields, own_u, health_m, weights, sums, ystress, force, deform, end_weights,
    isem, ssem, rsem, ssem2, rsem2, ready,
):
    loads = [
        pltpu.make_async_copy(src, dst, isem.at[n])
        for n, (src, dst) in enumerate((
            (pairs_in, pairs), (disp_in, disp), (vol_in, vol), (hea_in, hea), (dam_in, dam)))
    ]
    for load in loads:
        load.start()
    n_gx, n_gy = lax.axis_size("gx"), lax.axis_size("gy")
    me_x, me_y = lax.axis_index("gx"), lax.axis_index("gy")

    def device(cx, cy):
        return (me_x + cx, me_y + cy)

    inside = {-1: (me_x > 0, me_y > 0), 1: (me_x < n_gx - 1, me_y < n_gy - 1)}

    def present(cx, cy):
        if cx and cy:
            return jnp.logical_and(inside[cx][0], inside[cy][1])
        return inside[cx][0] if cx else inside[cy][1]

    early = jnp.logical_and(lax.rem(me_x, PLANE) == 0, inside[-1][0])
    late = jnp.logical_and(lax.rem(me_x, PLANE) == PLANE - 1, inside[1][0])

    def direct_to(cx, cy):
        here = present(cx, cy)
        return jnp.logical_and(here, jnp.logical_not(early)) if cx == -1 else here

    def direct_from(cx, cy):
        here = present(cx, cy)
        return jnp.logical_and(here, jnp.logical_not(late)) if cx == 1 and cy else here

    barrier = pltpu.get_barrier_semaphore()
    waits = 0
    for cx in (-1, 0, 1):
        for cy in (-1, 0, 1):
            if cx or cy:

                greet = present(cx, cy)
                if cx == 1:
                    greet = jnp.logical_and(greet, jnp.logical_not(late))

                @pl.when(greet)
                def _():
                    pl.semaphore_signal(
                        barrier, inc=1, device_id=device(cx, cy), device_id_type=MESH)

                waits = waits + direct_to(cx, cy).astype(jnp.int32)

    for n, cx in enumerate((-1, 1)):

        @pl.when(jnp.logical_not(present(cx, 0)))
        def _():
            xrecv[n] = jnp.zeros(xrecv.shape[1:], jnp.float32)
            xrecv2[n] = jnp.zeros(xrecv2.shape[1:], jnp.float32)

    for n, cy in enumerate((1, -1)):

        @pl.when(jnp.logical_not(present(0, cy)))
        def _():
            yrecv[n] = jnp.zeros(yrecv.shape[1:], jnp.float32)
            yrecv2[n] = jnp.zeros(yrecv2.shape[1:], jnp.float32)

    for n, (cx, cy) in enumerate(CORNERS):

        @pl.when(jnp.logical_not(present(cx, cy)))
        def _():
            crecv2[n] = jnp.zeros(crecv2.shape[1:], jnp.float32)

    row, lane = iota(0), iota(1)
    block_y, y_in, z_at = lane // 32, (lane // 8) % 4, lane % 8
    y_at = lane // 8

    for n, (cx, cy) in enumerate(CORNERS):
        empty = jnp.logical_not(present(cx, cy))
        if cx == 1:
            empty = jnp.logical_and(empty, jnp.logical_not(late))

        @pl.when(empty)
        def _():
            crecv[n] = jnp.zeros(crecv.shape[1:], jnp.float32)

    for load in loads:
        load.wait()
    slots = pairs.shape[1]
    ax, ay, bx, by = (pairs[i : i + 1, :] for i in range(4))
    q = 3 * (bx - ax) + (by - ay) - 1
    wide = lax.broadcasted_iota(jnp.int32, (LANES, slots), 0)
    tall = lax.broadcasted_iota(jnp.int32, (8, slots), 0)
    flags = None
    for at_x, at_y, way in ((ax, ay, q), (bx, by, q + 4)):
        in_row = jnp.where(tall == at_x - 1, 1.0, 0.0)
        in_lane = jnp.where(wide == 8 * at_y + way, 1.0, 0.0)
        flags = add(flags, lax.dot_general(
            in_row, in_lane, (((1,), (1,)), ((), ())), preferred_element_type=jnp.float32))

    def u_tile(c, b):
        return disp[pl.ds(4 * c + b, 8, stride=12), :]

    def row_tile(array, b):
        return array[pl.ds(b, 8, stride=4), :]

    raw = []
    for b in range(BYN):
        v = row_tile(vol, b)
        raw.append([row_tile(hea, b), v] + [v * u_tile(c, b) for c in range(3)])
    for n, b in enumerate((0, 3)):
        for f in range(5):
            ysend[n, f] = raw[b][f]
            for m, r in enumerate((0, 7)):
                csend[2 * m + n, f : f + 1, :] = raw[b][f][r : r + 1]
        ysend[n, 5] = flags
        for m, r in enumerate((0, 7)):
            csend[2 * m + n, 5:6, :] = flags[r : r + 1]
    for m, r in enumerate((0, 7)):
        xsend[m, 0:12, :] = disp[12 * r : 12 * r + 12, :]
        xsend[m, 12:16, :] = vol[4 * r : 4 * r + 4, :]
        xsend[m, 16:20, :] = hea[4 * r : 4 * r + 4, :]
        xsend[m, 20:21, :] = flags[r : r + 1]
    pl.semaphore_wait(barrier, waits)

    @pl.when(late)
    def _():
        pl.semaphore_signal(ready, inc=1, device_id=device(1, 0), device_id_type=MESH)

    def y_moves(src, dst):
        return [(src.at[n], dst.at[n], 0, -cy) for n, cy in enumerate((1, -1))]

    def x_moves(src, dst):
        return [(src.at[1 - n], dst.at[n], -cx, 0) for n, cx in enumerate((-1, 1))]

    def corner_moves(src, dst):
        return [
            (src.at[2 * (0 if cx == 1 else 1) + (0 if cy == 1 else 1)], dst.at[n], -cx, -cy)
            for n, (cx, cy) in enumerate(CORNERS)
        ]

    def exchange(moves, sends, recvs, first=0, to=present):
        copies = [
            (pltpu.make_async_remote_copy(
                src_ref=src, dst_ref=dst, send_sem=sends.at[first + n], recv_sem=recvs.at[first + n],
                device_id=device(tx, ty), device_id_type=MESH), tx, ty)
            for n, (src, dst, tx, ty) in enumerate(moves)
        ]
        for copy, tx, ty in copies:

            @pl.when(to(tx, ty))
            def _():
                copy.start()

        return copies

    def arrive(copies, come=present):
        for copy, tx, ty in copies:

            @pl.when(come(-tx, -ty))
            def _():
                copy.wait_recv()

    copies = exchange(
        corner_moves(csend, crecv) + x_moves(xsend, xrecv) + y_moves(ysend, yrecv),
        ssem, rsem, to=direct_to)

    around = pltpu.make_async_remote_copy(
        src_ref=cpass, dst_ref=crecv.at[2:4], send_sem=ssem.at[8], recv_sem=rsem.at[8],
        device_id=device(-1, 0), device_id_type=MESH)

    to_x = [16 * z_at + 4 * y_in + t for t in range(4)]

    def lattice_tile(of_block, t):
        got = take(of_block[0], to_x[t])
        for b in range(1, BYN):
            got = jnp.where(block_y == b, take(of_block[b], to_x[t]), got)
        return got

    own = [[lattice_tile([raw[b][f] for b in range(BYN)], t) for t in range(4)] for f in range(5)]
    dam_raw = [row_tile(dam, b).astype(jnp.float32) for b in range(BYN)]
    for t in range(4):
        for c in range(3):
            own_u[c, t] = lattice_tile([u_tile(c, b) for b in range(BYN)], t)
        own_u[3, t] = 1.0 - lattice_tile(dam_raw, t)
    def flag_ext(tile, cx):
        if cx == 0:
            return tile
        return jnp.where(row == (0 if cx < 0 else 7), 0.0, row_roll(tile, -cx))

    seen, enabled = {}, {}

    def see(cy, tile):
        for cx in (-1, 0, 1):
            seen[(cx, cy)] = flag_ext(tile, cx)
        for cx in (-1, 0, 1):
            if cx == 0 and cy == 0:
                continue
            mine = take(flags, 8 * (block_y + 1) + direction(cx, cy))
            back = direction(-cx, -cy)
            theirs = take(seen[(cx, 0)], 8 * (block_y + cy + 1) + back)
            if cy == 1:
                theirs = jnp.where(block_y == 3, take(seen[(cx, 1)], 8 + back + 0 * lane), theirs)
            if cy == -1:
                theirs = jnp.where(block_y == 0, take(seen[(cx, -1)], 32 + back + 0 * lane), theirs)
            enabled[(cx, cy)] = jnp.minimum(jnp.maximum(mine, theirs), 1.0)

    def hold_health(dys):
        for dy in dys:
            deep = max(m for (a, _), m in COLUMNS.items() if a == dy)
            by_cx = {}
            for cx in (-1, 0, 1):
                near = enabled.get((cx, 0))
                if dy == 0:
                    by_cx[cx] = near
                    continue
                near = 1.0 if near is None else near
                if dy > 0:
                    by_cx[cx] = jnp.where(y_in + dy >= 4, enabled[(cx, 1)], near)
                else:
                    by_cx[cx] = jnp.where(y_in + dy < 0, enabled[(cx, -1)], near)
            for dx in range(-deep, deep + 1):
                for t in range(4):
                    flag = by_cx[(t + dx) // 4]
                    h = own[0][t]
                    health_m[dy + 3, dx + 3, t] = h if flag is None else h * flag

    z_ok = {dz: (z_at + dz >= 0) & (z_at + dz < 8) for dz in range(-3, 4)}

    def dz_of(dy):
        return [dz for dz in range(-3, 4) if (dy, dz) in COLUMNS]

    def gather_sums(k, dys, fresh):
        total = {}
        for dy in dys:
            part = {}
            for dz in dz_of(dy):
                deep = COLUMNS[(dy, dz)]
                turn = -(8 * dy + dz)
                value = spread(lane_roll(fields[dy + 3, k + 1], turn), deep)
                if k is FIRST:
                    h = lane_roll(fields[dy + 3, 0], turn)
                    if dz != 0:
                        h = jnp.where(z_ok[dz][None], h, 0.0)
                    h = spread(h, deep, row[None])
                a0, a1, a2 = None, None, None
                for reach in range(deep + 1):
                    terms = []
                    for dx in (reach, -reach) if reach else (0,):
                        lo = deep + dx
                        at = W_AT[(dy, dz)] + lo
                        if dy == 0 and dz == 0 and dx == 0:
                            continue
                        if k is FIRST:
                            w = jnp.minimum(health_m[dy + 3, dx + 3], h[lo : lo + 4])
                            weights[at] = w
                        else:
                            w = weights[at]
                        terms.append(w * value[lo : lo + 4])
                    if not terms:
                        continue
                    both = terms[0] if reach == 0 else terms[0] + terms[1]
                    a0 = add(a0, both)
                    if reach:
                        a1 = add(a1, times(reach, terms[0] - terms[1]))
                        if k is FIRST:
                            a2 = add(a2, times(reach * reach, both))
                if dy != 0:
                    part["y"] = add(part.get("y"), a0)
                if dz != 0:
                    part["z"] = add(part.get("z"), times(dz, a0))
                    if k is FIRST:
                        part["zz"] = add(part.get("zz"), times(dz * dz, a0))
                        if a1 is not None:
                            part["xz"] = add(part.get("xz"), times(dz, a1))
                if a1 is not None:
                    part["x"] = add(part.get("x"), a1)
                if a2 is not None:
                    part["xx"] = add(part.get("xx"), a2)
            for name in ("x", "z", "xx", "zz", "xz"):
                if name in part:
                    total[name] = add(total.get(name), part[name])
            if dy != 0:
                total["y"] = add(total.get("y"), times(dy, part["y"]))
                if k is FIRST:
                    total["yy"] = add(total.get("yy"), times(dy * dy, part["y"]))
                    for name, to in (("x", "xy"), ("z", "yz")):
                        if name in part:
                            total[to] = add(total.get(to), times(dy, part[name]))
        for n, name in enumerate(("x", "y", "z")):
            if name in total:
                at = 6 + 3 * k + n
                sums[at] = total[name] if fresh or name == "y" else sums[at] + total[name]
        for n, name in enumerate(ORDER[:6]):
            if name in total:
                sums[n] = total[name] if fresh or "y" in name else sums[n] + total[name]

    def first_sums(dys, fresh):
        gather_sums(FIRST, dys, fresh)

        def feature(k, carry):
            gather_sums(k, dys, fresh)
            return carry

        lax.fori_loop(1, 4, feature, 0)

    see(0, flags)
    hold_health((0,))
    for f in range(5):
        for t in range(4):
            fields[3, f, t] = own[f][t]
    first_sums((0,), True)

    arrive(copies[6:])
    see(1, yrecv[0, 5])
    see(-1, yrecv[1, 5])
    hold_health(OTHERS)

    side_lane = lane < 64
    for f in range(5):
        for t in range(4):
            outer = jnp.where(side_lane, take(yrecv[0, f], to_x[t]), take(yrecv[1, f], to_x[t]))
            for k in (1, 2, 3):
                fields[3 + k, f, t] = jnp.where(y_at < k, outer, own[f][t])
                fields[3 - k, f, t] = jnp.where(y_at >= 16 - k, outer, own[f][t])
    first_sums(OTHERS, False)

    @pl.when(early)
    def _():
        for n in range(2):
            for f in range(6):
                cpass[n, f : f + 1, :] = yrecv[n, f, 0:1, :]
        pl.semaphore_wait(ready, 1)
        copies[5][0].start()
        around.start()

    def end_pack(tile_of):
        got = jnp.zeros((8, LANES), jnp.float32)
        for t in range(3):
            got = jnp.where(row == t, tile_of(t)[0:1], got)
            got = jnp.where(row == 6 - t, tile_of(t + 1)[7:8], got)
        return got

    end_sums = [end_pack(lambda t: sums[n, t]) for n in range(18)]
    end_u = [end_pack(lambda t: own_u[c, t]) for c in range(4)]
    end_volume = end_pack(lambda t: own[1][t])

    def row_sum(tile):
        tile = tile + jnp.where(row % 2 == 0, row_roll(tile, -1), row_roll(tile, 1))
        return tile + jnp.where(row % 4 < 2, row_roll(tile, -2), row_roll(tile, 2))

    arrive(copies[:6], direct_from)

    @pl.when(late)
    def _():
        around.wait_recv()

    edge = [
        jnp.concatenate([xrecv[0, 4 * k : 4 * k + 4, :], xrecv[1, 4 * k : 4 * k + 4, :]], axis=0)
        for k in (4, 3, 0, 1, 2)
    ]
    edge = edge[:2] + [edge[1] * e for e in edge[2:]]

    def edge_tile(f, t):
        return row_sum(jnp.where(row % 4 == block_y, take(edge[f], to_x[t]), 0.0))

    corner_low = [
        jnp.where(side_lane, take(crecv[0], to_x[t]), take(crecv[1], to_x[t])) for t in range(4)]
    corner_high = [
        jnp.where(side_lane, take(crecv[2], to_x[t]), take(crecv[3], to_x[t])) for t in range(4)]

    low_end = row < 4

    def end_rows(low, high):
        return jnp.where(low_end, low, high)

    end_flags = end_rows(flags[0:1], flags[7:8])
    end_seen = {
        0: end_rows(xrecv[0, 20:21, :], xrecv[1, 20:21, :]),
        1: end_rows(crecv[0, 5:6, :], crecv[2, 5:6, :]),
        -1: end_rows(crecv[1, 5:6, :], crecv[3, 5:6, :]),
    }
    end_enabled = {}
    for cy in (-1, 0, 1):
        forth = jnp.where(low_end, direction(-1, cy), direction(1, cy))
        back = jnp.where(low_end, direction(1, -cy), direction(-1, -cy))
        theirs = take(end_seen[0], 8 * (block_y + cy + 1) + back)
        if cy == 1:
            theirs = jnp.where(block_y == 3, take(end_seen[1], 8 + back), theirs)
        if cy == -1:
            theirs = jnp.where(block_y == 0, take(end_seen[-1], 32 + back), theirs)
        mine = take(end_flags, 8 * (block_y + 1) + forth)
        end_enabled[cy] = jnp.minimum(jnp.maximum(mine, theirs), 1.0)

    def end_health(table):
        got = jnp.zeros((8, LANES), jnp.float32)
        for r, (_, t, _) in table.items():
            got = jnp.where(row == r, own[0][t][0:1] if r < 4 else own[0][t][7:8], got)
        return got

    def steps(table):
        got = jnp.zeros((8, LANES), jnp.float32)
        for r, (_, _, dx) in table.items():
            got = jnp.where(row == r, float(dx), got)
        return got

    step_two, step_three = steps(REACH_TWO), steps(REACH_THREE)
    health_two = end_health(REACH_TWO)
    end_fields = {0: [], 1: [], 3: []}
    for f in range(5):
        rim = [edge_tile(f, t) for t in range(4)]
        end_fields[0].append(place(row, REACH_TWO, lambda low, t: rim[t]))
        end_fields[1].append(place(
            row, REACH_TWO, lambda low, t: (corner_low if low else corner_high)[t][f : f + 1]))
        end_fields[3].append(place(row, REACH_THREE, lambda low, t: rim[t]))

    end_total = {}
    for dy in range(-2, 3):
        held = health_two
        if dy > 0:
            held = health_two * jnp.where(y_in + dy >= 4, end_enabled[1], end_enabled[0])
        elif dy < 0:
            held = health_two * jnp.where(y_in + dy < 0, end_enabled[-1], end_enabled[0])
        else:
            held = health_two * end_enabled[0]
        src_y = []
        for f in range(5):
            inner, outer = end_fields[0][f], end_fields[1][f]
            if dy > 0:
                inner = jnp.where(y_at < dy, outer, inner)
            elif dy < 0:
                inner = jnp.where(y_at >= 16 + dy, outer, inner)
            src_y.append(inner)
        part = {}
        for dz in range(-3, 4):
            if COLUMNS.get((dy, dz), 0) < 1:
                continue
            src = [lane_roll(e, -(8 * dy + dz)) for e in src_y]
            h = src[0]
            if dz != 0:
                h = jnp.where(z_ok[dz], h, 0.0)
            if COLUMNS[(dy, dz)] == 1:
                h = jnp.where(row % 4 == 2, h, 0.0)
            w = jnp.minimum(held, h)
            end_weights[ENDS.index((dy, dz))] = w
            for k in range(4):
                value = w * src[k + 1]
                part["s", k] = add(part.get(("s", k)), value)
                if dz != 0:
                    part["z", k] = add(part.get(("z", k)), times(dz, value))
                    if k == 0:
                        part["zz"] = add(part.get("zz"), times(dz * dz, value))
        for name in part:
            end_total[name] = add(end_total.get(name), part[name])
        if dy != 0:
            for k in range(4):
                end_total["y", k] = add(end_total.get(("y", k)), times(dy, part["s", k]))
            end_total["yy"] = add(end_total.get("yy"), times(dy * dy, part["s", 0]))
            end_total["yz"] = add(end_total.get("yz"), times(dy, part["z", 0]))
    for k in range(4):
        end_total["x", k] = step_two * end_total["s", k]
    end_total["xx"] = step_two * end_total["x", 0]
    end_total["xy"] = step_two * end_total["y", 0]
    end_total["xz"] = step_two * end_total["z", 0]
    w = jnp.minimum(end_health(REACH_THREE) * end_enabled[0], end_fields[3][0])
    end_weights[len(ENDS)] = w
    three = {("x", k): step_three * (w * end_fields[3][k + 1]) for k in range(4)}
    three["xx"] = step_three * three["x", 0]
    end_more = [ends_of(row, end_total[name], three.get(name, 0.0)) for name in ORDER]

    def material(full, u):
        kxx, kxy, kxz, kyy, kyz, kzz = full[:6]
        span = full[6:9]
        sym = [kxx, kxy, kxz, kxy, kyy, kyz, kxz, kyz, kzz]
        moment = [
            sym[3 * c + d] + full[9 + 3 * c + d] - u[c] * span[d]
            for c in range(3) for d in range(3)
        ]
        shape = [sym[n] + 1.0 if n % 4 == 0 else sym[n] for n in range(9)]
        inv = inverse_of(shape)
        grad = product(moment, inv)
        flip = [grad[3 * (n % 3) + n // 3] for n in range(9)]
        twice = product(flip, grad)
        strain = [0.5 * (twice[n] - 1.0) if n % 4 == 0 else 0.5 * twice[n] for n in range(9)]
        trace = LAME * (strain[0] + strain[4] + strain[8])
        second = [
            trace + 2.0 * SHEAR * strain[n] if n % 4 == 0 else 2.0 * SHEAR * strain[n]
            for n in range(9)
        ]
        first = [e * u[3] for e in product(grad, second)]
        return grad, product(first, inv)

    _, end_mapped = material([a + b for a, b in zip(end_sums, end_more)], end_u)
    for n in range(9):
        tile = end_volume * end_mapped[n]
        xsend2[0, 3 * n : 3 * n + 3, :] = tile[0:3]
        xsend2[1, 3 * n : 3 * n + 3, :] = tile[4:7]
        for k, slot in enumerate((0, 3)):
            wide_tile = take(tile, 32 * slot + lane % 32)
            wide_tile = jnp.where(block_y == row % 4, wide_tile, 0.0)
            wide_tile = wide_tile + (row_roll(wide_tile, -1) + row_roll(wide_tile, -2))
            for m in range(2):
                csend2[2 * m + k, n : n + 1, :] = wide_tile[4 * m : 4 * m + 1]
    copies2 = exchange(corner_moves(csend2, crecv2) + x_moves(xsend2, xrecv2), ssem2, rsem2)

    to_raw = [8 * (4 * b + (lane // 4) % 4) + lane // 16 for b in range(BYN)]
    x_in = lane % 4

    def block_tile(of_x, b):
        got = take(of_x[0], to_raw[b])
        for t in range(1, 4):
            got = jnp.where(x_in == t, take(of_x[t], to_raw[b]), got)
        return got

    stress = []
    for t in range(4):
        full = [with_ends(sums[n, t], end_more[n], row, t) for n in range(18)]
        grad, mapped = material(full, [own_u[c, t] for c in range(4)])
        span = full[6:9]
        for c in range(3):
            force[c, t] = mapped[3 * c] * span[0] + mapped[3 * c + 1] * span[1] + mapped[3 * c + 2] * span[2]
        v = own[1][t]
        for n in range(9):
            deform[n, t] = grad[n]
        stress.append([v * e for e in mapped])

    for n in range(9):
        of_x = [stress[t][n] for t in range(4)]
        low = of_x[0]
        high = lane_roll(of_x[0], 32)
        for t in range(1, 4):
            low = jnp.where(block_y == t, lane_roll(of_x[t], 32 * t), low)
            high = jnp.where(block_y == t, lane_roll(of_x[t], 32 * (t - 3)), high)
        for k, tile in enumerate((low, high)):
            ysend2[k, n] = tile
        for t in range(4):
            ystress[3, n, t] = of_x[t]

    copies2 += exchange(y_moves(ysend2, yrecv2), ssem2, rsem2, 6)

    def second_sums(dys):
        def component(c, carry):
            total = force[c]
            for dy in dys:
                for dz in dz_of(dy):
                    deep = COLUMNS[(dy, dz)]
                    turn = -(8 * dy + dz)
                    fixed = None
                    if dy != 0:
                        fixed = add(fixed, times(dy, ystress[dy + 3, 3 * c + 1]))
                    if dz != 0:
                        fixed = add(fixed, times(dz, ystress[dy + 3, 3 * c + 2]))
                    if fixed is not None:
                        fixed = spread(lane_roll(fixed, turn), deep)
                    slope = spread(lane_roll(ystress[dy + 3, 3 * c], turn), deep) if deep else None
                    for dx in range(-deep, deep + 1):
                        lo = deep + dx
                        value = None if fixed is None else fixed[lo : lo + 4]
                        if dx != 0:
                            value = add(value, times(dx, slope[lo : lo + 4]))
                        if value is not None:
                            total = total + weights[W_AT[(dy, dz)] + lo] * value
            force[c] = total
            return carry

        lax.fori_loop(0, 3, component, 0)

    second_sums((0,))
    for n in range(9):
        for b in range(BYN):
            dg_out[pl.ds(4 * n + b, 8, stride=36), :] = block_tile([deform[n, t] for t in range(4)], b)

    arrive(copies2[6:])
    for n in range(9):
        for t in range(4):
            inner = ystress[3, n, t]
            outer = jnp.where(
                side_lane, lane_roll(yrecv2[0, n], -32 * t), lane_roll(yrecv2[1, n], 32 * (3 - t)))
            for k in (1, 2, 3):
                ystress[3 + k, n, t] = jnp.where(y_at < k, outer, inner)
                ystress[3 - k, n, t] = jnp.where(y_at >= 16 - k, outer, inner)
    second_sums(OTHERS)

    for c in range(3):
        for b in range(BYN):
            force_out[pl.ds(4 * c + b, 8, stride=12), :] = block_tile([force[c, t] for t in range(4)], b)

    arrive(copies2[:6])

    def corner2(low, high, slots):
        return [
            jnp.where(lane[0:1] < 64, lane_roll(crecv2[low], -32 * k), lane_roll(crecv2[high], 32 * (3 - k)))
            for k in slots
        ]

    corner_low2, corner_high2 = corner2(0, 1, (3, 2, 1, 0)), corner2(2, 3, (0, 1, 2, 3))

    def halo_row(n, low, t):
        at = 3 * n + (3 - t if low else t)
        return xrecv2[0 if low else 1, at : at + 1, :]

    end_inner, end_outer, end_force = [], [], []
    for n in range(9):
        scale = step_two if n % 3 == 0 else 1.0
        end_inner.append(scale * place(row, REACH_TWO, lambda low, t: halo_row(n, low, t)))
        end_outer.append(scale * place(
            row, REACH_TWO, lambda low, t: (corner_low2 if low else corner_high2)[t][n : n + 1]))
    for c in range(3):
        total = None
        for dy in range(-2, 3):
            src_y = []
            for d in range(3):
                inner, outer = end_inner[3 * c + d], end_outer[3 * c + d]
                if dy > 0:
                    inner = jnp.where(y_at < dy, outer, inner)
                elif dy < 0:
                    inner = jnp.where(y_at >= 16 + dy, outer, inner)
                src_y.append(inner)
            fixed = src_y[0] if dy == 0 else src_y[0] + times(dy, src_y[1])
            for dz in range(-3, 4):
                if COLUMNS.get((dy, dz), 0) < 1:
                    continue
                value = fixed if dz == 0 else fixed + times(dz, src_y[2])
                value = lane_roll(value, -(8 * dy + dz))
                total = add(total, end_weights[ENDS.index((dy, dz))] * value)
        three = step_three * place(row, REACH_THREE, lambda low, t: halo_row(3 * c, low, t))
        end_force.append(ends_of(row, total, end_weights[len(ENDS)] * three))
    own_x = jnp.where(low_end, row, 7 - row)
    for c in range(3):
        for b in range(BYN):
            at = pl.ds(4 * c + b, 8, stride=12)
            more = row_sum(jnp.where(x_in == own_x, take(end_force[c], to_raw[b]), 0.0))
            force_out[at, :] = force_out[at, :] + jnp.where(row % 7 == 0, more, 0.0)
    for group, to in ((copies[:4], direct_to), (copies[4:] + copies2, present)):
        for copy, tx, ty in group:

            @pl.when(to(tx, ty))
            def _():
                copy.wait_send()

    @pl.when(early)
    def _():
        around.wait_send()


def store(dg, force, dg_out, force_out, sem):
    copies = [
        pltpu.make_async_copy(dg, dg_out, sem.at[0]),
        pltpu.make_async_copy(force, force_out, sem.at[1]),
    ]
    for copy in copies:
        copy.start()
    for copy in copies:
        copy.wait()


def local(displacement, volume, health, damage, block_pairs):
    pairs = block_pairs[0, 0].T
    disp = jnp.transpose(displacement, (0, 2, 1, 3)).reshape(-1, LANES)
    rows = [a.reshape(-1, LANES) for a in (volume, health, damage)]
    f32 = jnp.float32
    vmem = pl.BlockSpec(memory_space=pltpu.VMEM)
    dg, force = pl.pallas_call(
        kernel,
        out_shape=(
            pltpu.VMEM((BXN * 9 * BYN, LANES), f32),
            pltpu.VMEM((BXN * 3 * BYN, LANES), f32),
        ),
        in_specs=[pl.BlockSpec(memory_space=pl.ANY)] * 5,
        out_specs=(vmem, vmem),
        scratch_shapes=[
            pltpu.VMEM(disp.shape, f32),
            pltpu.VMEM(rows[0].shape, f32),
            pltpu.VMEM(rows[1].shape, f32),
            pltpu.VMEM(rows[2].shape, jnp.int32),
            pltpu.VMEM(pairs.shape, jnp.int32),
            pltpu.VMEM((2, 6, 8, LANES), f32),
            pltpu.VMEM((2, 6, 8, LANES), f32),
            pltpu.VMEM((2, 24, LANES), f32),
            pltpu.VMEM((2, 24, LANES), f32),
            pltpu.VMEM((4, 8, LANES), f32),
            pltpu.VMEM((4, 8, LANES), f32),
            pltpu.VMEM((2, 8, LANES), f32),
            pltpu.VMEM((2, 9, 8, LANES), f32),
            pltpu.VMEM((2, 9, 8, LANES), f32),
            pltpu.VMEM((2, 27, LANES), f32),
            pltpu.VMEM((2, 27, LANES), f32),
            pltpu.VMEM((4, 9, LANES), f32),
            pltpu.VMEM((4, 9, LANES), f32),
            pltpu.VMEM((7, 5, 4, 8, LANES), f32),
            pltpu.VMEM((4, 4, 8, LANES), f32),
            pltpu.VMEM((7, 7, 4, 8, LANES), f32),
            pltpu.VMEM((W_COUNT, 4, 8, LANES), f32),
            pltpu.VMEM((18, 4, 8, LANES), f32),
            pltpu.VMEM((7, 9, 4, 8, LANES), f32),
            pltpu.VMEM((3, 4, 8, LANES), f32),
            pltpu.VMEM((9, 4, 8, LANES), f32),
            pltpu.VMEM((len(ENDS) + 1, 8, LANES), f32),
            pltpu.SemaphoreType.DMA((5,)),
            pltpu.SemaphoreType.DMA((9,)),
            pltpu.SemaphoreType.DMA((9,)),
            pltpu.SemaphoreType.DMA((8,)),
            pltpu.SemaphoreType.DMA((8,)),
            pltpu.SemaphoreType.REGULAR,
        ],
        compiler_params=pltpu.CompilerParams(collective_id=0, has_side_effects=True),
        name="peridynamics",
    )(disp, *rows, pairs)
    dg, force = (pltpu.with_memory_space_constraint(a, pltpu.VMEM) for a in (dg, force))
    hbm = pl.BlockSpec(memory_space=pltpu.HBM)
    dg, force = pl.pallas_call(
        store,
        out_shape=(
            jax.ShapeDtypeStruct(dg.shape, f32),
            jax.ShapeDtypeStruct(force.shape, f32),
        ),
        in_specs=[vmem] * 2,
        out_specs=(hbm, hbm),
        scratch_shapes=[pltpu.SemaphoreType.DMA((2,))],
        name="store",
    )(dg, force)
    dg, force = (a.reshape(BXN, -1, BYN, LANES) for a in (dg, force))
    return jnp.transpose(dg, (0, 2, 1, 3)), jnp.transpose(force, (0, 2, 1, 3))


def solution(mesh):
    in_specs = (
        P("gx", "gy", None, None),
        P("gx", "gy", None),
        P("gx", "gy", None),
        P("gx", "gy", None),
        P("gx", "gy", None, None),
    )
    out_specs = (P("gx", "gy", None, None), P("gx", "gy", None, None))
    return jax.shard_map(local, mesh=mesh, in_specs=in_specs, out_specs=out_specs, check_vma=False)
```
